128 devices in a mesh: dev: 128 (over x, y, z, core).
Axes of the slice: x: 4, y: 4, z: 4, core: 2. Of those that a mesh axis runs over, the one named last changes fastest.
Arguments:
- features: bfloat16 [65536, 1024], P('dev'), may hold values from -6 to 6
- w_hidden: bfloat16 [1024, 512], replicated, may hold values from -0.1875 to 0.1875
- w_out: bfloat16 [512, 128], replicated, may hold values from -0.25 to 0.25
- items: bfloat16 [262144, 128], P('dev'), may hold values from -200 to 200
- routes: int32 [65536, 4], P('dev'), may hold values from 0 to 2047, all different within a row; in each aligned block of 512 rows (0 to 511, 512 to 1023, ...) at most 2 rows name the same one
- cluster_slot: int32 [2048], replicated, may hold values from 0 to 2047, each once
- sample_ids: int32 [2048, 4096], P('dev'), may hold values from 0 to 127
- sample_counts: int32 [2048, 4096], P('dev'), may hold values from 1 to 4095
- positives: int32 [65536, 4], P('dev'), may hold values from 0 to 4095
Outputs:
- slot_loss: float32 [2048], P('dev')
- grad_hidden: float32 [1024, 512], replicated
- grad_out: float32 [512, 128], replicated
- item_grad: float32 [262144, 128], P('dev')
The draws below stay inside these ranges and needn't reach their ends.
Inputs may be any that keep to these rules, and one draw needn't show every extreme that they name: `routes`: each row names 4 different clusters; within the rows of one device no cluster is named more than 2 times; every cluster is named by some row. `cluster_slot`: each cluster has one slot.
All inputs are finite; a program needn't handle non-finite values.
Results may differ from the reference program's by a relative error of at most 0.012.
The reference program's roundings to bfloat16 on the way (of `hidden`, `query`, `weight`, `dquery`, `dq_total` and `dpre`) count: a program that leaves them out, or rounds other values in their place, can miss the bound.
Values may be sent and summed in bfloat16 or wider, within the bound.
No kernel may reach another device: no remote copies, remote signals or barrier semaphores. Data moves between devices by JAX's collectives and lax.ppermute only.
A program may use at most 128 MiB of HBM per device.

```python
import math
import jax
import jax.numpy as jnp
import numpy as np
from jax import lax

FEAT = 1024
HID = 512
EMB = 128
ROUTES = 4
U_DEV = 512
CL_DEV = 16
SAMPLES = 4096
ITEM_CL = 128
ITEM_DEV = 2048
USERS = 65536
CLUSTERS = 2048
CAP = 2
ITEMS = 262144
N_DEV = 128


def draw_items(key, part):
    keys = jax.random.split(jax.random.fold_in(key, 17), 1)
    base = jax.random.normal(keys[0], (ITEMS, EMB), jnp.float32) * EMB ** (-0.5)
    return base.astype(jnp.bfloat16)


def place_ends(drawn, own_key, smallest, high):
    longest = drawn.shape.index(max(drawn.shape))
    spots = []
    for shift in (0, 1):
        where = [jax.random.randint(jax.random.fold_in(own_key, axis), (), 0, length) for axis, length in enumerate(drawn.shape)]
        where[longest] = (where[longest] + shift) % drawn.shape[longest]
        spots.append(tuple(where))
    return drawn.at[spots[0]].set(smallest).at[spots[1]].set(high)


def block_levels(own_key, shape, cuts, smallest, top_value):
    def one(axis_at, parts):
        heights = jax.random.uniform(jax.random.fold_in(jax.random.fold_in(own_key, 6), axis_at), (parts,), jnp.float32, smallest / len(cuts), top_value / len(cuts))
        return jnp.repeat(jnp.exp(heights), shape[axis_at] // parts).reshape((-1,) + (1,) * (len(shape) - axis_at - 1))

    gain = one(*cuts[0])
    for cut in cuts[1:]:
        gain = gain * one(*cut)
    return gain


def assign_block(key, own, number, rows, amount, top, bound, lean):
    order = jax.random.permutation(key, amount)
    packed, usual = portions_of(amount, rows * top, bound, lean, True), portions_of(amount, rows * top, bound, lean, False)
    places = jnp.arange(amount)

    def named(sizes, rotation):
        used = int((sizes > 0).sum())
        fixed = max(1, used // 4)
        shifted = fixed + (places - fixed + rotation * (used - fixed)) % max(1, amount - fixed)
        return jnp.zeros((amount,), jnp.int32).at[order[jnp.where(places < fixed, places, shifted)]].set(jnp.asarray(sizes, jnp.int32))

    sizes = jnp.where(number % 4 == 0, named(packed, number // 4), named(usual, number - number // 4 - 1))
    mixed = jax.random.permutation(jax.random.fold_in(own, 3), amount)
    giver, taker = mixed[0:amount // 2 * 2:2], mixed[1:amount // 2 * 2:2]
    slack = jnp.minimum(sizes[giver] - 1, bound - sizes[taker]) // 2
    slack = jnp.where((giver == order[0]) | (taker == order[0]) | (sizes[taker] == 0), 0, jnp.maximum(slack, 0))
    shifted = jax.random.randint(jax.random.fold_in(own, 4), (amount // 2,), 0, 1 << 20) % (slack + 1)
    sizes = sizes.at[giver].add(-shifted).at[taker].add(shifted)
    labels = jnp.searchsorted(jnp.cumsum(sizes), jnp.arange(rows * top), side="right").astype(jnp.int32)
    grid = labels.reshape(top, rows).T
    grid = grid[jax.random.permutation(jax.random.fold_in(own, 1), rows)]
    rotation = jax.random.randint(jax.random.fold_in(own, 2), (rows, 1), 0, top)
    return jnp.take_along_axis(grid, (jnp.arange(top)[None, :] + rotation) % top, axis=1)


def portions_of(amount, total, bound, slope, full):
    loads = [(1 << 20) // math.isqrt(standing ** slope) + 1 for standing in range(1, amount + 1)]
    largest = bound if full else min(bound, max(-(-total // amount), total * loads[0] // sum(loads)))
    least = 1 if total - largest >= amount - 1 else 0
    holding, spare = [largest] + [least] * (amount - 1), total - largest - least * (amount - 1)
    while spare > 0:
        free = [i for i in range(1, amount) if holding[i] < largest] or [i for i in range(1, amount) if holding[i] < bound]
        whole, left = sum([loads[i] for i in free]), spare
        for i in free:
            more = min(bound - holding[i], max(1, left * loads[i] // whole), spare)
            holding[i] = holding[i] + more
            spare = spare - more
    return np.array(holding)


def gaussian(stream_key, extent, spread, limit, shards=(), kind=jnp.bfloat16):
    array = jax.random.normal(stream_key, extent, jnp.float32) * spread
    if len(shards) > 0:
        array = block_levels(stream_key, extent, shards, -0.22, 0.18) * array
    return jnp.clip(array, min=-limit, max=limit).astype(kind)


def setup_inputs(seed: int = 0) -> dict:
    arg_keys = jax.random.split(jax.random.key(seed), 10)
    features = gaussian(arg_keys[0], (USERS, FEAT), 1.0, 6.0, ((0, 128),))
    w_hidden = gaussian(arg_keys[1], (FEAT, HID), FEAT ** -0.5, 0.1875)
    w_out = gaussian(arg_keys[2], (HID, EMB), HID ** -0.5, 0.25)
    items = draw_items(jax.random.fold_in(arg_keys[9], 71), 0)
    routes_keys = jax.random.split(jax.random.fold_in(arg_keys[4], 1), USERS // U_DEV)
    routes_turns = jax.random.permutation(jax.random.fold_in(arg_keys[4], 3), USERS // U_DEV)
    routes = jax.vmap(lambda own, number: assign_block(jax.random.fold_in(arg_keys[4], 2), own, number, U_DEV, CLUSTERS, ROUTES, CAP, 2))(routes_keys, routes_turns).reshape((USERS, ROUTES))
    cluster_slot = jax.random.permutation(arg_keys[5], CLUSTERS).astype(jnp.int32)
    sample_ids = place_ends(jax.random.randint(arg_keys[6], (CLUSTERS, SAMPLES), 0, ITEM_CL), jax.random.fold_in(arg_keys[6], 1), 0, ITEM_CL - 1).astype(jnp.int32)
    sample_counts = place_ends(jax.random.randint(arg_keys[7], (CLUSTERS, SAMPLES), 1, 4096), jax.random.fold_in(arg_keys[7], 1), 1, 4095).astype(jnp.int32)
    positives = place_ends(jax.random.randint(arg_keys[8], (USERS, ROUTES), 0, SAMPLES), jax.random.fold_in(arg_keys[8], 1), 0, SAMPLES - 1).astype(jnp.int32)
    return dict(features=features, w_hidden=w_hidden, w_out=w_out, items=items, routes=routes, cluster_slot=cluster_slot, sample_ids=sample_ids, sample_counts=sample_counts, positives=positives)


def silu_grad(value):
    sig = jax.nn.sigmoid(value)
    return sig * (1.0 + value * (1.0 - sig))

def slot_ranks(keys):
    order = jnp.argsort(keys, stable=True).astype(jnp.int32)
    sorted_keys = keys[order]
    first = jnp.searchsorted(sorted_keys, sorted_keys, side='left').astype(jnp.int32)
    ranked = jnp.arange(keys.shape[0], dtype=jnp.int32) - first
    return jnp.zeros_like(keys).at[order].set(ranked)

def score_block(queries, targets, table, counts):
    scores = jnp.einsum('cqe,cse->cqs', queries.astype(jnp.float32), table.astype(jnp.float32))
    scores = scores - jnp.log(counts.astype(jnp.float32))[:, None, :]
    top = lax.optimization_barrier(jnp.max(scores, axis=2, keepdims=True))
    expo = jnp.exp(scores - top)
    total = lax.optimization_barrier(jnp.sum(expo, axis=2, keepdims=True))
    hit = lax.broadcasted_iota(jnp.int32, scores.shape, 2) == targets[:, :, None]
    picked = lax.optimization_barrier(jnp.sum(jnp.where(hit, scores, 0.0), axis=2))
    losses = jnp.log(total[:, :, 0]) + top[:, :, 0] - picked
    live = targets >= 0
    cluster_loss = lax.optimization_barrier(jnp.sum(jnp.where(live, losses, 0.0), axis=1)) / lax.optimization_barrier(jnp.sum(live.astype(jnp.float32), axis=1))
    weight = (expo / total - hit.astype(jnp.float32)).astype(jnp.bfloat16)
    dquery = jnp.einsum('cqs,cse->cqe', weight.astype(jnp.float32), table.astype(jnp.float32)).astype(jnp.bfloat16)
    dtable = jnp.einsum('cqs,cqe->cse', weight.astype(jnp.float32), queries.astype(jnp.float32))
    return (cluster_loss, dquery, dtable)

def pick_rows(block, ids):
    return block[ids]

def sum_rows(values, ids):
    return jax.ops.segment_sum(values, ids, num_segments=ITEM_CL)

def reference(features, w_hidden, w_out, items, routes, cluster_slot, sample_ids, sample_counts, positives):
    pre = jnp.dot(features, w_hidden, preferred_element_type=jnp.float32)
    hidden = jax.nn.silu(pre).astype(jnp.bfloat16)
    query = jnp.dot(hidden, w_out, preferred_element_type=jnp.float32).astype(jnp.bfloat16)
    users = features.shape[0]
    slots = cluster_slot[routes]
    source = jnp.broadcast_to((jnp.arange(users, dtype=jnp.int32) // U_DEV)[:, None], slots.shape)
    keys = (source * CLUSTERS + slots).reshape(-1)
    ranks = slot_ranks(keys)
    column = source.reshape(-1) * CAP + ranks
    row = slots.reshape(-1)
    width = N_DEV * CAP
    qbuf = jnp.zeros((CLUSTERS, width, EMB), jnp.bfloat16).at[row, column].set(jnp.repeat(query, ROUTES, axis=0))
    tbuf = jnp.full((CLUSTERS, width), -1, jnp.int32).at[row, column].set(positives.reshape(-1))

    def owner(carry, index):
        start = (index * CL_DEV).astype(jnp.int32)
        queries = lax.dynamic_slice_in_dim(qbuf, start, CL_DEV, 0)
        targets = lax.dynamic_slice_in_dim(tbuf, start, CL_DEV, 0)
        table_ids = lax.dynamic_slice_in_dim(sample_ids, start, CL_DEV, 0)
        counts = lax.dynamic_slice_in_dim(sample_counts, start, CL_DEV, 0)
        block_rows = lax.dynamic_slice_in_dim(items, (index * ITEM_DEV).astype(jnp.int32), ITEM_DEV, 0)
        block_rows = block_rows.reshape(CL_DEV, ITEM_CL, EMB)
        table = jax.vmap(pick_rows)(block_rows, table_ids)
        cluster_loss, dquery, dtable = score_block(queries, targets, table, counts)
        grads = jax.vmap(sum_rows)(dtable, table_ids)
        return (carry, (cluster_loss, dquery, grads))
    _, (losses, dqbuf, igrad) = lax.scan(owner, jnp.zeros((), jnp.float32), jnp.arange(N_DEV, dtype=jnp.int32))
    slot_loss = losses.reshape(-1)
    item_grad = igrad.reshape(ITEMS, EMB)
    dq_pairs = dqbuf.reshape(CLUSTERS, width, EMB)[row, column].astype(jnp.float32).reshape(users, ROUTES, EMB)
    dq_total = lax.optimization_barrier(jnp.sum(dq_pairs, axis=1)).astype(jnp.bfloat16)
    grad_out = jnp.dot(hidden.T, dq_total, preferred_element_type=jnp.float32)
    dhidden = jnp.dot(dq_total, w_out.T, preferred_element_type=jnp.float32)
    dpre = (dhidden * silu_grad(pre)).astype(jnp.bfloat16)
    grad_hidden = jnp.dot(features.T, dpre, preferred_element_type=jnp.float32)
    return (slot_loss, grad_hidden, grad_out, item_grad)
```

```python
import jax
import jax.numpy as jnp
from jax import lax
from jax.experimental import pallas as pl
from jax.experimental.pallas import tpu as pltpu
from jax.sharding import PartitionSpec as P

F32 = jnp.float32
BF16 = jnp.bfloat16
NONE = -3.0e38
KEY = 4096
LANES = 128


def vmem(count):
    return [pl.BlockSpec(memory_space=pltpu.VMEM)] * count


def params(megabytes):
    return pltpu.CompilerParams(vmem_limit_bytes=megabytes << 20)


def iota(shape, axis):
    return lax.broadcasted_iota(jnp.int32, shape, axis)


def one_hot(mask):
    return jnp.where(mask, 1.0, 0.0).astype(BF16)


def mm(a, b, dims=((1,), (0,))):
    return lax.dot_general(a, b, (dims, ((), ())), preferred_element_type=F32)


def route_body(
    routes_ref, pos_ref, cslot_ref, feat_ref, wh_ref, wo_ref, send_ref, place_ref, pre_ref, tail_ref
):
    users = routes_ref.shape[1]
    visits = routes_ref.shape[0]
    clusters = cslot_ref.shape[0] * LANES
    devices, rows, width = send_ref.shape
    local = clusters // devices
    cslot = cslot_ref[...]
    high = ((cslot >> 6) << 6).astype(F32).astype(BF16)
    low = (cslot & 63).astype(F32).astype(BF16)
    lane_at = iota((LANES, users), 0)
    row_at = iota((cslot.shape[0], users), 0)
    user_at = iota((1, users), 1)
    slots = []
    keys = []
    for r in range(visits):
        cluster = routes_ref[r : r + 1, :]
        pick = one_hot(lane_at == (cluster & (LANES - 1)))
        found = mm(high, pick) + mm(low, pick)
        slot = jnp.sum(jnp.where(row_at == (cluster >> 7), found, 0.0), axis=0, keepdims=True)
        slots.append(slot)
        keys.append((user_at * KEY + pos_ref[r : r + 1, :]).astype(F32))
    pre = mm(feat_ref[...], wh_ref[...])
    pre_ref[...] = pre
    hidden = (pre * jax.nn.sigmoid(pre)).astype(BF16)
    query = mm(hidden, wo_ref[...]).astype(BF16)
    block = LANES
    groups = block // local
    sub = iota((block, users), 0).astype(F32)
    lane_user = iota((block, users), 1).astype(F32)
    tail_lane = iota((block, LANES), 1)
    tail_row = iota((block, LANES), 0)
    tail_hit = ((tail_lane & (local - 1)) == (tail_row & (local - 1))) & (tail_lane < 4 * local)
    tail_kind = tail_lane // local
    for b in range(clusters // block):
        slot_at = sub + float(b * block)
        key = jnp.full((block, users), -1.0, F32)
        for r in range(visits):
            key = jnp.where(slot_at == slots[r], keys[r], key)
        most = jnp.max(key, axis=1, keepdims=True)
        least = jnp.min(jnp.where(key < 0.0, 3.0e38, key), axis=1, keepdims=True)
        some = most >= 0.0
        both = most > least
        first = jnp.where(some, least, -1.0)
        second = jnp.where(both, most, -1.0)
        ends = []
        parts = []
        for chosen in (first, second):
            user = jnp.floor(chosen * (1.0 / KEY))
            mark = chosen - user * KEY + 1.0
            mark = jnp.where(chosen < 0.0, 0.0, mark)
            top = jnp.floor(mark * (1.0 / 64.0))
            ends += [top, mark - top * 64.0]
            parts.append(jnp.where(lane_user == user, 1.0, 0.0).reshape(groups, local, users))
        place = jnp.concatenate(parts, axis=1).reshape(2 * block, users).astype(BF16)
        place_ref[b * 2 * block : (b + 1) * 2 * block, :] = place
        tail = jnp.where(
            tail_kind == 0,
            ends[0],
            jnp.where(tail_kind == 1, ends[1], jnp.where(tail_kind == 2, ends[2], ends[3])),
        )
        tail = jnp.where(tail_hit, tail, 0.0).reshape(groups, local, LANES)
        tail_ref[b * groups : (b + 1) * groups, :] = jnp.sum(tail, axis=1)
        sent = mm(place, query).astype(BF16)
        send_ref[b * groups : (b + 1) * groups, 0 : 2 * local, :] = sent.reshape(
            groups, 2 * local, width
        )
    tails = jnp.broadcast_to(tail_ref[...][:, None, :], (devices, rows - 2 * local, width))
    send_ref[:, 2 * local : rows, :] = tails.astype(BF16)


def route(routes, positives, cluster_slot, features, w_hidden, w_out, devices):
    users, visits = routes.shape
    clusters = cluster_slot.shape[0]
    width = w_out.shape[1]
    hid = w_hidden.shape[1]
    rows = 2 * clusters // devices + 8
    return pl.pallas_call(
        route_body,
        out_shape=(
            jax.ShapeDtypeStruct((devices, rows, width), BF16),
            jax.ShapeDtypeStruct((2 * clusters, users), BF16),
            jax.ShapeDtypeStruct((users, hid), F32),
        ),
        in_specs=vmem(6),
        out_specs=vmem(3),
        scratch_shapes=[pltpu.VMEM((devices, LANES), F32)],
        compiler_params=params(48),
        name="route",
    )(
        routes.T,
        positives.T,
        cluster_slot.reshape(clusters // LANES, LANES),
        features,
        w_hidden,
        w_out,
    )


def table_body(ids_ref, counts_ref, mass_ref, tabs_ref, inv_ref):
    total = ids_ref.shape[0]
    chunks = total // 16
    ids = ids_ref[...]
    counts = counts_ref[...]
    inv_ref[...] = 1.0 / counts.astype(F32)
    tabs_ref[:, 0:LANES] = (ids * 4096).astype(F32).astype(BF16)
    tabs_ref[:, LANES : 2 * LANES] = ((counts >> 6) << 6).astype(F32).astype(BF16)
    tabs_ref[:, 2 * LANES : 3 * LANES] = (counts & 63).astype(F32).astype(BF16)
    item_at = iota((LANES, LANES), 0)
    lane_at = iota((LANES, LANES), 1)
    mass_ref[...] = jnp.zeros_like(mass_ref)

    def cluster(k, carry):
        acc = jnp.zeros((LANES, LANES), F32)
        for h in range(chunks):
            at = k * chunks + h
            hit = item_at == ids_ref[pl.ds(at, 1), :]
            acc = acc + jnp.where(hit, inv_ref[pl.ds(at, 1), :], 0.0)
        column = jnp.sum(acc, axis=1, keepdims=True)
        mass_ref[...] = jnp.where(lane_at == k, column, mass_ref[...])
        return carry

    lax.fori_loop(0, 16, cluster, 0)


def tables(sample_ids, sample_counts):
    total = sample_ids.size // LANES
    return pl.pallas_call(
        table_body,
        out_shape=(
            jax.ShapeDtypeStruct((LANES, LANES), F32),
            jax.ShapeDtypeStruct((total, 3 * LANES), BF16),
        ),
        in_specs=vmem(2),
        out_specs=vmem(2),
        scratch_shapes=[pltpu.VMEM((total, LANES), F32)],
        compiler_params=params(16),
        cost_estimate=pl.CostEstimate(flops=30_000_000, bytes_accessed=1 << 20, transcendentals=0),
        name="tables",
    )(sample_ids.reshape(total, LANES), sample_counts.reshape(total, LANES))


def owner_body(
    got_ref, items_ref, mass_ref, tabs_ref, dq_ref, weight_ref, q_ref, loss_ref, got32_ref, dq32_ref
):
    devices, rows, width = got_ref.shape
    local = q_ref.shape[0]
    chunks = tabs_ref.shape[0] // local
    got32_ref[...] = got_ref[...].astype(F32).reshape(devices * rows, width)
    tail = got32_ref[pl.ds(2 * local, devices, stride=rows), :].T
    pairs = 2 * devices
    item_at = iota((LANES, pairs), 0)
    row_at = iota((chunks, pairs), 0)
    loss_lane = iota((1, LANES), 1)
    losses = jnp.zeros((1, LANES), F32)
    mass = mass_ref[...]
    for k in range(local):
        marks = []
        for c in range(2):
            top = tail[(2 * c) * local + k : (2 * c) * local + k + 1, :]
            low = tail[(2 * c + 1) * local + k : (2 * c + 1) * local + k + 1, :]
            marks.append(top * 64.0 + low)
        mark = jnp.concatenate(marks, axis=1)
        live = mark > 0.0
        target = jnp.where(live, mark - 1.0, 0.0).astype(jnp.int32)
        pick = one_hot(item_at == (target & (LANES - 1)))
        tab = tabs_ref[k * chunks : (k + 1) * chunks, :]
        found = (
            mm(tab[:, 0:LANES], pick)
            + mm(tab[:, LANES : 2 * LANES], pick)
            + mm(tab[:, 2 * LANES : 3 * LANES], pick)
        )
        packed = jnp.sum(
            jnp.where(row_at == (target >> 7), found, 0.0), axis=0, keepdims=True
        ).astype(jnp.int32)
        item = jnp.where(live, packed >> 12, -1)
        count = (packed & 4095).astype(F32)
        queries = jnp.concatenate(
            [
                got32_ref[pl.ds(k, devices, stride=rows), :],
                got32_ref[pl.ds(local + k, devices, stride=rows), :],
            ],
            axis=0,
        ).astype(BF16)
        q_ref[k] = queries
        block = items_ref[k * LANES : (k + 1) * LANES, :]
        column = mass[:, k : k + 1]
        scores = mm(block, queries, ((1,), (1,)))
        masked = jnp.where(column > 0.0, scores, NONE)
        top = jnp.max(masked, axis=0, keepdims=True)
        expo = jnp.exp(masked - top) * column
        total = jnp.sum(expo, axis=0, keepdims=True)
        hit = item_at == item
        picked = jnp.sum(jnp.where(hit, scores, 0.0), axis=0, keepdims=True)
        loss = jnp.log(total) + top - (picked - jnp.log(count))
        loss = jnp.sum(jnp.where(live, loss, 0.0), axis=1, keepdims=True) / jnp.sum(
            jnp.where(live, 1.0, 0.0), axis=1, keepdims=True
        )
        losses = jnp.where(loss_lane == k, loss, losses)
        weight = expo * (1.0 / total) - jnp.where(hit, 1.0, 0.0)
        high = weight.astype(BF16)
        low = (weight - high.astype(F32)).astype(BF16)
        weight_ref[k, :, 0:pairs] = high
        weight_ref[k, :, pairs : 2 * pairs] = low
        dq = mm(high, block, ((0,), (0,))) + mm(low, block, ((0,), (0,)))
        dq32_ref[pl.ds(k, devices, stride=2 * local), :] = dq[0:devices, :]
        dq32_ref[pl.ds(local + k, devices, stride=2 * local), :] = dq[devices:pairs, :]
    loss_ref[...] = losses
    dq_ref[...] = dq32_ref[...].reshape(devices, 2 * local, width).astype(BF16)


def owner(got, items, mass, tabs):
    devices, rows, width = got.shape
    local = items.shape[0] // LANES
    return pl.pallas_call(
        owner_body,
        out_shape=(
            jax.ShapeDtypeStruct((devices, 2 * local, width), BF16),
            jax.ShapeDtypeStruct((local, LANES, 4 * devices), BF16),
            jax.ShapeDtypeStruct((local, 2 * devices, width), BF16),
            jax.ShapeDtypeStruct((1, LANES), F32),
        ),
        in_specs=vmem(4),
        out_specs=vmem(4),
        scratch_shapes=[
            pltpu.VMEM((devices * rows, width), F32),
            pltpu.VMEM((devices * 2 * local, width), F32),
        ],
        compiler_params=params(40),
        name="owner",
    )(got, items, mass, tabs)


def item_body(weight_ref, q_ref, grad_ref):
    pairs = q_ref.shape[1]
    weight = weight_ref[0]
    queries = q_ref[0]
    grad_ref[...] = mm(weight[:, 0:pairs], queries) + mm(weight[:, pairs : 2 * pairs], queries)


def item_grads(weight, queries):
    local, pairs, width = queries.shape
    return pl.pallas_call(
        item_body,
        grid=(local,),
        out_shape=jax.ShapeDtypeStruct((local * LANES, width), F32),
        in_specs=[
            pl.BlockSpec((1, LANES, 2 * pairs), lambda k: (k, 0, 0)),
            pl.BlockSpec((1, pairs, width), lambda k: (k, 0, 0)),
        ],
        out_specs=pl.BlockSpec((LANES, width), lambda k: (k, 0)),
        compiler_params=params(8),
        cost_estimate=pl.CostEstimate(
            flops=270_000_000, bytes_accessed=4 << 20, transcendentals=0
        ),
        name="item_grads",
    )(weight, queries)


def tower_body(back_ref, place_ref, pre_ref, feat_ref, wo_ref, grad_ref):
    devices, rows, width = back_ref.shape
    back = back_ref[...].reshape(devices * rows, width)
    dq_t = mm(back, place_ref[...], ((0,), (0,))).astype(BF16)
    pre = pre_ref[...]
    sig = jax.nn.sigmoid(pre)
    hidden = (pre * sig).astype(BF16)
    out_t = mm(dq_t, hidden)
    dhidden = mm(dq_t.astype(F32).T.astype(BF16), wo_ref[...], ((1,), (1,)))
    dpre = (dhidden * (sig * (1.0 + pre * (1.0 - sig)))).astype(BF16)
    big = mm(feat_ref[...], dpre)
    parts = [
        big[:, c * LANES : (c + 1) * LANES].reshape(devices, 8, LANES)
        for c in range(big.shape[1] // LANES)
    ]
    for c in range(0, len(parts), 2):
        grad_ref[:, c * 8 : c * 8 + 16, :] = jnp.concatenate(parts[c : c + 2], axis=1).astype(BF16)
    small = out_t.T
    filled = small.shape[0] // 8
    at = len(parts) * 8
    grad_ref[0:filled, at : at + 8, :] = small.reshape(filled, 8, LANES).astype(BF16)
    grad_ref[filled:devices, at : at + 8, :] = jnp.zeros((devices - filled, 8, LANES), BF16)


def tower_back(back, place, pre, features_t, w_out):
    devices = back.shape[0]
    rows = (pre.shape[1] * features_t.shape[0] // devices) // LANES + 8
    return pl.pallas_call(
        tower_body,
        out_shape=jax.ShapeDtypeStruct((devices, rows, LANES), BF16),
        in_specs=vmem(5),
        out_specs=vmem(1)[0],
        compiler_params=params(48),
        name="tower_back",
    )(back, place, pre, features_t, w_out)


def sum_body(parts_ref, out_ref):
    total = jnp.sum(parts_ref[...].astype(F32), axis=0, keepdims=True)
    out_ref[...] = jnp.broadcast_to(total, out_ref.shape).astype(BF16)


def sum_parts(parts):
    return pl.pallas_call(
        sum_body,
        out_shape=jax.ShapeDtypeStruct(parts.shape, BF16),
        in_specs=vmem(1),
        out_specs=vmem(1)[0],
        compiler_params=params(24),
        name="sum_parts",
    )(parts)


def spread_body(in_ref, hidden_ref, out_ref):
    devices = in_ref.shape[0]
    got = in_ref[...].astype(F32)
    blocks = hidden_ref.shape[1] // LANES
    for c in range(blocks):
        hidden_ref[:, c * LANES : (c + 1) * LANES] = got[:, c * 8 : c * 8 + 8, :].reshape(
            devices * 8, LANES
        )
    filled = out_ref.shape[0] // 8
    out_ref[...] = got[0:filled, blocks * 8 : blocks * 8 + 8, :].reshape(out_ref.shape)


def spread(summed, hidden_shape, out_shape):
    return pl.pallas_call(
        spread_body,
        out_shape=(
            jax.ShapeDtypeStruct(hidden_shape, F32),
            jax.ShapeDtypeStruct(out_shape, F32),
        ),
        in_specs=vmem(1),
        out_specs=vmem(2),
        compiler_params=params(24),
        name="spread",
    )(summed)


def exchange(x):
    return lax.all_to_all(x, "dev", split_axis=0, concat_axis=0, tiled=True)


def local(
    features, w_hidden, w_out, items, routes, cluster_slot, sample_ids, sample_counts, positives
):
    devices = lax.axis_size("dev")
    send, place, pre = route(routes, positives, cluster_slot, features, w_hidden, w_out, devices)
    mass, tabs = tables(sample_ids, sample_counts)
    features_t = features.T
    got = exchange(send)
    dq, weight, queries, losses = owner(got, items, mass, tabs)
    back = exchange(dq)
    item_grad = item_grads(weight, queries)
    partial = tower_back(back, place, pre, features_t, w_out)
    summed = sum_parts(exchange(partial))
    grad_hidden, grad_out = spread(exchange(summed), w_hidden.shape, w_out.shape)
    slot_loss = losses[0, : sample_ids.shape[0]]
    return (slot_loss, grad_hidden, grad_out, item_grad)


def solution(mesh):
    in_specs = (
        P("dev", None),
        P(),
        P(),
        P("dev", None),
        P("dev", None),
        P(),
        P("dev", None),
        P("dev", None),
        P("dev", None),
    )
    out_specs = (P("dev"), P(), P(), P("dev", None))
    return jax.shard_map(local, mesh=mesh, in_specs=in_specs, out_specs=out_specs, check_vma=False)
```

```python
import jax
import jax.numpy as jnp
from jax import lax
from jax.experimental import pallas as pl
from jax.experimental.pallas import tpu as pltpu
from jax.sharding import PartitionSpec as P

F32 = jnp.float32
BF16 = jnp.bfloat16
NONE = -3.0e38
KEY = 4096
LANES = 128


def vmem(count):
    return [pl.BlockSpec(memory_space=pltpu.VMEM)] * count


def in_hbm(arrays):
    return tuple(pltpu.with_memory_space_constraint(a, pltpu.HBM) for a in arrays)


def outs_hbm(arrays):
    return tuple(pltpu.HBM(a.shape, a.dtype) for a in arrays)


def hbm(count):
    return [pl.BlockSpec(memory_space=pltpu.HBM)] * count


def params(megabytes):
    return pltpu.CompilerParams(vmem_limit_bytes=megabytes << 20)


def iota(shape, axis):
    return lax.broadcasted_iota(jnp.int32, shape, axis)


def one_hot(mask):
    return jnp.where(mask, 1.0, 0.0).astype(BF16)


def mm(a, b, dims=((1,), (0,))):
    return lax.dot_general(a, b, (dims, ((), ())), preferred_element_type=F32)


def route_body(
    routes_hbm,
    pos_hbm,
    cslot_hbm,
    feat_hbm,
    wh_hbm,
    wo_hbm,
    send_hbm,
    place_hbm,
    mine_hbm,
    other_hbm,
    routes_ref,
    pos_ref,
    cslot_ref,
    feat_ref,
    wh_ref,
    wo_ref,
    send_ref,
    place_ref,
    mine_ref,
    other_ref,
    in_sem,
    out_sem,
    send_sem,
    place_sem,
):
    loads = [
        pltpu.make_async_copy(src, dst, in_sem.at[i])
        for i, (src, dst) in enumerate(
            [
                (routes_hbm, routes_ref),
                (pos_hbm, pos_ref),
                (cslot_hbm, cslot_ref),
                (feat_hbm, feat_ref),
                (wh_hbm, wh_ref),
                (wo_hbm, wo_ref),
            ]
        )
    ]
    for load in loads:
        load.start()
    visits, users = routes_ref.shape
    clusters = cslot_ref.shape[0] * LANES
    devices, rows, width = send_ref.shape
    local = clusters // devices
    for load in loads[:3]:
        load.wait()
    cslot = cslot_ref[...]
    high = ((cslot >> 6) << 6).astype(F32).astype(BF16)
    low = (cslot & 63).astype(F32).astype(BF16)
    lane_at = iota((LANES, users), 0)
    row_at = iota((cslot.shape[0], users), 0)
    user_at = iota((1, users), 1)
    slots = []
    keys = []
    for r in range(visits):
        cluster = routes_ref[r : r + 1, :]
        pick = one_hot(lane_at == (cluster & (LANES - 1)))
        found = mm(high, pick) + mm(low, pick)
        slot = jnp.sum(jnp.where(row_at == (cluster >> 7), found, 0.0), axis=0, keepdims=True)
        slots.append(slot)
        keys.append((user_at * KEY + pos_ref[r : r + 1, :] + 1).astype(F32))
    for load in loads[3:]:
        load.wait()
    pre = mm(feat_ref[...], wh_ref[...])
    half = pre.shape[1] // 2
    core = lax.axis_index("dev") % 2
    mine_ref[...] = jnp.where(core == 0, pre[:, 0:half], pre[:, half:])
    other_ref[...] = jnp.where(core == 0, pre[:, half:], pre[:, 0:half])
    stores = [
        pltpu.make_async_copy(mine_ref, mine_hbm, out_sem.at[0]),
        pltpu.make_async_copy(other_ref, other_hbm, out_sem.at[1]),
    ]
    for store in stores:
        store.start()
    hidden = (pre * jax.nn.sigmoid(pre)).astype(BF16)
    query = mm(hidden, wo_ref[...]).astype(BF16)
    block = LANES
    groups = block // local
    sub = iota((block, users), 0).astype(F32)
    lane_user = iota((block, users), 1).astype(F32)
    tail_lane = iota((block, LANES), 1)
    tail_row = iota((block, LANES), 0)
    tail_hit = ((tail_lane & (local - 1)) == (tail_row & (local - 1))) & (tail_lane < 4 * local)
    tail_kind = tail_lane // local
    for b in range(clusters // block):
        slot_at = sub + float(b * block)
        key = jnp.zeros((block, users), F32)
        for r in range(visits):
            key = jnp.where(slot_at == slots[r], keys[r], key)
        most = jnp.max(key, axis=1, keepdims=True)
        rest = jnp.sum(key, axis=1, keepdims=True) - most
        ends = []
        parts = []
        for chosen in (most, rest):
            user = jnp.floor((chosen - 1.0) * (1.0 / KEY))
            mark = jnp.where(chosen > 0.0, chosen - user * KEY, 0.0)
            top = jnp.floor(mark * (1.0 / 64.0))
            ends += [top, mark - top * 64.0]
            parts.append(jnp.where(lane_user == user, 1.0, 0.0).reshape(groups, local, users))
        place = jnp.concatenate(parts, axis=1).reshape(2 * block, users).astype(BF16)
        span = pl.ds(b * 2 * block, 2 * block)
        place_ref[span, :] = place
        stores.append(
            pltpu.make_async_copy(place_ref.at[span, :], place_hbm.at[span, :], place_sem.at[b])
        )
        stores[-1].start()
        tail = jnp.where(
            tail_kind == 0,
            ends[0],
            jnp.where(tail_kind == 1, ends[1], jnp.where(tail_kind == 2, ends[2], ends[3])),
        )
        tail = jnp.where(tail_hit, tail, 0.0).reshape(groups, local, LANES)
        tail = jnp.sum(tail, axis=1)
        span = pl.ds(b * groups, groups)
        sent = mm(place, query).astype(BF16)
        send_ref[span, 0 : 2 * local, :] = sent.reshape(groups, 2 * local, width)
        send_ref[span, 2 * local : rows, :] = jnp.broadcast_to(
            tail[:, None, :], (groups, rows - 2 * local, width)
        ).astype(BF16)
        stores.append(pltpu.make_async_copy(send_ref.at[span], send_hbm.at[span], send_sem.at[b]))
        stores[-1].start()
    for store in stores:
        store.wait()


def route(routes, positives, cluster_slot, features, w_hidden, w_out, devices):
    users, visits = routes.shape
    clusters = cluster_slot.shape[0]
    width = w_out.shape[1]
    hid = w_hidden.shape[1]
    rows = 2 * clusters // devices + 8
    args = (
        routes.T,
        positives.T,
        cluster_slot.reshape(clusters // LANES, LANES),
        features,
        w_hidden,
        w_out,
    )
    outs = (
        jax.ShapeDtypeStruct((devices, rows, width), BF16),
        jax.ShapeDtypeStruct((2 * clusters, users), BF16),
        jax.ShapeDtypeStruct((users, hid // 2), F32),
        jax.ShapeDtypeStruct((users, hid // 2), F32),
    )
    return pl.pallas_call(
        route_body,
        out_shape=outs_hbm(outs),
        in_specs=hbm(6),
        out_specs=hbm(4),
        scratch_shapes=[pltpu.VMEM(a.shape, a.dtype) for a in args + outs]
        + [
            pltpu.SemaphoreType.DMA((6,)),
            pltpu.SemaphoreType.DMA((2,)),
            pltpu.SemaphoreType.DMA((clusters // LANES,)),
            pltpu.SemaphoreType.DMA((clusters // LANES,)),
        ],
        compiler_params=params(48),
        name="route",
    )(*in_hbm(args))


def table_body(ids_ref, counts_ref, mass_ref, tabs_ref, inv_ref):
    clusters = tabs_ref.shape[0]
    chunks = ids_ref.shape[0] // clusters
    ids = ids_ref[...]
    counts = counts_ref[...]
    inv_ref[...] = 1.0 / counts.astype(F32)
    digits = ((ids * 4096), ((counts >> 6) << 6), (counts & 63))
    for d, digit in enumerate(digits):
        tabs_ref[:, d * chunks : (d + 1) * chunks, :] = (
            digit.astype(F32).reshape(clusters, chunks, LANES).astype(BF16)
        )
    item_at = iota((LANES, LANES), 0)
    lane_at = iota((LANES, LANES), 1)
    mass_ref[...] = jnp.zeros_like(mass_ref)

    def cluster(k, carry):
        acc = jnp.zeros((LANES, LANES), F32)
        for h in range(chunks):
            at = k * chunks + h
            hit = item_at == ids_ref[pl.ds(at, 1), :]
            acc = acc + jnp.where(hit, inv_ref[pl.ds(at, 1), :], 0.0)
        column = jnp.sum(acc, axis=1, keepdims=True)
        mass_ref[...] = jnp.where(lane_at == k, column, mass_ref[...])
        return carry

    lax.fori_loop(0, clusters, cluster, 0)


def tables(sample_ids, sample_counts):
    clusters, samples = sample_ids.shape
    total = sample_ids.size // LANES
    return pl.pallas_call(
        table_body,
        out_shape=(
            jax.ShapeDtypeStruct((LANES, LANES), F32),
            jax.ShapeDtypeStruct((clusters, 3 * samples // LANES, LANES), BF16),
        ),
        in_specs=vmem(2),
        out_specs=vmem(2),
        scratch_shapes=[pltpu.VMEM((total, LANES), F32)],
        compiler_params=params(16),
        cost_estimate=pl.CostEstimate(flops=30_000_000, bytes_accessed=1 << 20, transcendentals=0),
        name="tables",
    )(sample_ids.reshape(total, LANES), sample_counts.reshape(total, LANES))


def owner_body(
    got_ref,
    items_ref,
    mass_ref,
    tabs_ref,
    dq_hbm,
    weight_hbm,
    q_hbm,
    loss_ref,
    got32_ref,
    dq32_ref,
    dq_ref,
    weight_ref,
    q_ref,
    dq_sem,
    weight_sem,
    q_sem,
):
    devices, rows, width = got_ref.shape
    local = q_ref.shape[0]
    chunks = tabs_ref.shape[1] // 3
    got32_ref[...] = got_ref[...].astype(F32).reshape(devices * rows, width)
    tail = got32_ref[pl.ds(2 * local, devices, stride=rows), :].T
    pairs = 2 * devices
    item_at = iota((LANES, pairs), 0)
    row_at = iota((chunks, pairs), 0)
    loss_lane = iota((1, LANES), 1)
    losses = jnp.zeros((1, LANES), F32)
    mass = mass_ref[...]
    stores = []
    for k in range(local):
        marks = []
        for c in range(2):
            top = tail[(2 * c) * local + k : (2 * c) * local + k + 1, :]
            low = tail[(2 * c + 1) * local + k : (2 * c + 1) * local + k + 1, :]
            marks.append(top * 64.0 + low)
        mark = jnp.concatenate(marks, axis=1)
        live = mark > 0.0
        target = jnp.where(live, mark - 1.0, 0.0).astype(jnp.int32)
        pick = one_hot(item_at == (target & (LANES - 1)))
        found = mm(tabs_ref[k], pick)
        found = found[0:chunks] + found[chunks : 2 * chunks] + found[2 * chunks : 3 * chunks]
        packed = jnp.sum(
            jnp.where(row_at == (target >> 7), found, 0.0), axis=0, keepdims=True
        ).astype(jnp.int32)
        item = jnp.where(live, packed >> 12, -1)
        count = (packed & 4095).astype(F32)
        queries = jnp.concatenate(
            [
                got32_ref[pl.ds(k, devices, stride=rows), :],
                got32_ref[pl.ds(local + k, devices, stride=rows), :],
            ],
            axis=0,
        ).astype(BF16)
        q_ref[k] = queries
        stores.append(pltpu.make_async_copy(q_ref.at[k], q_hbm.at[k], q_sem.at[k]))
        stores[-1].start()
        block = items_ref[k * LANES : (k + 1) * LANES, :]
        column = mass[:, k : k + 1]
        scores = mm(block, queries, ((1,), (1,)))
        masked = jnp.where(column > 0.0, scores, NONE)
        top = jnp.max(masked, axis=0, keepdims=True)
        expo = jnp.exp(masked - top) * column
        total = jnp.sum(expo, axis=0, keepdims=True)
        hit = item_at == item
        picked = jnp.sum(jnp.where(hit, scores, 0.0), axis=0, keepdims=True)
        loss = jnp.log(total) + top - (picked - jnp.log(count))
        loss = jnp.sum(jnp.where(live, loss, 0.0), axis=1, keepdims=True) / jnp.sum(
            jnp.where(live, 1.0, 0.0), axis=1, keepdims=True
        )
        losses = jnp.where(loss_lane == k, loss, losses)
        weight = (expo * (1.0 / total) - jnp.where(hit, 1.0, 0.0)).astype(BF16)
        weight_ref[k] = weight
        stores.append(pltpu.make_async_copy(weight_ref.at[k], weight_hbm.at[k], weight_sem.at[k]))
        stores[-1].start()
        dq = mm(weight, block, ((0,), (0,)))
        dq32_ref[pl.ds(k, devices, stride=2 * local), :] = dq[0:devices, :]
        dq32_ref[pl.ds(local + k, devices, stride=2 * local), :] = dq[devices:pairs, :]
    loss_ref[...] = losses
    quarter = devices // 4
    for part in range(4):
        span = pl.ds(part * quarter, quarter)
        flat = quarter * 2 * local
        dq_ref[span] = (
            dq32_ref[part * flat : (part + 1) * flat, :]
            .reshape(quarter, 2 * local, width)
            .astype(BF16)
        )
        stores.append(pltpu.make_async_copy(dq_ref.at[span], dq_hbm.at[span], dq_sem.at[part]))
        stores[-1].start()
    for store in stores:
        store.wait()


def owner(got, items, mass, tabs):
    devices, rows, width = got.shape
    local = items.shape[0] // LANES
    outs = (
        jax.ShapeDtypeStruct((devices, 2 * local, width), BF16),
        jax.ShapeDtypeStruct((local, LANES, 2 * devices), BF16),
        jax.ShapeDtypeStruct((local, 2 * devices, width), BF16),
    )
    return pl.pallas_call(
        owner_body,
        out_shape=outs_hbm(outs) + (jax.ShapeDtypeStruct((1, LANES), F32),),
        in_specs=vmem(4),
        out_specs=hbm(3) + vmem(1),
        scratch_shapes=[
            pltpu.VMEM((devices * rows, width), F32),
            pltpu.VMEM((devices * 2 * local, width), F32),
        ]
        + [pltpu.VMEM(a.shape, a.dtype) for a in outs]
        + [
            pltpu.SemaphoreType.DMA((4,)),
            pltpu.SemaphoreType.DMA((local,)),
            pltpu.SemaphoreType.DMA((local,)),
        ],
        compiler_params=params(40),
        name="owner",
    )(got, items, mass, tabs)


def item_body(weight_ref, q_ref, grad_ref):
    for k in range(weight_ref.shape[0]):
        grad_ref[k * LANES : (k + 1) * LANES, :] = mm(weight_ref[k], q_ref[k])


def item_grads(weight, queries):
    local, pairs, width = queries.shape
    step = 4
    return pl.pallas_call(
        item_body,
        grid=(local // step,),
        out_shape=jax.ShapeDtypeStruct((local * LANES, width), F32),
        in_specs=[
            pl.BlockSpec((step, LANES, pairs), lambda k: (k, 0, 0)),
            pl.BlockSpec((step, pairs, width), lambda k: (k, 0, 0)),
        ],
        out_specs=pl.BlockSpec((step * LANES, width), lambda k: (k, 0)),
        compiler_params=params(8),
        cost_estimate=pl.CostEstimate(
            flops=135_000_000, bytes_accessed=3 << 20, transcendentals=0
        ),
        name="item_grads",
    )(weight, queries)


def ready_body(mine_ref, theirs_ref, hidden_ref, slope_ref):
    users = mine_ref.shape[0]
    for i, ref in enumerate((mine_ref, theirs_ref)):
        pre = ref[...]
        sig = jax.nn.sigmoid(pre)
        hidden_ref[:, i * users : (i + 1) * users] = (pre * sig).T.astype(BF16)
        slope_ref[i * users : (i + 1) * users, :] = sig * (1.0 + pre * (1.0 - sig))


def ready(mine, theirs):
    users, half = mine.shape
    return pl.pallas_call(
        ready_body,
        out_shape=(
            jax.ShapeDtypeStruct((half, 2 * users), BF16),
            jax.ShapeDtypeStruct((2 * users, half), F32),
        ),
        in_specs=vmem(2),
        out_specs=vmem(2),
        compiler_params=params(16),
        cost_estimate=pl.CostEstimate(
            flops=3_000_000, bytes_accessed=3 << 20, transcendentals=1 << 19
        ),
        name="ready",
    )(mine, theirs)


def collect_body(back_ref, place_hbm, dq_ref, place_ref, sem):
    devices, rows, width = back_ref.shape
    parts = sem.shape[0]
    step = place_ref.shape[0] // parts
    loads = []
    for i in range(parts):
        span = pl.ds(i * step, step)
        loads.append(
            pltpu.make_async_copy(place_hbm.at[span, :], place_ref.at[span, :], sem.at[i])
        )
        loads[-1].start()
    total = jnp.zeros((width, place_ref.shape[1]), F32)
    group = devices // parts
    for i in range(parts):
        back = back_ref[i * group : (i + 1) * group].reshape(step, width)
        loads[i].wait()
        total = total + mm(back, place_ref[i * step : (i + 1) * step, :], ((0,), (0,)))
    dq_ref[...] = total.T.astype(BF16)


def collect(back, place):
    users = place.shape[1]
    return pl.pallas_call(
        collect_body,
        out_shape=jax.ShapeDtypeStruct((users, back.shape[2]), BF16),
        in_specs=vmem(1) + hbm(1),
        out_specs=vmem(1)[0],
        scratch_shapes=[pltpu.VMEM(place.shape, BF16), pltpu.SemaphoreType.DMA((4,))],
        compiler_params=params(24),
        name="collect",
    )(back, place)


def tower_body(dq_ref, other_ref, hidden_ref, slope_ref, feat_ref, feat_other_ref, wo_ref, grad_ref):
    users = dq_ref.shape[0]
    half = hidden_ref.shape[0]
    peers = grad_ref.shape[0]
    core = lax.axis_index("dev") % 2
    w_out = wo_ref[pl.ds(pl.multiple_of(core * half, half), half), :]
    big = None
    small = None
    for i, (dq, feat) in enumerate(((dq_ref, feat_ref), (other_ref, feat_other_ref))):
        dq = dq[...]
        dhidden = mm(dq, w_out, ((1,), (1,)))
        dpre = (dhidden * slope_ref[i * users : (i + 1) * users, :]).astype(BF16)
        part = mm(feat[...], dpre)
        big = part if big is None else big + part
        part = mm(hidden_ref[:, i * users : (i + 1) * users], dq)
        small = part if small is None else small + part
    tall = big.shape[0] // peers
    blocks = half // LANES
    for c in range(blocks):
        grad_ref[:, c * tall : (c + 1) * tall, :] = (
            big[:, c * LANES : (c + 1) * LANES].reshape(peers, tall, LANES).astype(BF16)
        )
    filled = half // 8
    at = blocks * tall
    grad_ref[0:filled, at : at + 8, :] = small.reshape(filled, 8, LANES).astype(BF16)
    grad_ref[filled:peers, at : at + 8, :] = jnp.zeros((peers - filled, 8, LANES), BF16)


def tower_back(dq, other, hidden, slope, features_t, features_other_t, w_out, peers):
    half = hidden.shape[0]
    rows = half * features_t.shape[0] // peers // LANES + 8
    return pl.pallas_call(
        tower_body,
        out_shape=jax.ShapeDtypeStruct((peers, rows, LANES), BF16),
        in_specs=vmem(7),
        out_specs=vmem(1)[0],
        compiler_params=params(40),
        name="tower_back",
    )(dq, other, hidden, slope, features_t, features_other_t, w_out)


def sum_body(parts_ref, out_ref):
    total = jnp.sum(parts_ref[...].astype(F32), axis=0, keepdims=True)
    out_ref[...] = jnp.broadcast_to(total, out_ref.shape).astype(BF16)


def sum_parts(parts):
    return pl.pallas_call(
        sum_body,
        out_shape=jax.ShapeDtypeStruct(parts.shape, BF16),
        in_specs=vmem(1),
        out_specs=vmem(1)[0],
        compiler_params=params(24),
        name="sum_parts",
    )(parts)


def spread_body(mine_ref, other_ref, hidden_ref, out_ref):
    peers = mine_ref.shape[0]
    core = lax.axis_index("dev") % 2
    half = out_ref.shape[0] // 2
    tall = hidden_ref.shape[0] // peers
    blocks = half // LANES
    filled = half // 8
    for side, ref in ((core, mine_ref), (1 - core, other_ref)):
        got = ref[...].astype(F32)
        for c in range(blocks):
            at = pl.multiple_of(side * half + c * LANES, LANES)
            hidden_ref[:, pl.ds(at, LANES)] = got[:, c * tall : (c + 1) * tall, :].reshape(
                hidden_ref.shape[0], LANES
            )
        at = blocks * tall
        out_ref[pl.ds(pl.multiple_of(side * half, half), half), :] = got[
            0:filled, at : at + 8, :
        ].reshape(half, LANES)


def spread(mine, other, hidden_shape, out_shape):
    return pl.pallas_call(
        spread_body,
        out_shape=(
            jax.ShapeDtypeStruct(hidden_shape, F32),
            jax.ShapeDtypeStruct(out_shape, F32),
        ),
        in_specs=vmem(2),
        out_specs=vmem(2),
        compiler_params=params(24),
        name="spread",
    )(mine, other)


def exchange(x):
    return lax.all_to_all(x, "dev", split_axis=0, concat_axis=0, tiled=True)


def exchange_peers(x):
    devices = lax.axis_size("dev")
    groups = [list(range(c, devices, 2)) for c in range(2)]
    return lax.all_to_all(
        x, "dev", split_axis=0, concat_axis=0, axis_index_groups=groups, tiled=True
    )


def swap(x):
    devices = lax.axis_size("dev")
    return lax.ppermute(x, "dev", [(d, d ^ 1) for d in range(devices)])


def local(
    features, w_hidden, w_out, items, routes, cluster_slot, sample_ids, sample_counts, positives
):
    devices = lax.axis_size("dev")
    features_other = swap(features)
    send, place, mine, other = route(
        routes, positives, cluster_slot, features, w_hidden, w_out, devices
    )
    mass, tabs = tables(sample_ids, sample_counts)
    got = exchange(send)
    theirs = swap(other)
    got, mass, tabs, theirs, features_other = lax.optimization_barrier(
        (got, mass, tabs, theirs, features_other)
    )
    dq_slots, weight, queries, losses = owner(got, items, mass, tabs)
    back = exchange(dq_slots)
    hidden, slope = ready(mine, theirs)
    item_grad = item_grads(weight, queries)
    features_t, features_other_t = features.T, features_other.T
    back, hidden, slope, item_grad, features_t, features_other_t = lax.optimization_barrier(
        (back, hidden, slope, item_grad, features_t, features_other_t)
    )
    dq = collect(back, place)
    partial = tower_back(
        dq, swap(dq), hidden, slope, features_t, features_other_t, w_out, devices // 2
    )
    summed = exchange_peers(sum_parts(exchange_peers(partial)))
    grad_hidden, grad_out = spread(summed, swap(summed), w_hidden.shape, w_out.shape)
    slot_loss = losses[0, : sample_ids.shape[0]]
    return (slot_loss, grad_hidden, grad_out, item_grad)


def solution(mesh):
    in_specs = (
        P("dev", None),
        P(),
        P(),
        P("dev", None),
        P("dev", None),
        P(),
        P("dev", None),
        P("dev", None),
        P("dev", None),
    )
    out_specs = (P("dev"), P(), P(), P("dev", None))
    return jax.shard_map(local, mesh=mesh, in_specs=in_specs, out_specs=out_specs, check_vma=False)
```

```python
import jax
import jax.numpy as jnp
from jax import lax
from jax.experimental import pallas as pl
from jax.experimental.pallas import tpu as pltpu
from jax.sharding import PartitionSpec as P

F32 = jnp.float32
BF16 = jnp.bfloat16
NONE = -3.0e38
KEY = 4096
AHEAD = 1
LANES = 128


def vmem(count):
    return [pl.BlockSpec(memory_space=pltpu.VMEM)] * count


def in_hbm(arrays):
    return tuple(pltpu.with_memory_space_constraint(a, pltpu.HBM) for a in arrays)


def outs_hbm(arrays):
    return tuple(pltpu.HBM(a.shape, a.dtype) for a in arrays)


def hbm(count):
    return [pl.BlockSpec(memory_space=pltpu.HBM)] * count


def params(megabytes):
    return pltpu.CompilerParams(vmem_limit_bytes=megabytes << 20)


def iota(shape, axis):
    return lax.broadcasted_iota(jnp.int32, shape, axis)


def one_hot(mask):
    return jnp.where(mask, 1.0, 0.0).astype(BF16)


def mm(a, b, dims=((1,), (0,))):
    return lax.dot_general(a, b, (dims, ((), ())), preferred_element_type=F32)


def route_body(
    routes_hbm,
    pos_hbm,
    cslot_hbm,
    feat_hbm,
    wh_hbm,
    wo_hbm,
    send_hbm,
    named_hbm,
    mine_hbm,
    other_hbm,
    routes_ref,
    pos_ref,
    cslot_ref,
    feat_ref,
    wh_ref,
    wo_ref,
    send_ref,
    named_ref,
    mine_ref,
    other_ref,
    place_ref,
    in_sem,
    out_sem,
    send_sem,
):
    loads = [
        pltpu.make_async_copy(src, dst, in_sem.at[i])
        for i, (src, dst) in enumerate(
            [
                (routes_hbm, routes_ref),
                (pos_hbm, pos_ref),
                (cslot_hbm, cslot_ref),
                (feat_hbm, feat_ref),
                (wh_hbm, wh_ref),
                (wo_hbm, wo_ref),
            ]
        )
    ]
    for load in loads:
        load.start()
    visits, users = routes_ref.shape
    clusters = cslot_ref.shape[0] * LANES
    devices, rows, width = send_ref.shape
    local = clusters // devices
    for load in loads[:3]:
        load.wait()
    cslot = cslot_ref[...]
    row_at = iota((cslot.shape[0], LANES), 0)
    user_at = iota((1, users), 1)
    slots = []
    keys = []
    for r in range(visits):
        found = []
        for part in range(users // LANES):
            cluster = routes_ref[r : r + 1, part * LANES : (part + 1) * LANES]
            lane = jnp.broadcast_to(cluster & (LANES - 1), cslot.shape)
            row = jnp.take_along_axis(cslot, lane, axis=1)
            found.append(
                jnp.sum(jnp.where(row_at == (cluster >> 7), row, 0), axis=0, keepdims=True)
            )
        slots.append(jnp.concatenate(found, axis=1).astype(F32))
        keys.append((user_at * KEY + pos_ref[r : r + 1, :] + 1).astype(F32))
    block = LANES
    groups = block // local
    sub = iota((block, users), 0).astype(F32)
    lane_user = iota((block, users), 1).astype(F32)
    tail_lane = iota((block, LANES), 1)
    tail_row = iota((block, LANES), 0)
    tail_hit = ((tail_lane & (local - 1)) == (tail_row & (local - 1))) & (tail_lane < 4 * local)
    tail_kind = tail_lane // local
    stores = []
    named_lane = iota((block, LANES), 1)
    named = [jnp.zeros((block, LANES), F32)]

    def assign(b):
        slot_at = sub + float(b * block)
        key = jnp.zeros((block, users), F32)
        for r in range(visits):
            key = jnp.where(slot_at == slots[r], keys[r], key)
        most = jnp.max(key, axis=1, keepdims=True)
        rest = jnp.sum(key, axis=1, keepdims=True) - most
        ends = []
        parts = []
        for c, chosen in enumerate((most, rest)):
            user = jnp.floor((chosen - 1.0) * (1.0 / KEY))
            named[0] = jnp.where(named_lane == 2 * b + c, user, named[0])
            mark = jnp.where(chosen > 0.0, chosen - user * KEY, 0.0)
            top = jnp.floor(mark * (1.0 / 64.0))
            ends += [top, mark - top * 64.0]
            parts.append(jnp.where(lane_user == user, 1.0, 0.0).reshape(block // 8, 8, users))
        place = jnp.concatenate(parts, axis=1).reshape(2 * block, users).astype(BF16)
        span = pl.ds(b * 2 * block, 2 * block)
        place_ref[span, :] = place
        tail = jnp.where(
            tail_kind == 0,
            ends[0],
            jnp.where(tail_kind == 1, ends[1], jnp.where(tail_kind == 2, ends[2], ends[3])),
        )
        tail = jnp.where(tail_hit, tail, 0.0).reshape(groups, local, LANES)
        tail = jnp.sum(tail, axis=1)
        send_ref[b * groups : (b + 1) * groups, 2 * local : rows, :] = jnp.broadcast_to(
            tail[:, None, :], (groups, rows - 2 * local, width)
        ).astype(BF16)

    early = 6
    for b in range(early):
        assign(b)
    for load in loads[3:]:
        load.wait()
    pre = mm(feat_ref[...], wh_ref[...])
    half = pre.shape[1] // 2
    core = lax.axis_index("dev") % 2
    mine_ref[...] = jnp.where(core == 0, pre[:, 0:half], pre[:, half:])
    other_ref[...] = jnp.where(core == 0, pre[:, half:], pre[:, 0:half])
    for src, dst, i in ((mine_ref, mine_hbm, 0), (other_ref, other_hbm, 1)):
        stores.append(pltpu.make_async_copy(src, dst, out_sem.at[i]))
        stores[-1].start()
    hidden = (pre * jax.nn.sigmoid(pre)).astype(BF16)
    query = mm(hidden, wo_ref[...]).astype(BF16)
    blocks = clusters // block
    for b in range(blocks):
        if b + early < blocks:
            assign(b + early)
        if b + early == blocks:
            named_ref[...] = named[0]
            stores.append(pltpu.make_async_copy(named_ref, named_hbm, out_sem.at[2]))
            stores[-1].start()
        sent = mm(place_ref[b * 2 * block : (b + 1) * 2 * block, :], query).astype(BF16)
        span = pl.ds(b * groups, groups)
        send_ref[span, 0 : 2 * local, :] = sent.reshape(groups, 2 * local, width)
        if b % 4 == 3:
            span = pl.ds((b - 3) * groups, 4 * groups)
            stores.append(
                pltpu.make_async_copy(send_ref.at[span], send_hbm.at[span], send_sem.at[b // 4])
            )
            stores[-1].start()
    for store in stores:
        store.wait()


def route(routes, positives, cluster_slot, features, w_hidden, w_out, devices):
    users, visits = routes.shape
    clusters = cluster_slot.shape[0]
    width = w_out.shape[1]
    hid = w_hidden.shape[1]
    rows = 2 * clusters // devices + 8
    args = (
        routes.T,
        positives.T,
        cluster_slot.reshape(clusters // LANES, LANES),
        features,
        w_hidden,
        w_out,
    )
    outs = (
        jax.ShapeDtypeStruct((devices, rows, width), BF16),
        jax.ShapeDtypeStruct((LANES, LANES), F32),
        jax.ShapeDtypeStruct((users, hid // 2), F32),
        jax.ShapeDtypeStruct((users, hid // 2), F32),
    )
    return pl.pallas_call(
        route_body,
        out_shape=outs_hbm(outs),
        in_specs=hbm(6),
        out_specs=hbm(4),
        scratch_shapes=[pltpu.VMEM(a.shape, a.dtype) for a in args + outs]
        + [
            pltpu.VMEM((2 * clusters, users), BF16),
            pltpu.SemaphoreType.DMA((6,)),
            pltpu.SemaphoreType.DMA((3,)),
            pltpu.SemaphoreType.DMA((4,)),
        ],
        compiler_params=params(48),
        name="route",
    )(*in_hbm(args))


def table_body(ids_ref, counts_ref, mass_hbm, tabs_hbm, inv_ref, mass_ref, tabs_ref, sem):
    clusters, chunks, lanes = tabs_ref.shape
    inv_ref[...] = 1.0 / counts_ref[...].astype(F32)
    tabs_ref[...] = ((ids_ref[...] << 12) | counts_ref[...]).reshape(tabs_ref.shape)
    store = pltpu.make_async_copy(tabs_ref, tabs_hbm, sem.at[0])
    store.start()
    item_at = iota((LANES, LANES), 0)

    def cluster(k, carry):
        acc = jnp.zeros((LANES, LANES), F32)
        for h in range(chunks):
            at = k * chunks + h
            hit = item_at == ids_ref[pl.ds(at, 1), :]
            acc = acc + jnp.where(hit, inv_ref[pl.ds(at, 1), :], 0.0)
        mass_ref[k] = jnp.broadcast_to(jnp.sum(acc, axis=1, keepdims=True), acc.shape)
        return carry

    lax.fori_loop(0, clusters, cluster, 0)
    last = pltpu.make_async_copy(mass_ref, mass_hbm, sem.at[1])
    last.start()
    last.wait()
    store.wait()


def tables(sample_ids, sample_counts):
    clusters, samples = sample_ids.shape
    total = sample_ids.size // LANES
    outs = (
        jax.ShapeDtypeStruct((clusters, LANES, LANES), F32),
        jax.ShapeDtypeStruct((clusters, samples // LANES, LANES), jnp.int32),
    )
    return pl.pallas_call(
        table_body,
        out_shape=outs_hbm(outs),
        in_specs=vmem(2),
        out_specs=hbm(2),
        scratch_shapes=[pltpu.VMEM((total, LANES), F32)]
        + [pltpu.VMEM(a.shape, a.dtype) for a in outs]
        + [pltpu.SemaphoreType.DMA((2,))],
        compiler_params=params(16),
        cost_estimate=pl.CostEstimate(flops=30_000_000, bytes_accessed=1 << 20, transcendentals=0),
        name="tables",
    )(sample_ids.reshape(total, LANES), sample_counts.reshape(total, LANES))


def row_of(slot):
    return slot // 8 * 16 + slot % 8


def owner_body(
    got_ref,
    items_hbm,
    mass_hbm,
    tabs_hbm,
    dq_hbm,
    weight_hbm,
    q_hbm,
    loss_ref,
    got32_ref,
    dq32_ref,
    dq_ref,
    weight_ref,
    q_ref,
    items_ref,
    mass_ref,
    tabs_ref,
    losses_ref,
    load_sem,
    dq_sem,
    weight_sem,
    q_sem,
):
    loads = [
        pltpu.make_async_copy(tabs_hbm, tabs_ref, load_sem.at[0]),
        pltpu.make_async_copy(items_hbm, items_ref, load_sem.at[1]),
    ]
    for part in range(mass_ref.shape[0] // 4):
        span = pl.ds(part * 4, 4)
        loads.append(
            pltpu.make_async_copy(mass_hbm.at[span], mass_ref.at[span], load_sem.at[2 + part])
        )
    for load in loads:
        load.start()
    devices, rows, width = got_ref.shape
    local = q_ref.shape[0]
    chunks = tabs_ref.shape[1]
    pairs = 2 * devices
    got32_ref[...] = got_ref[...].astype(F32).reshape(devices * rows, width)
    tail = got32_ref[pl.ds(2 * local, devices, stride=rows), :].T
    marks = [
        tail[2 * c * local : (2 * c + 1) * local, :] * 64.0
        + tail[(2 * c + 1) * local : (2 * c + 2) * local, :]
        for c in range(2)
    ]
    targets = [jnp.maximum(mark - 1.0, 0.0).astype(jnp.int32) for mark in marks]
    item_at = iota((LANES, pairs), 0)
    row_at = iota((chunks, devices), 0)
    for load in loads[0:2]:
        load.wait()
    stores = []

    def fetch(k):
        packed = []
        for target in targets:
            at = target[k : k + 1, :]
            lane = jnp.broadcast_to(at & (LANES - 1), (chunks, devices))
            found = jnp.take_along_axis(tabs_ref[k], lane, axis=1)
            packed.append(jnp.sum(jnp.where(row_at == (at >> 7), found, 0), axis=0, keepdims=True))
        packed = jnp.concatenate(packed, axis=1)
        live = jnp.concatenate([mark[k : k + 1, :] for mark in marks], axis=1) > 0.0
        queries = jnp.concatenate(
            [
                got32_ref[pl.ds(row_of(k), devices, stride=rows), :],
                got32_ref[pl.ds(row_of(k) + 8, devices, stride=rows), :],
            ],
            axis=0,
        ).astype(BF16)
        q_ref[k] = queries
        stores.append(pltpu.make_async_copy(q_ref.at[k], q_hbm.at[k], q_sem.at[k]))
        stores[-1].start()
        scores = mm(items_ref[k * LANES : (k + 1) * LANES, :], queries, ((1,), (1,)))
        return live, packed, scores

    def soften(k, live, packed, scores):
        item = jnp.where(live, packed >> 12, -1)
        count = (packed & 4095).astype(F32)
        if k % 4 == 0:
            loads[2 + k // 4].wait()
        column = jnp.concatenate([mass_ref[k]] * (pairs // LANES), axis=1)
        masked = jnp.where(column > 0.0, scores, NONE)
        top = jnp.max(masked, axis=0, keepdims=True)
        expo = jnp.exp(masked - top) * column
        total = jnp.sum(expo, axis=0, keepdims=True)
        hit = item_at == item
        picked = jnp.sum(jnp.where(hit, scores, 0.0), axis=0, keepdims=True)
        losses_ref[k : k + 1, :] = jnp.log(total) + top - (picked - jnp.log(count))
        weight = (expo * (1.0 / total) - jnp.where(hit, 1.0, 0.0)).astype(BF16)
        weight_ref[k] = weight
        stores.append(pltpu.make_async_copy(weight_ref.at[k], weight_hbm.at[k], weight_sem.at[k]))
        stores[-1].start()
        return weight

    def give(k, weight):
        dq = mm(weight, items_ref[k * LANES : (k + 1) * LANES, :], ((0,), (0,)))
        dq32_ref[pl.ds(row_of(k), devices, stride=rows), :] = dq[0:devices, :]
        dq32_ref[pl.ds(row_of(k) + 8, devices, stride=rows), :] = dq[devices:pairs, :]
        if k % 8 == 7:
            at = row_of(k) - 7
            dq_ref[:, at : at + 16, :] = (
                dq32_ref[...].reshape(devices, rows, width)[:, at : at + 16, :].astype(BF16)
            )
            span = (slice(None), pl.ds(at, 16))
            stores.append(
                pltpu.make_async_copy(dq_ref.at[span], dq_hbm.at[span], dq_sem.at[k // 8])
            )
            stores[-1].start()

    fetched = [fetch(k) for k in range(AHEAD)]
    for k in range(local):
        if k + AHEAD < local:
            fetched.append(fetch(k + AHEAD))
        give(k, soften(k, *fetched[k]))
    live = jnp.concatenate(marks, axis=1) > 0.0
    total = jnp.sum(jnp.where(live, losses_ref[...], 0.0), axis=1, keepdims=True)
    loss_ref[...] = total / jnp.sum(jnp.where(live, 1.0, 0.0), axis=1, keepdims=True)
    for store in stores:
        store.wait()


def owner(got, items, mass, tabs):
    devices, rows, width = got.shape
    local = items.shape[0] // LANES
    outs = (
        jax.ShapeDtypeStruct((devices, 2 * local, width), BF16),
        jax.ShapeDtypeStruct((local, LANES, 2 * devices), BF16),
        jax.ShapeDtypeStruct((local, 2 * devices, width), BF16),
    )
    return pl.pallas_call(
        owner_body,
        out_shape=outs_hbm(outs) + (jax.ShapeDtypeStruct((local, 1), F32),),
        in_specs=vmem(1) + hbm(3),
        out_specs=hbm(3) + vmem(1),
        scratch_shapes=[
            pltpu.VMEM((devices * rows, width), F32),
            pltpu.VMEM((devices * rows, width), F32),
        ]
        + [pltpu.VMEM(a.shape, a.dtype) for a in outs + (items, mass, tabs)]
        + [
            pltpu.VMEM((local, 2 * devices), F32),
            pltpu.SemaphoreType.DMA((2 + local // 4,)),
            pltpu.SemaphoreType.DMA((local // 8,)),
            pltpu.SemaphoreType.DMA((local,)),
            pltpu.SemaphoreType.DMA((local,)),
        ],
        compiler_params=params(40),
        name="owner",
    )(got, *in_hbm((items, mass, tabs)))


def item_body(weight_ref, q_ref, grad_ref):
    for k in range(weight_ref.shape[0]):
        grad_ref[k * LANES : (k + 1) * LANES, :] = mm(weight_ref[k], q_ref[k])


def item_grads(weight, queries):
    local, pairs, width = queries.shape
    step = 4
    return pl.pallas_call(
        item_body,
        grid=(local // step,),
        out_shape=jax.ShapeDtypeStruct((local * LANES, width), F32),
        in_specs=[
            pl.BlockSpec((step, LANES, pairs), lambda k: (k, 0, 0)),
            pl.BlockSpec((step, pairs, width), lambda k: (k, 0, 0)),
        ],
        out_specs=pl.BlockSpec((step * LANES, width), lambda k: (k, 0)),
        compiler_params=params(8),
        cost_estimate=pl.CostEstimate(
            flops=135_000_000, bytes_accessed=3 << 20, transcendentals=0
        ),
        name="item_grads",
    )(*in_hbm((weight, queries)))


def ready_body(mine_ref, theirs_ref, hidden_ref, slope_ref):
    for i, ref in enumerate((mine_ref, theirs_ref)):
        pre = ref[...]
        sig = jax.nn.sigmoid(pre)
        hidden_ref[i] = (pre * sig).T.astype(BF16)
        slope_ref[i] = sig * (1.0 + pre * (1.0 - sig))


def ready(mine, theirs):
    users, half = mine.shape
    step = users // 2
    outs = (
        jax.ShapeDtypeStruct((2, half, users), BF16),
        jax.ShapeDtypeStruct((2, users, half), F32),
    )
    return pl.pallas_call(
        ready_body,
        grid=(users // step,),
        out_shape=outs_hbm(outs),
        in_specs=[pl.BlockSpec((step, half), lambda i: (i, 0))] * 2,
        out_specs=[
            pl.BlockSpec((2, half, step), lambda i: (0, 0, i)),
            pl.BlockSpec((2, step, half), lambda i: (0, i, 0)),
        ],
        compiler_params=params(16),
        cost_estimate=pl.CostEstimate(
            flops=3_000_000, bytes_accessed=3 << 20, transcendentals=1 << 19
        ),
        name="ready",
    )(*in_hbm((mine, theirs)))


def collect_body(back_ref, named_ref, dq_ref):
    devices, rows, width = back_ref.shape
    users = dq_ref.shape[0]
    block = LANES
    named = named_ref[...]
    lane_user = iota((block, users), 1).astype(F32)
    total = jnp.zeros((width, users), F32)
    group = 2 * block // rows
    for b in range(devices // group):
        parts = [
            jnp.where(lane_user == named[:, 2 * b + c : 2 * b + c + 1], 1.0, 0.0).reshape(
                block // 8, 8, users
            )
            for c in range(2)
        ]
        place = jnp.concatenate(parts, axis=1).reshape(2 * block, users).astype(BF16)
        back = back_ref[b * group : (b + 1) * group].reshape(2 * block, width)
        total = total + mm(back, place, ((0,), (0,)))
    dq_ref[...] = total.T.astype(BF16)


def collect(back, named, users):
    return pl.pallas_call(
        collect_body,
        out_shape=jax.ShapeDtypeStruct((users, back.shape[2]), BF16),
        in_specs=vmem(2),
        out_specs=vmem(1)[0],
        compiler_params=params(24),
        name="collect",
    )(back, named)


def tower_body(
    dq_ref,
    other_ref,
    hidden_hbm,
    slope_hbm,
    feat_hbm,
    feat_other_hbm,
    wo_hbm,
    grad_ref,
    hidden_ref,
    slope_ref,
    feat_ref,
    feat_other_ref,
    wo_ref,
    sem,
):
    users = dq_ref.shape[0]
    half = hidden_ref.shape[1]
    peers = grad_ref.shape[0]
    core = lax.axis_index("dev") % 2
    wo_at = wo_hbm.at[pl.ds(pl.multiple_of(core * half, half), half), :]
    loads = [
        pltpu.make_async_copy(src, dst, sem.at[i])
        for i, (src, dst) in enumerate(
            [
                (wo_at, wo_ref),
                (slope_hbm, slope_ref),
                (feat_hbm, feat_ref),
                (feat_other_hbm, feat_other_ref),
                (hidden_hbm, hidden_ref),
            ]
        )
    ]
    for load in loads:
        load.start()
    for load in loads[:2]:
        load.wait()
    w_out = wo_ref[...]
    dqs = (dq_ref[...], other_ref[...])
    dpres = [
        (mm(dq, w_out, ((1,), (1,))) * slope_ref[i]).astype(BF16) for i, dq in enumerate(dqs)
    ]
    loads[2].wait()
    big = mm(feat_ref[...], dpres[0])
    loads[3].wait()
    big = big + mm(feat_other_ref[...], dpres[1])
    loads[4].wait()
    small = mm(hidden_ref[0], dqs[0]) + mm(hidden_ref[1], dqs[1])
    tall = big.shape[0] // peers
    blocks = half // LANES
    for c in range(blocks):
        grad_ref[:, c * tall : (c + 1) * tall, :] = (
            big[:, c * LANES : (c + 1) * LANES].reshape(peers, tall, LANES).astype(BF16)
        )
    filled = half // 8
    at = blocks * tall
    grad_ref[0:filled, at : at + 8, :] = small.reshape(filled, 8, LANES).astype(BF16)
    grad_ref[filled:peers, at : at + 8, :] = jnp.zeros((peers - filled, 8, LANES), BF16)


def tower_back(dq, other, hidden, slope, features_t, features_other_t, w_out, peers):
    half = hidden.shape[1]
    rows = half * features_t.shape[0] // peers // LANES + 8
    held = (hidden, slope, features_t, features_other_t)
    return pl.pallas_call(
        tower_body,
        out_shape=jax.ShapeDtypeStruct((peers, rows, LANES), BF16),
        in_specs=vmem(2) + hbm(5),
        out_specs=vmem(1)[0],
        scratch_shapes=[pltpu.VMEM(a.shape, a.dtype) for a in held]
        + [pltpu.VMEM((half, w_out.shape[1]), BF16), pltpu.SemaphoreType.DMA((5,))],
        compiler_params=params(40),
        name="tower_back",
    )(dq, other, *in_hbm(held + (w_out,)))


def sum_body(parts_ref, out_ref):
    total = jnp.sum(parts_ref[...].astype(F32), axis=0, keepdims=True)
    out_ref[...] = jnp.broadcast_to(total, out_ref.shape).astype(BF16)


def sum_parts(parts):
    return pl.pallas_call(
        sum_body,
        out_shape=jax.ShapeDtypeStruct(parts.shape, BF16),
        in_specs=vmem(1),
        out_specs=vmem(1)[0],
        compiler_params=params(24),
        name="sum_parts",
    )(parts)


def spread_body(mine_ref, other_ref, hidden_ref, out_ref):
    peers = mine_ref.shape[0]
    core = lax.axis_index("dev") % 2
    half = out_ref.shape[0] // 2
    tall = hidden_ref.shape[0] // peers
    blocks = half // LANES
    filled = half // 8
    for side, ref in ((core, mine_ref), (1 - core, other_ref)):
        got = ref[...].astype(F32)
        for c in range(blocks):
            at = pl.multiple_of(side * half + c * LANES, LANES)
            hidden_ref[:, pl.ds(at, LANES)] = got[:, c * tall : (c + 1) * tall, :].reshape(
                hidden_ref.shape[0], LANES
            )
        at = blocks * tall
        out_ref[pl.ds(pl.multiple_of(side * half, half), half), :] = got[
            0:filled, at : at + 8, :
        ].reshape(half, LANES)


def spread(mine, other, hidden_shape, out_shape):
    return pl.pallas_call(
        spread_body,
        out_shape=(
            jax.ShapeDtypeStruct(hidden_shape, F32),
            jax.ShapeDtypeStruct(out_shape, F32),
        ),
        in_specs=vmem(2),
        out_specs=vmem(2),
        compiler_params=params(24),
        name="spread",
    )(mine, other)


def exchange(x):
    return lax.all_to_all(x, "dev", split_axis=0, concat_axis=0, tiled=True)


def exchange_peers(x):
    devices = lax.axis_size("dev")
    groups = [list(range(c, devices, 2)) for c in range(2)]
    return lax.all_to_all(
        x, "dev", split_axis=0, concat_axis=0, axis_index_groups=groups, tiled=True
    )


def swap(x):
    devices = lax.axis_size("dev")
    return lax.ppermute(x, "dev", [(d, d ^ 1) for d in range(devices)])


def local(
    features, w_hidden, w_out, items, routes, cluster_slot, sample_ids, sample_counts, positives
):
    devices = lax.axis_size("dev")
    features_other = swap(features)
    send, named, mine, other = route(
        routes, positives, cluster_slot, features, w_hidden, w_out, devices
    )
    mass, tabs = tables(sample_ids, sample_counts)
    got = exchange(send)
    theirs = swap(other)
    got, mass, tabs, theirs, features_other = lax.optimization_barrier(
        (got, *in_hbm((mass, tabs)), theirs, features_other)
    )
    dq_slots, weight, queries, losses = owner(got, items, mass, tabs)
    back = exchange(dq_slots)
    hidden, slope = ready(mine, theirs)
    item_grad = item_grads(weight, queries)
    features_t, features_other_t = features.T, features_other.T
    back, hidden, slope, item_grad, features_t, features_other_t = lax.optimization_barrier(
        (back, hidden, slope, item_grad, features_t, features_other_t)
    )
    dq = collect(back, named, features.shape[0])
    partial = tower_back(
        dq, swap(dq), hidden, slope, features_t, features_other_t, w_out, devices // 2
    )
    summed = exchange_peers(sum_parts(exchange_peers(partial)))
    grad_hidden, grad_out = spread(summed, swap(summed), w_hidden.shape, w_out.shape)
    slot_loss = losses[:, 0]
    return (slot_loss, grad_hidden, grad_out, item_grad)


def solution(mesh):
    in_specs = (
        P("dev", None),
        P(),
        P(),
        P("dev", None),
        P("dev", None),
        P(),
        P("dev", None),
        P("dev", None),
        P("dev", None),
    )
    out_specs = (P("dev"), P(), P(), P("dev", None))
    return jax.shard_map(local, mesh=mesh, in_specs=in_specs, out_specs=out_specs, check_vma=False)
```

```python
import functools

import jax
import jax.numpy as jnp
from jax import lax
from jax.experimental import pallas as pl
from jax.experimental.pallas import tpu as pltpu
from jax.sharding import PartitionSpec as P

F32 = jnp.float32
BF16 = jnp.bfloat16
NONE = -3.0e38
KEY = 4096
AHEAD = 1
LANES = 128


def vmem(count):
    return [pl.BlockSpec(memory_space=pltpu.VMEM)] * count


def in_hbm(arrays):
    return tuple(pltpu.with_memory_space_constraint(a, pltpu.HBM) for a in arrays)


def outs_hbm(arrays):
    return tuple(pltpu.HBM(a.shape, a.dtype) for a in arrays)


def hbm(count):
    return [pl.BlockSpec(memory_space=pltpu.HBM)] * count


def params(megabytes):
    return pltpu.CompilerParams(vmem_limit_bytes=megabytes << 20)


def iota(shape, axis):
    return lax.broadcasted_iota(jnp.int32, shape, axis)


def one_hot(mask):
    return jnp.where(mask, 1.0, 0.0).astype(BF16)


def mm(a, b, dims=((1,), (0,))):
    return lax.dot_general(a, b, (dims, ((), ())), preferred_element_type=F32)


def route_body(
    routes_hbm,
    pos_hbm,
    cslot_hbm,
    feat_hbm,
    wh_hbm,
    wo_hbm,
    send_hbm,
    named_hbm,
    routes_ref,
    pos_ref,
    cslot_ref,
    feat_ref,
    wh_ref,
    wo_ref,
    send_ref,
    named_ref,
    place_ref,
    in_sem,
    out_sem,
    send_sem,
):
    loads = [
        pltpu.make_async_copy(src, dst, in_sem.at[i])
        for i, (src, dst) in enumerate(
            [
                (routes_hbm, routes_ref),
                (pos_hbm, pos_ref),
                (cslot_hbm, cslot_ref),
                (feat_hbm, feat_ref),
                (wh_hbm, wh_ref),
                (wo_hbm, wo_ref),
            ]
        )
    ]
    for load in loads:
        load.start()
    visits, users = routes_ref.shape
    clusters = cslot_ref.shape[0] * LANES
    devices, rows, width = send_ref.shape
    local = clusters // devices
    for load in loads[:3]:
        load.wait()
    cslot = cslot_ref[...]
    row_at = iota((cslot.shape[0], LANES), 0)
    user_at = iota((1, users), 1)
    slots = []
    keys = []
    for r in range(visits):
        found = []
        for part in range(users // LANES):
            cluster = routes_ref[r : r + 1, part * LANES : (part + 1) * LANES]
            lane = jnp.broadcast_to(cluster & (LANES - 1), cslot.shape)
            row = jnp.take_along_axis(cslot, lane, axis=1)
            found.append(
                jnp.sum(jnp.where(row_at == (cluster >> 7), row, 0), axis=0, keepdims=True)
            )
        slots.append(jnp.concatenate(found, axis=1).astype(F32))
        keys.append((user_at * KEY + pos_ref[r : r + 1, :] + 1).astype(F32))
    block = LANES
    groups = block // local
    sub = iota((block, users), 0).astype(F32)
    stores = []
    named_lane = iota((block, LANES), 1)
    named = [jnp.zeros((block, LANES), F32)]

    def assign(b):
        slot_at = sub + float(b * block)
        key = jnp.zeros((block, users), F32)
        for r in range(visits):
            key = jnp.where(slot_at == slots[r], keys[r], key)
        most = jnp.max(key, axis=1, keepdims=True)
        rest = jnp.sum(key, axis=1, keepdims=True) - most
        parts = []
        for c, chosen in enumerate((most, rest)):
            named[0] = jnp.where(named_lane == 2 * b + c, chosen, named[0])
            chosen = jnp.where(chosen > 0.0, chosen, -1.0)
            parts.append(jnp.where(key == chosen, 1.0, 0.0).reshape(block // 8, 8, users))
        place = jnp.concatenate(parts, axis=1).reshape(2 * block, users).astype(BF16)
        place_ref[b * 2 * block : (b + 1) * 2 * block, :] = place

    def name_users():
        user = jnp.floor((named[0] - 1.0) * (1.0 / KEY))
        named_ref[...] = user
        stores.append(pltpu.make_async_copy(named_ref, named_hbm, out_sem.at[0]))
        stores[-1].start()
        chosen = named[0].T
        user = jnp.floor((chosen - 1.0) * (1.0 / KEY))
        mark = jnp.where(chosen > 0.0, chosen - user * KEY, 0.0)
        top = jnp.floor(mark * (1.0 / 64.0))
        low = mark - top * 64.0
        for b in range(clusters // block):
            tail = jnp.concatenate([top[2 * b : 2 * b + 2], low[2 * b : 2 * b + 2]], axis=0)
            tail = jnp.concatenate([tail, tail], axis=0)
            send_ref[b * groups : (b + 1) * groups, 2 * local : rows, :] = jnp.broadcast_to(
                tail[None], (groups, rows - 2 * local, width)
            ).astype(BF16)
        span = (slice(None), pl.ds(2 * local, rows - 2 * local))
        stores.append(pltpu.make_async_copy(send_ref.at[span], send_hbm.at[span], out_sem.at[1]))
        stores[-1].start()

    early = 4
    for b in range(early):
        assign(b)
    for load in loads[3:]:
        load.wait()
    pre = mm(feat_ref[...], wh_ref[...])
    hidden = (pre * jax.nn.sigmoid(pre)).astype(BF16)
    query = mm(hidden, wo_ref[...]).astype(BF16)
    blocks = clusters // block
    for b in range(blocks):
        if b + early < blocks:
            assign(b + early)
        if b + early == blocks:
            name_users()
        sent = mm(place_ref[b * 2 * block : (b + 1) * 2 * block, :], query).astype(BF16)
        send_ref[b * groups : (b + 1) * groups, 0 : 2 * local, :] = sent.reshape(
            groups, 2 * local, width
        )
        if b % 4 == 3:
            span = (pl.ds((b - 3) * groups, 4 * groups), pl.ds(0, 2 * local))
            stores.append(
                pltpu.make_async_copy(send_ref.at[span], send_hbm.at[span], send_sem.at[b // 4])
            )
            stores[-1].start()
    for store in stores:
        store.wait()


def route(routes, positives, cluster_slot, features, w_hidden, w_out, devices):
    users, visits = routes.shape
    clusters = cluster_slot.shape[0]
    width = w_out.shape[1]
    rows = 2 * clusters // devices + 8
    args = (
        routes.T,
        positives.T,
        cluster_slot.reshape(clusters // LANES, LANES),
        features,
        w_hidden,
        w_out,
    )
    outs = (
        jax.ShapeDtypeStruct((devices, rows, width), BF16),
        jax.ShapeDtypeStruct((LANES, LANES), F32),
    )
    return pl.pallas_call(
        route_body,
        out_shape=outs_hbm(outs),
        in_specs=hbm(6),
        out_specs=hbm(2),
        scratch_shapes=[pltpu.VMEM(a.shape, a.dtype) for a in args + outs]
        + [
            pltpu.VMEM((2 * clusters, users), BF16),
            pltpu.SemaphoreType.DMA((6,)),
            pltpu.SemaphoreType.DMA((2,)),
            pltpu.SemaphoreType.DMA((4,)),
        ],
        compiler_params=params(48),
        name="route",
    )(*in_hbm(args))


def table_body(ids_ref, counts_ref, mass_hbm, tabs_hbm, inv_ref, mass_ref, tabs_ref, sem):
    clusters, chunks, lanes = tabs_ref.shape
    inv_ref[...] = 1.0 / counts_ref[...].astype(F32)
    tabs_ref[...] = ((ids_ref[...] << 12) | counts_ref[...]).reshape(tabs_ref.shape)
    store = pltpu.make_async_copy(tabs_ref, tabs_hbm, sem.at[0])
    store.start()
    item_at = iota((LANES, LANES), 0)

    def cluster(k, carry):
        acc = jnp.zeros((LANES, LANES), F32)
        for h in range(chunks):
            at = k * chunks + h
            hit = item_at == ids_ref[pl.ds(at, 1), :]
            acc = acc + jnp.where(hit, inv_ref[pl.ds(at, 1), :], 0.0)
        mass_ref[k] = jnp.broadcast_to(jnp.sum(acc, axis=1, keepdims=True), acc.shape)
        return carry

    lax.fori_loop(0, clusters, cluster, 0)
    last = pltpu.make_async_copy(mass_ref, mass_hbm, sem.at[1])
    last.start()
    last.wait()
    store.wait()


def tables(sample_ids, sample_counts):
    clusters, samples = sample_ids.shape
    total = sample_ids.size // LANES
    outs = (
        jax.ShapeDtypeStruct((clusters, LANES, LANES), F32),
        jax.ShapeDtypeStruct((clusters, samples // LANES, LANES), jnp.int32),
    )
    return pl.pallas_call(
        table_body,
        out_shape=outs_hbm(outs),
        in_specs=vmem(2),
        out_specs=hbm(2),
        scratch_shapes=[pltpu.VMEM((total, LANES), F32)]
        + [pltpu.VMEM(a.shape, a.dtype) for a in outs]
        + [pltpu.SemaphoreType.DMA((2,))],
        compiler_params=params(16),
        cost_estimate=pl.CostEstimate(flops=30_000_000, bytes_accessed=1 << 20, transcendentals=0),
        name="tables",
    )(sample_ids.reshape(total, LANES), sample_counts.reshape(total, LANES))


def row_of(slot):
    return slot // 8 * 16 + slot % 8


def owner_body(
    got_ref,
    items_hbm,
    mass_hbm,
    tabs_hbm,
    dq_hbm,
    weight_hbm,
    q_hbm,
    loss_ref,
    got32_ref,
    dq32_ref,
    dq_ref,
    weight_ref,
    q_ref,
    items_ref,
    mass_ref,
    tabs_ref,
    losses_ref,
    load_sem,
    dq_sem,
    weight_sem,
    q_sem,
):
    loads = [
        pltpu.make_async_copy(tabs_hbm, tabs_ref, load_sem.at[0]),
        pltpu.make_async_copy(items_hbm, items_ref, load_sem.at[1]),
    ]
    for part in range(mass_ref.shape[0] // 4):
        span = pl.ds(part * 4, 4)
        loads.append(
            pltpu.make_async_copy(mass_hbm.at[span], mass_ref.at[span], load_sem.at[2 + part])
        )
    for load in loads:
        load.start()
    devices, rows, width = got_ref.shape
    local = q_ref.shape[0]
    chunks = tabs_ref.shape[1]
    pairs = 2 * devices
    got32_ref[...] = got_ref[...].astype(F32).reshape(devices * rows, width)
    place_at = lax.axis_index("dev") % (LANES // local) * local
    tail_lane = iota((devices, LANES), 1)
    tail = jnp.zeros((devices, LANES), F32)
    for c in range(2):
        top = got32_ref[pl.ds(2 * local + c, devices, stride=rows), :]
        low = got32_ref[pl.ds(2 * local + 2 + c, devices, stride=rows), :]
        moved = pltpu.roll(top * 64.0 + low, (LANES + c * local - place_at) % LANES, 1)
        tail = jnp.where(tail_lane // local == c, moved, tail)
    tail = tail.T
    marks = [tail[c * local : (c + 1) * local, :] for c in range(2)]
    targets = [jnp.maximum(mark - 1.0, 0.0).astype(jnp.int32) for mark in marks]
    item_at = iota((LANES, pairs), 0)
    row_at = iota((chunks, devices), 0)
    for load in loads[0:2]:
        load.wait()
    stores = []

    def fetch(k):
        packed = []
        for target in targets:
            at = target[k : k + 1, :]
            lane = jnp.broadcast_to(at & (LANES - 1), (chunks, devices))
            found = jnp.take_along_axis(tabs_ref[k], lane, axis=1)
            packed.append(jnp.sum(jnp.where(row_at == (at >> 7), found, 0), axis=0, keepdims=True))
        packed = jnp.concatenate(packed, axis=1)
        live = jnp.concatenate([mark[k : k + 1, :] for mark in marks], axis=1) > 0.0
        queries = jnp.concatenate(
            [
                got32_ref[pl.ds(row_of(k), devices, stride=rows), :],
                got32_ref[pl.ds(row_of(k) + 8, devices, stride=rows), :],
            ],
            axis=0,
        ).astype(BF16)
        q_ref[k] = queries
        stores.append(pltpu.make_async_copy(q_ref.at[k], q_hbm.at[k], q_sem.at[k]))
        stores[-1].start()
        scores = mm(items_ref[k * LANES : (k + 1) * LANES, :], queries, ((1,), (1,)))
        return live, packed, scores

    def soften(k, live, packed, scores):
        item = jnp.where(live, packed >> 12, -1)
        count = (packed & 4095).astype(F32)
        if k % 4 == 0:
            loads[2 + k // 4].wait()
        column = jnp.concatenate([mass_ref[k]] * (pairs // LANES), axis=1)
        masked = jnp.where(column > 0.0, scores, NONE)
        top = jnp.max(masked, axis=0, keepdims=True)
        expo = jnp.exp(masked - top) * column
        total = jnp.sum(expo, axis=0, keepdims=True)
        hit = item_at == item
        picked = jnp.sum(jnp.where(hit, scores, 0.0), axis=0, keepdims=True)
        losses_ref[k : k + 1, :] = jnp.log(total) + top - (picked - jnp.log(count))
        weight = (expo * (1.0 / total) - jnp.where(hit, 1.0, 0.0)).astype(BF16)
        weight_ref[k] = weight
        stores.append(pltpu.make_async_copy(weight_ref.at[k], weight_hbm.at[k], weight_sem.at[k]))
        stores[-1].start()
        return weight

    def give(k, weight):
        dq = mm(weight, items_ref[k * LANES : (k + 1) * LANES, :], ((0,), (0,)))
        dq32_ref[pl.ds(row_of(k), devices, stride=rows), :] = dq[0:devices, :]
        dq32_ref[pl.ds(row_of(k) + 8, devices, stride=rows), :] = dq[devices:pairs, :]
        if k % 8 == 7:
            at = row_of(k) - 7
            dq_ref[:, at : at + 16, :] = (
                dq32_ref[...].reshape(devices, rows, width)[:, at : at + 16, :].astype(BF16)
            )
            span = (slice(None), pl.ds(at, 16))
            stores.append(
                pltpu.make_async_copy(dq_ref.at[span], dq_hbm.at[span], dq_sem.at[k // 8])
            )
            stores[-1].start()

    fetched = [fetch(k) for k in range(AHEAD)]
    for k in range(local):
        if k + AHEAD < local:
            fetched.append(fetch(k + AHEAD))
        give(k, soften(k, *fetched[k]))
    live = jnp.concatenate(marks, axis=1) > 0.0
    total = jnp.sum(jnp.where(live, losses_ref[...], 0.0), axis=1, keepdims=True)
    loss_ref[...] = total / jnp.sum(jnp.where(live, 1.0, 0.0), axis=1, keepdims=True)
    for store in stores:
        store.wait()


def owner(got, items, mass, tabs):
    devices, rows, width = got.shape
    local = items.shape[0] // LANES
    outs = (
        jax.ShapeDtypeStruct((devices, 2 * local, width), BF16),
        jax.ShapeDtypeStruct((local, LANES, 2 * devices), BF16),
        jax.ShapeDtypeStruct((local, 2 * devices, width), BF16),
    )
    return pl.pallas_call(
        owner_body,
        out_shape=outs_hbm(outs) + (jax.ShapeDtypeStruct((local, 1), F32),),
        in_specs=vmem(1) + hbm(3),
        out_specs=hbm(3) + vmem(1),
        scratch_shapes=[
            pltpu.VMEM((devices * rows, width), F32),
            pltpu.VMEM((devices * rows, width), F32),
        ]
        + [pltpu.VMEM(a.shape, a.dtype) for a in outs + (items, mass, tabs)]
        + [
            pltpu.VMEM((local, 2 * devices), F32),
            pltpu.SemaphoreType.DMA((2 + local // 4,)),
            pltpu.SemaphoreType.DMA((local // 8,)),
            pltpu.SemaphoreType.DMA((local,)),
            pltpu.SemaphoreType.DMA((local,)),
        ],
        compiler_params=params(40),
        name="owner",
    )(got, *in_hbm((items, mass, tabs)))


def item_body(weight_ref, q_ref, grad_ref):
    for k in range(weight_ref.shape[0]):
        grad_ref[k * LANES : (k + 1) * LANES, :] = mm(weight_ref[k], q_ref[k])


def item_grads(weight, queries):
    local, pairs, width = queries.shape
    step = 4
    return pl.pallas_call(
        item_body,
        grid=(local // step,),
        out_shape=jax.ShapeDtypeStruct((local * LANES, width), F32),
        in_specs=[
            pl.BlockSpec((step, LANES, pairs), lambda k: (k, 0, 0)),
            pl.BlockSpec((step, pairs, width), lambda k: (k, 0, 0)),
        ],
        out_specs=pl.BlockSpec((step * LANES, width), lambda k: (k, 0)),
        compiler_params=params(8),
        cost_estimate=pl.CostEstimate(
            flops=135_000_000, bytes_accessed=3 << 20, transcendentals=0
        ),
        name="item_grads",
    )(*in_hbm((weight, queries)))


def ready_body(feat_ref, feat_other_ref, wh_ref, hidden_ref, slope_ref):
    half = hidden_ref.shape[1]
    core = lax.axis_index("dev") % 2
    weight = wh_ref[:, pl.ds(pl.multiple_of(core * half, half), half)]
    for i, ref in enumerate((feat_ref, feat_other_ref)):
        pre = mm(weight, ref[...], ((0,), (0,)))
        sig = jax.nn.sigmoid(pre)
        hidden_ref[i] = (pre * sig).astype(BF16)
        slope_ref[i] = (sig * (1.0 + pre * (1.0 - sig))).T


def ready(features_t, features_other_t, w_hidden):
    feats, users = features_t.shape
    hid = w_hidden.shape[1]
    half = hid // 2
    step = users // 2
    outs = (
        jax.ShapeDtypeStruct((2, half, users), BF16),
        jax.ShapeDtypeStruct((2, users, half), F32),
    )
    return pl.pallas_call(
        ready_body,
        grid=(users // step,),
        out_shape=outs_hbm(outs),
        in_specs=[pl.BlockSpec((feats, step), lambda i: (0, i))] * 2
        + [pl.BlockSpec((feats, hid), lambda i: (0, 0))],
        out_specs=[
            pl.BlockSpec((2, half, step), lambda i: (0, 0, i)),
            pl.BlockSpec((2, step, half), lambda i: (0, i, 0)),
        ],
        compiler_params=params(24),
        cost_estimate=pl.CostEstimate(
            flops=550_000_000, bytes_accessed=5 << 20, transcendentals=1 << 19
        ),
        name="ready",
    )(*in_hbm((features_t, features_other_t, w_hidden)))


def collect_body(back_ref, named_ref, dq_ref):
    devices, rows, width = back_ref.shape
    users = dq_ref.shape[0]
    block = LANES
    named = named_ref[...]
    lane_user = iota((block, users), 1).astype(F32)
    total = jnp.zeros((width, users), F32)
    group = 2 * block // rows
    for b in range(devices // group):
        parts = [
            jnp.where(lane_user == named[:, 2 * b + c : 2 * b + c + 1], 1.0, 0.0).reshape(
                block // 8, 8, users
            )
            for c in range(2)
        ]
        place = jnp.concatenate(parts, axis=1).reshape(2 * block, users).astype(BF16)
        back = back_ref[b * group : (b + 1) * group].reshape(2 * block, width)
        total = total + mm(back, place, ((0,), (0,)))
    dq_ref[...] = total.T.astype(BF16)


def collect(back, named, users):
    return pl.pallas_call(
        collect_body,
        out_shape=jax.ShapeDtypeStruct((users, back.shape[2]), BF16),
        in_specs=vmem(2),
        out_specs=vmem(1)[0],
        compiler_params=params(24),
        name="collect",
    )(back, named)


def tower_body(
    dq_ref,
    other_ref,
    hidden_hbm,
    slope_hbm,
    feat_hbm,
    feat_other_hbm,
    wo_hbm,
    grad_ref,
    hidden_ref,
    slope_ref,
    feat_ref,
    feat_other_ref,
    wo_ref,
    sem,
):
    users = dq_ref.shape[0]
    half = hidden_ref.shape[1]
    peers = grad_ref.shape[0]
    core = lax.axis_index("dev") % 2
    wo_at = wo_hbm.at[pl.ds(pl.multiple_of(core * half, half), half), :]
    loads = [
        pltpu.make_async_copy(src, dst, sem.at[i])
        for i, (src, dst) in enumerate(
            [
                (wo_at, wo_ref),
                (slope_hbm, slope_ref),
                (feat_hbm, feat_ref),
                (feat_other_hbm, feat_other_ref),
                (hidden_hbm, hidden_ref),
            ]
        )
    ]
    for load in loads:
        load.start()
    for load in loads[:2]:
        load.wait()
    w_out = wo_ref[...]
    dqs = (dq_ref[...], other_ref[...])
    dpres = [
        (mm(dq, w_out, ((1,), (1,))) * slope_ref[i]).astype(BF16) for i, dq in enumerate(dqs)
    ]
    loads[2].wait()
    big = mm(feat_ref[...], dpres[0])
    loads[3].wait()
    big = big + mm(feat_other_ref[...], dpres[1])
    loads[4].wait()
    small = mm(hidden_ref[0], dqs[0]) + mm(hidden_ref[1], dqs[1])
    tall = big.shape[0] // peers
    blocks = half // LANES
    for c in range(blocks):
        grad_ref[:, c * tall : (c + 1) * tall, :] = (
            big[:, c * LANES : (c + 1) * LANES].reshape(peers, tall, LANES).astype(BF16)
        )
    filled = half // 8
    at = blocks * tall
    grad_ref[0:filled, at : at + 8, :] = small.reshape(filled, 8, LANES).astype(BF16)
    grad_ref[filled:peers, at : at + 8, :] = jnp.zeros((peers - filled, 8, LANES), BF16)


def tower_back(dq, other, hidden, slope, features_t, features_other_t, w_out, peers):
    half = hidden.shape[1]
    rows = half * features_t.shape[0] // peers // LANES + 8
    held = (hidden, slope, features_t, features_other_t)
    return pl.pallas_call(
        tower_body,
        out_shape=jax.ShapeDtypeStruct((peers, rows, LANES), BF16),
        in_specs=vmem(2) + hbm(5),
        out_specs=vmem(1)[0],
        scratch_shapes=[pltpu.VMEM(a.shape, a.dtype) for a in held]
        + [pltpu.VMEM((half, w_out.shape[1]), BF16), pltpu.SemaphoreType.DMA((5,))],
        compiler_params=params(40),
        name="tower_back",
    )(dq, other, *in_hbm(held + (w_out,)))


def sum_body(parts_ref, out_ref):
    total = jnp.sum(parts_ref[...].astype(F32), axis=0, keepdims=True)
    out_ref[...] = jnp.broadcast_to(total, out_ref.shape).astype(BF16)


def sum_parts(parts):
    return pl.pallas_call(
        sum_body,
        out_shape=jax.ShapeDtypeStruct(parts.shape, BF16),
        in_specs=vmem(1),
        out_specs=vmem(1)[0],
        compiler_params=params(24),
        name="sum_parts",
    )(parts)


def spread_body(side_of, got_ref, *refs):
    hidden_hbm, out_hbm, hidden_ref, out_ref, sem = refs[-5:]
    peers = got_ref.shape[0]
    side = lax.axis_index("dev") % 2
    side = side_of(side)
    half = out_ref.shape[0]
    tall = hidden_ref.shape[0] // peers
    blocks = half // LANES
    filled = half // 8
    stores = []
    for c in range(blocks):
        hidden_ref[:, c * LANES : (c + 1) * LANES] = (
            got_ref[:, c * tall : (c + 1) * tall, :].astype(F32).reshape(-1, LANES)
        )
        at = pl.multiple_of(side * half + c * LANES, LANES)
        stores.append(
            pltpu.make_async_copy(
                hidden_ref.at[:, pl.ds(c * LANES, LANES)],
                hidden_hbm.at[:, pl.ds(at, LANES)],
                sem.at[c],
            )
        )
        stores[-1].start()
    at = blocks * tall
    out_ref[...] = got_ref[0:filled, at : at + 8, :].astype(F32).reshape(half, LANES)
    stores.append(
        pltpu.make_async_copy(
            out_ref, out_hbm.at[pl.ds(pl.multiple_of(side * half, half), half), :], sem.at[blocks]
        )
    )
    stores[-1].start()
    for store in stores:
        store.wait()


def spread(got, side_of, hidden_shape, out_shape, begun=()):
    half = out_shape[0] // 2
    outs = (
        jax.ShapeDtypeStruct(hidden_shape, F32),
        jax.ShapeDtypeStruct(out_shape, F32),
    )
    return pl.pallas_call(
        functools.partial(spread_body, side_of),
        out_shape=outs_hbm(outs),
        in_specs=vmem(1) + hbm(len(begun)),
        out_specs=hbm(2),
        scratch_shapes=[
            pltpu.VMEM((hidden_shape[0], half), F32),
            pltpu.VMEM((half, LANES), F32),
            pltpu.SemaphoreType.DMA((half // LANES + 1,)),
        ],
        input_output_aliases={1 + i: i for i in range(len(begun))},
        compiler_params=params(16),
        cost_estimate=pl.CostEstimate(flops=300_000, bytes_accessed=2 << 20, transcendentals=0),
        name="spread",
    )(got, *in_hbm(begun))


def exchange(x):
    return lax.all_to_all(x, "dev", split_axis=0, concat_axis=0, tiled=True)


def exchange_peers(x):
    devices = lax.axis_size("dev")
    groups = [list(range(c, devices, 2)) for c in range(2)]
    return lax.all_to_all(
        x, "dev", split_axis=0, concat_axis=0, axis_index_groups=groups, tiled=True
    )


def swap(x):
    devices = lax.axis_size("dev")
    return lax.ppermute(x, "dev", [(d, d ^ 1) for d in range(devices)])


def local(
    features, w_hidden, w_out, items, routes, cluster_slot, sample_ids, sample_counts, positives
):
    devices = lax.axis_size("dev")
    features_t = features.T
    features_other_t = swap(features_t)
    send, named = route(routes, positives, cluster_slot, features, w_hidden, w_out, devices)
    mass, tabs = tables(sample_ids, sample_counts)
    got = exchange(send)
    got, mass, tabs, features_other_t = lax.optimization_barrier(
        (got, *in_hbm((mass, tabs)), features_other_t)
    )
    dq_slots, weight, queries, losses = owner(got, items, mass, tabs)
    back = exchange(dq_slots)
    hidden, slope = ready(features_t, features_other_t, w_hidden)
    item_grad = item_grads(weight, queries)
    back, hidden, slope, item_grad = lax.optimization_barrier((back, hidden, slope, item_grad))
    dq = collect(back, named, features.shape[0])
    partial = tower_back(
        dq, swap(dq), hidden, slope, features_t, features_other_t, w_out, devices // 2
    )
    summed = exchange_peers(sum_parts(exchange_peers(partial)))
    begun = spread(summed, lambda core: core, w_hidden.shape, w_out.shape)
    grad_hidden, grad_out = spread(
        swap(summed), lambda core: 1 - core, w_hidden.shape, w_out.shape, begun
    )
    slot_loss = losses[:, 0]
    return (slot_loss, grad_hidden, grad_out, item_grad)


def solution(mesh):
    in_specs = (
        P("dev", None),
        P(),
        P(),
        P("dev", None),
        P("dev", None),
        P(),
        P("dev", None),
        P("dev", None),
        P("dev", None),
    )
    out_specs = (P("dev"), P(), P(), P("dev", None))
    return jax.shard_map(local, mesh=mesh, in_specs=in_specs, out_specs=out_specs, check_vma=False)
```

```python
import functools

import jax
import jax.numpy as jnp
from jax import lax
from jax.experimental import pallas as pl
from jax.experimental.pallas import tpu as pltpu
from jax.sharding import PartitionSpec as P

F32 = jnp.float32
BF16 = jnp.bfloat16
NONE = -3.0e38
KEY = 4096
AHEAD = 1
LANES = 128


def vmem(count):
    return [pl.BlockSpec(memory_space=pltpu.VMEM)] * count


def in_hbm(arrays):
    return tuple(pltpu.with_memory_space_constraint(a, pltpu.HBM) for a in arrays)


def outs_hbm(arrays):
    return tuple(pltpu.HBM(a.shape, a.dtype) for a in arrays)


def hbm(count):
    return [pl.BlockSpec(memory_space=pltpu.HBM)] * count


def params(megabytes):
    return pltpu.CompilerParams(vmem_limit_bytes=megabytes << 20)


def iota(shape, axis):
    return lax.broadcasted_iota(jnp.int32, shape, axis)


def one_hot(mask):
    return jnp.where(mask, 1.0, 0.0).astype(BF16)


def mm(a, b, dims=((1,), (0,))):
    return lax.dot_general(a, b, (dims, ((), ())), preferred_element_type=F32)


def route_body(
    routes_hbm,
    pos_hbm,
    cslot_hbm,
    feat_hbm,
    wh_hbm,
    wo_hbm,
    send_hbm,
    named_hbm,
    routes_ref,
    pos_ref,
    cslot_ref,
    feat_ref,
    wh_ref,
    wo_ref,
    send_ref,
    named_ref,
    place_ref,
    in_sem,
    out_sem,
    send_sem,
):
    loads = [
        pltpu.make_async_copy(src, dst, in_sem.at[i])
        for i, (src, dst) in enumerate(
            [
                (routes_hbm, routes_ref),
                (pos_hbm, pos_ref),
                (cslot_hbm, cslot_ref),
                (feat_hbm, feat_ref),
                (wh_hbm, wh_ref),
                (wo_hbm, wo_ref),
            ]
        )
    ]
    for load in loads:
        load.start()
    visits, users = routes_ref.shape
    clusters = cslot_ref.shape[0] * LANES
    devices, rows, width = send_ref.shape
    local = clusters // devices
    for load in loads[:3]:
        load.wait()
    cslot = cslot_ref[...]
    row_at = iota((cslot.shape[0], LANES), 0)
    user_at = iota((1, users), 1)
    slots = []
    keys = []
    for r in range(visits):
        found = []
        for part in range(users // LANES):
            cluster = routes_ref[r : r + 1, part * LANES : (part + 1) * LANES]
            lane = jnp.broadcast_to(cluster & (LANES - 1), cslot.shape)
            row = jnp.take_along_axis(cslot, lane, axis=1)
            found.append(
                jnp.sum(jnp.where(row_at == (cluster >> 7), row, 0), axis=0, keepdims=True)
            )
        slots.append(jnp.concatenate(found, axis=1).astype(F32))
        keys.append((user_at * KEY + pos_ref[r : r + 1, :] + 1).astype(F32))
    block = LANES
    groups = block // local
    sub = iota((block, users), 0).astype(F32)
    stores = []
    named_lane = iota((block, LANES), 1)
    named = [jnp.zeros((block, LANES), F32)]

    def assign(b):
        slot_at = sub + float(b * block)
        key = jnp.zeros((block, users), F32)
        for r in range(visits):
            key = jnp.where(slot_at == slots[r], keys[r], key)
        most = jnp.max(key, axis=1, keepdims=True)
        rest = jnp.sum(key, axis=1, keepdims=True) - most
        parts = []
        for c, chosen in enumerate((most, rest)):
            named[0] = jnp.where(named_lane == 2 * b + c, chosen, named[0])
            chosen = jnp.where(chosen > 0.0, chosen, -1.0)
            parts.append(jnp.where(key == chosen, 1.0, 0.0).reshape(block // 8, 8, users))
        place = jnp.concatenate(parts, axis=1).reshape(2 * block, users).astype(BF16)
        place_ref[b * 2 * block : (b + 1) * 2 * block, :] = place

    def name_users():
        user = jnp.floor((named[0] - 1.0) * (1.0 / KEY))
        named_ref[...] = user
        stores.append(pltpu.make_async_copy(named_ref, named_hbm, out_sem.at[0]))
        stores[-1].start()
        chosen = named[0].T
        user = jnp.floor((chosen - 1.0) * (1.0 / KEY))
        mark = jnp.where(chosen > 0.0, chosen - user * KEY, 0.0)
        top = jnp.floor(mark * (1.0 / 64.0))
        low = mark - top * 64.0
        for b in range(clusters // block):
            tail = jnp.concatenate([top[2 * b : 2 * b + 2], low[2 * b : 2 * b + 2]], axis=0)
            tail = jnp.concatenate([tail, tail], axis=0)
            send_ref[b * groups : (b + 1) * groups, 2 * local : rows, :] = jnp.broadcast_to(
                tail[None], (groups, rows - 2 * local, width)
            ).astype(BF16)
        span = (slice(None), pl.ds(2 * local, rows - 2 * local))
        stores.append(pltpu.make_async_copy(send_ref.at[span], send_hbm.at[span], out_sem.at[1]))
        stores[-1].start()

    early = 4
    for b in range(early):
        assign(b)
    for load in loads[3:]:
        load.wait()
    pre = mm(feat_ref[...], wh_ref[...])
    hidden = (pre * jax.nn.sigmoid(pre)).astype(BF16)
    query = mm(hidden, wo_ref[...]).astype(BF16)
    blocks = clusters // block
    for b in range(blocks):
        if b + early < blocks:
            assign(b + early)
        if b + early == blocks:
            name_users()
        sent = mm(place_ref[b * 2 * block : (b + 1) * 2 * block, :], query).astype(BF16)
        send_ref[b * groups : (b + 1) * groups, 0 : 2 * local, :] = sent.reshape(
            groups, 2 * local, width
        )
        if b % 4 == 3:
            span = (pl.ds((b - 3) * groups, 4 * groups), pl.ds(0, 2 * local))
            stores.append(
                pltpu.make_async_copy(send_ref.at[span], send_hbm.at[span], send_sem.at[b // 4])
            )
            stores[-1].start()
    for store in stores:
        store.wait()


def route(routes, positives, cluster_slot, features, w_hidden, w_out, devices):
    users, visits = routes.shape
    clusters = cluster_slot.shape[0]
    width = w_out.shape[1]
    rows = 2 * clusters // devices + 8
    args = (
        routes.T,
        positives.T,
        cluster_slot.reshape(clusters // LANES, LANES),
        features,
        w_hidden,
        w_out,
    )
    outs = (
        jax.ShapeDtypeStruct((devices, rows, width), BF16),
        jax.ShapeDtypeStruct((LANES, LANES), F32),
    )
    return pl.pallas_call(
        route_body,
        out_shape=outs_hbm(outs),
        in_specs=hbm(6),
        out_specs=hbm(2),
        scratch_shapes=[pltpu.VMEM(a.shape, a.dtype) for a in args + outs]
        + [
            pltpu.VMEM((2 * clusters, users), BF16),
            pltpu.SemaphoreType.DMA((6,)),
            pltpu.SemaphoreType.DMA((2,)),
            pltpu.SemaphoreType.DMA((4,)),
        ],
        compiler_params=params(48),
        name="route",
    )(*in_hbm(args))


def table_body(ids_ref, counts_ref, mass_hbm, tabs_hbm, inv_ref, mass_ref, tabs_ref, sem):
    clusters, chunks, lanes = tabs_ref.shape
    inv_ref[...] = 1.0 / counts_ref[...].astype(F32)
    tabs_ref[...] = ((ids_ref[...] << 12) | counts_ref[...]).reshape(tabs_ref.shape)
    store = pltpu.make_async_copy(tabs_ref, tabs_hbm, sem.at[0])
    store.start()
    item_at = iota((LANES, LANES), 0)

    def cluster(k, carry):
        acc = jnp.zeros((LANES, LANES), F32)
        for h in range(chunks):
            at = k * chunks + h
            hit = item_at == ids_ref[pl.ds(at, 1), :]
            acc = acc + jnp.where(hit, inv_ref[pl.ds(at, 1), :], 0.0)
        mass_ref[k] = jnp.broadcast_to(jnp.sum(acc, axis=1, keepdims=True), acc.shape)
        return carry

    lax.fori_loop(0, clusters, cluster, 0)
    last = pltpu.make_async_copy(mass_ref, mass_hbm, sem.at[1])
    last.start()
    last.wait()
    store.wait()


def tables(sample_ids, sample_counts):
    clusters, samples = sample_ids.shape
    total = sample_ids.size // LANES
    outs = (
        jax.ShapeDtypeStruct((clusters, LANES, LANES), F32),
        jax.ShapeDtypeStruct((clusters, samples // LANES, LANES), jnp.int32),
    )
    return pl.pallas_call(
        table_body,
        out_shape=outs_hbm(outs),
        in_specs=vmem(2),
        out_specs=hbm(2),
        scratch_shapes=[pltpu.VMEM((total, LANES), F32)]
        + [pltpu.VMEM(a.shape, a.dtype) for a in outs]
        + [pltpu.SemaphoreType.DMA((2,))],
        compiler_params=params(16),
        cost_estimate=pl.CostEstimate(flops=30_000_000, bytes_accessed=1 << 20, transcendentals=0),
        name="tables",
    )(sample_ids.reshape(total, LANES), sample_counts.reshape(total, LANES))


def row_of(slot):
    return slot // 8 * 16 + slot % 8


def owner_body(
    got_ref,
    items_hbm,
    mass_hbm,
    tabs_hbm,
    dq_hbm,
    weight_hbm,
    q_hbm,
    loss_ref,
    got32_ref,
    dq32_ref,
    dq_ref,
    weight_ref,
    q_ref,
    items_ref,
    mass_ref,
    tabs_ref,
    losses_ref,
    load_sem,
    dq_sem,
    weight_sem,
    q_sem,
):
    loads = [
        pltpu.make_async_copy(tabs_hbm, tabs_ref, load_sem.at[0]),
        pltpu.make_async_copy(items_hbm, items_ref, load_sem.at[1]),
    ]
    for part in range(mass_ref.shape[0] // 4):
        span = pl.ds(part * 4, 4)
        loads.append(
            pltpu.make_async_copy(mass_hbm.at[span], mass_ref.at[span], load_sem.at[2 + part])
        )
    for load in loads:
        load.start()
    devices, rows, width = got_ref.shape
    local = q_ref.shape[0]
    chunks = tabs_ref.shape[1]
    pairs = 2 * devices
    got32_ref[...] = got_ref[...].astype(F32).reshape(devices * rows, width)
    place_at = lax.axis_index("dev") % (LANES // local) * local
    tail_lane = iota((devices, LANES), 1)
    tail = jnp.zeros((devices, LANES), F32)
    for c in range(2):
        top = got32_ref[pl.ds(2 * local + c, devices, stride=rows), :]
        low = got32_ref[pl.ds(2 * local + 2 + c, devices, stride=rows), :]
        moved = pltpu.roll(top * 64.0 + low, (LANES + c * local - place_at) % LANES, 1)
        tail = jnp.where(tail_lane // local == c, moved, tail)
    tail = tail.T
    marks = [tail[c * local : (c + 1) * local, :] for c in range(2)]
    targets = [jnp.maximum(mark - 1.0, 0.0).astype(jnp.int32) for mark in marks]
    item_at = iota((LANES, pairs), 0)
    row_at = iota((chunks, devices), 0)
    for load in loads[0:2]:
        load.wait()
    stores = []

    def fetch(k):
        packed = []
        for target in targets:
            at = target[k : k + 1, :]
            lane = jnp.broadcast_to(at & (LANES - 1), (chunks, devices))
            found = jnp.take_along_axis(tabs_ref[k], lane, axis=1)
            packed.append(jnp.sum(jnp.where(row_at == (at >> 7), found, 0), axis=0, keepdims=True))
        packed = jnp.concatenate(packed, axis=1)
        live = jnp.concatenate([mark[k : k + 1, :] for mark in marks], axis=1) > 0.0
        queries = jnp.concatenate(
            [
                got32_ref[pl.ds(row_of(k), devices, stride=rows), :],
                got32_ref[pl.ds(row_of(k) + 8, devices, stride=rows), :],
            ],
            axis=0,
        ).astype(BF16)
        q_ref[k] = queries
        stores.append(pltpu.make_async_copy(q_ref.at[k], q_hbm.at[k], q_sem.at[k]))
        stores[-1].start()
        scores = mm(items_ref[k * LANES : (k + 1) * LANES, :], queries, ((1,), (1,)))
        return live, packed, scores

    def soften(k, live, packed, scores):
        item = jnp.where(live, packed >> 12, -1)
        count = (packed & 4095).astype(F32)
        if k % 4 == 0:
            loads[2 + k // 4].wait()
        column = jnp.concatenate([mass_ref[k]] * (pairs // LANES), axis=1)
        masked = jnp.where(column > 0.0, scores, NONE)
        top = jnp.max(masked, axis=0, keepdims=True)
        expo = jnp.exp(masked - top) * column
        total = jnp.sum(expo, axis=0, keepdims=True)
        hit = item_at == item
        picked = jnp.sum(jnp.where(hit, scores, 0.0), axis=0, keepdims=True)
        losses_ref[k : k + 1, :] = jnp.log(total) + top - (picked - jnp.log(count))
        weight = (expo * (1.0 / total) - jnp.where(hit, 1.0, 0.0)).astype(BF16)
        weight_ref[k] = weight
        stores.append(pltpu.make_async_copy(weight_ref.at[k], weight_hbm.at[k], weight_sem.at[k]))
        stores[-1].start()
        return weight

    def give(k, weight):
        dq = mm(weight, items_ref[k * LANES : (k + 1) * LANES, :], ((0,), (0,)))
        dq32_ref[pl.ds(row_of(k), devices, stride=rows), :] = dq[0:devices, :]
        dq32_ref[pl.ds(row_of(k) + 8, devices, stride=rows), :] = dq[devices:pairs, :]
        if k % 8 == 7:
            at = row_of(k) - 7
            dq_ref[:, at : at + 16, :] = (
                dq32_ref[...].reshape(devices, rows, width)[:, at : at + 16, :].astype(BF16)
            )
            span = (slice(None), pl.ds(at, 16))
            stores.append(
                pltpu.make_async_copy(dq_ref.at[span], dq_hbm.at[span], dq_sem.at[k // 8])
            )
            stores[-1].start()

    fetched = [fetch(k) for k in range(AHEAD)]
    for k in range(local):
        if k + AHEAD < local:
            fetched.append(fetch(k + AHEAD))
        give(k, soften(k, *fetched[k]))
    live = jnp.concatenate(marks, axis=1) > 0.0
    total = jnp.sum(jnp.where(live, losses_ref[...], 0.0), axis=1, keepdims=True)
    loss_ref[...] = total / jnp.sum(jnp.where(live, 1.0, 0.0), axis=1, keepdims=True)
    for store in stores:
        store.wait()


def owner(got, items, mass, tabs):
    devices, rows, width = got.shape
    local = items.shape[0] // LANES
    outs = (
        jax.ShapeDtypeStruct((devices, 2 * local, width), BF16),
        jax.ShapeDtypeStruct((local, LANES, 2 * devices), BF16),
        jax.ShapeDtypeStruct((local, 2 * devices, width), BF16),
    )
    return pl.pallas_call(
        owner_body,
        out_shape=outs_hbm(outs) + (jax.ShapeDtypeStruct((local, 1), F32),),
        in_specs=vmem(1) + hbm(3),
        out_specs=hbm(3) + vmem(1),
        scratch_shapes=[
            pltpu.VMEM((devices * rows, width), F32),
            pltpu.VMEM((devices * rows, width), F32),
        ]
        + [pltpu.VMEM(a.shape, a.dtype) for a in outs + (items, mass, tabs)]
        + [
            pltpu.VMEM((local, 2 * devices), F32),
            pltpu.SemaphoreType.DMA((2 + local // 4,)),
            pltpu.SemaphoreType.DMA((local // 8,)),
            pltpu.SemaphoreType.DMA((local,)),
            pltpu.SemaphoreType.DMA((local,)),
        ],
        compiler_params=params(40),
        name="owner",
    )(got, *in_hbm((items, mass, tabs)))


def item_body(weight_ref, q_ref, grad_ref):
    for k in range(weight_ref.shape[0]):
        grad_ref[k * LANES : (k + 1) * LANES, :] = mm(weight_ref[k], q_ref[k])


def item_grads(weight, queries):
    local, pairs, width = queries.shape
    step = 4
    return pl.pallas_call(
        item_body,
        grid=(local // step,),
        out_shape=jax.ShapeDtypeStruct((local * LANES, width), F32),
        in_specs=[
            pl.BlockSpec((step, LANES, pairs), lambda k: (k, 0, 0)),
            pl.BlockSpec((step, pairs, width), lambda k: (k, 0, 0)),
        ],
        out_specs=pl.BlockSpec((step * LANES, width), lambda k: (k, 0)),
        compiler_params=params(8),
        cost_estimate=pl.CostEstimate(
            flops=135_000_000, bytes_accessed=3 << 20, transcendentals=0
        ),
        name="item_grads",
    )(*in_hbm((weight, queries)))


def ready_body(feat_ref, feat_other_ref, wh_ref, *outs):
    half = outs[0].shape[0]
    core = lax.axis_index("dev") % 2
    weight = wh_ref[:, pl.ds(pl.multiple_of(core * half, half), half)]
    for i, ref in enumerate((feat_ref, feat_other_ref)):
        hidden_ref, slope_ref = outs[2 * i : 2 * i + 2]
        pre = mm(weight, ref[...], ((0,), (0,)))
        sig = jax.nn.sigmoid(pre)
        hidden_ref[...] = (pre * sig).astype(BF16)
        slope_ref[...] = (sig * (1.0 + pre * (1.0 - sig))).T


def ready(features_t, features_other_t, w_hidden):
    feats, users = features_t.shape
    hid = w_hidden.shape[1]
    half = hid // 2
    step = users // 2
    outs = (
        jax.ShapeDtypeStruct((half, users), BF16),
        jax.ShapeDtypeStruct((users, half), F32),
    ) * 2
    return pl.pallas_call(
        ready_body,
        grid=(users // step,),
        out_shape=outs_hbm(outs),
        in_specs=[pl.BlockSpec((feats, step), lambda i: (0, i))] * 2
        + [pl.BlockSpec((feats, hid), lambda i: (0, 0))],
        out_specs=[
            pl.BlockSpec((half, step), lambda i: (0, i)),
            pl.BlockSpec((step, half), lambda i: (i, 0)),
        ]
        * 2,
        compiler_params=params(24),
        cost_estimate=pl.CostEstimate(
            flops=550_000_000, bytes_accessed=5 << 20, transcendentals=1 << 19
        ),
        name="ready",
    )(*in_hbm((features_t, features_other_t, w_hidden)))


def collect_body(back_ref, named_ref, dq_ref):
    devices, rows, width = back_ref.shape
    users = dq_ref.shape[0]
    block = LANES
    named = named_ref[...]
    lane_user = iota((block, users), 1).astype(F32)
    total = jnp.zeros((width, users), F32)
    group = 2 * block // rows
    for b in range(devices // group):
        parts = [
            jnp.where(lane_user == named[:, 2 * b + c : 2 * b + c + 1], 1.0, 0.0).reshape(
                block // 8, 8, users
            )
            for c in range(2)
        ]
        place = jnp.concatenate(parts, axis=1).reshape(2 * block, users).astype(BF16)
        back = back_ref[b * group : (b + 1) * group].reshape(2 * block, width)
        total = total + mm(back, place, ((0,), (0,)))
    dq_ref[...] = total.T.astype(BF16)


def collect(back, named, users):
    return pl.pallas_call(
        collect_body,
        out_shape=jax.ShapeDtypeStruct((users, back.shape[2]), BF16),
        in_specs=vmem(2),
        out_specs=vmem(1)[0],
        compiler_params=params(24),
        name="collect",
    )(back, named)


def own_body(
    dq_ref,
    hidden_hbm,
    slope_hbm,
    feat_hbm,
    wo_hbm,
    big_ref,
    small_ref,
    hidden_ref,
    slope_ref,
    feat_ref,
    wo_ref,
    sem,
):
    half = hidden_ref.shape[0]
    core = lax.axis_index("dev") % 2
    wo_at = wo_hbm.at[pl.ds(pl.multiple_of(core * half, half), half), :]
    loads = [
        pltpu.make_async_copy(src, dst, sem.at[i])
        for i, (src, dst) in enumerate(
            [
                (wo_at, wo_ref),
                (slope_hbm, slope_ref),
                (feat_hbm, feat_ref),
                (hidden_hbm, hidden_ref),
            ]
        )
    ]
    for load in loads:
        load.start()
    for load in loads[:2]:
        load.wait()
    dq = dq_ref[...]
    dpre = (mm(dq, wo_ref[...], ((1,), (1,))) * slope_ref[...]).astype(BF16)
    loads[2].wait()
    big_ref[...] = mm(feat_ref[...], dpre)
    loads[3].wait()
    small_ref[...] = mm(hidden_ref[...], dq)


def tower_own(dq, hidden, slope, features_t, w_out):
    half = hidden.shape[0]
    held = (hidden, slope, features_t)
    return pl.pallas_call(
        own_body,
        out_shape=(
            jax.ShapeDtypeStruct((features_t.shape[0], half), F32),
            jax.ShapeDtypeStruct((half, dq.shape[1]), F32),
        ),
        in_specs=vmem(1) + hbm(4),
        out_specs=vmem(2),
        scratch_shapes=[pltpu.VMEM(a.shape, a.dtype) for a in held]
        + [pltpu.VMEM((half, w_out.shape[1]), BF16), pltpu.SemaphoreType.DMA((4,))],
        compiler_params=params(16),
        cost_estimate=pl.CostEstimate(
            flops=340_000_000, bytes_accessed=3 << 20, transcendentals=0
        ),
        name="tower_own",
    )(dq, *in_hbm(held + (w_out,)))


def other_body(
    dq_ref, big_ref, small_ref, hidden_ref, slope_ref, feat_ref, wo_ref, grad_ref
):
    half = hidden_ref.shape[0]
    peers = grad_ref.shape[0]
    core = lax.axis_index("dev") % 2
    w_out = wo_ref[pl.ds(pl.multiple_of(core * half, half), half), :]
    dq = dq_ref[...]
    dpre = (mm(dq, w_out, ((1,), (1,))) * slope_ref[...]).astype(BF16)
    big = big_ref[...] + mm(feat_ref[...], dpre)
    small = small_ref[...] + mm(hidden_ref[...], dq)
    tall = big.shape[0] // peers
    blocks = half // LANES
    for c in range(blocks):
        grad_ref[:, c * tall : (c + 1) * tall, :] = (
            big[:, c * LANES : (c + 1) * LANES].reshape(peers, tall, LANES).astype(BF16)
        )
    filled = half // 8
    at = blocks * tall
    grad_ref[0:filled, at : at + 8, :] = small.reshape(filled, 8, LANES).astype(BF16)
    grad_ref[filled:peers, at : at + 8, :] = jnp.zeros((peers - filled, 8, LANES), BF16)


def tower_other(dq, big, small, hidden, slope, features_t, w_out, peers):
    half = hidden.shape[0]
    rows = half * features_t.shape[0] // peers // LANES + 8
    return pl.pallas_call(
        other_body,
        out_shape=jax.ShapeDtypeStruct((peers, rows, LANES), BF16),
        in_specs=vmem(7),
        out_specs=vmem(1)[0],
        compiler_params=params(16),
        name="tower_other",
    )(dq, big, small, hidden, slope, features_t, w_out)


def sum_body(parts_ref, out_ref):
    total = jnp.sum(parts_ref[...].astype(F32), axis=0, keepdims=True)
    out_ref[...] = jnp.broadcast_to(total, out_ref.shape).astype(BF16)


def sum_parts(parts):
    return pl.pallas_call(
        sum_body,
        out_shape=jax.ShapeDtypeStruct(parts.shape, BF16),
        in_specs=vmem(1),
        out_specs=vmem(1)[0],
        compiler_params=params(24),
        name="sum_parts",
    )(parts)


def spread_body(side_of, got_ref, *refs):
    hidden_hbm, out_hbm, hidden_ref, out_ref, sem = refs[-5:]
    peers = got_ref.shape[0]
    side = lax.axis_index("dev") % 2
    side = side_of(side)
    half = out_ref.shape[0]
    tall = hidden_ref.shape[0] // peers
    blocks = half // LANES
    filled = half // 8
    stores = []
    for c in range(blocks):
        hidden_ref[:, c * LANES : (c + 1) * LANES] = (
            got_ref[:, c * tall : (c + 1) * tall, :].astype(F32).reshape(-1, LANES)
        )
        at = pl.multiple_of(side * half + c * LANES, LANES)
        stores.append(
            pltpu.make_async_copy(
                hidden_ref.at[:, pl.ds(c * LANES, LANES)],
                hidden_hbm.at[:, pl.ds(at, LANES)],
                sem.at[c],
            )
        )
        stores[-1].start()
    at = blocks * tall
    out_ref[...] = got_ref[0:filled, at : at + 8, :].astype(F32).reshape(half, LANES)
    stores.append(
        pltpu.make_async_copy(
            out_ref, out_hbm.at[pl.ds(pl.multiple_of(side * half, half), half), :], sem.at[blocks]
        )
    )
    stores[-1].start()
    for store in stores:
        store.wait()


def spread(got, side_of, hidden_shape, out_shape, begun=()):
    half = out_shape[0] // 2
    outs = (
        jax.ShapeDtypeStruct(hidden_shape, F32),
        jax.ShapeDtypeStruct(out_shape, F32),
    )
    return pl.pallas_call(
        functools.partial(spread_body, side_of),
        out_shape=outs_hbm(outs),
        in_specs=vmem(1) + hbm(len(begun)),
        out_specs=hbm(2),
        scratch_shapes=[
            pltpu.VMEM((hidden_shape[0], half), F32),
            pltpu.VMEM((half, LANES), F32),
            pltpu.SemaphoreType.DMA((half // LANES + 1,)),
        ],
        input_output_aliases={1 + i: i for i in range(len(begun))},
        compiler_params=params(16),
        cost_estimate=pl.CostEstimate(flops=300_000, bytes_accessed=2 << 20, transcendentals=0),
        name="spread",
    )(got, *in_hbm(begun))


def exchange(x):
    return lax.all_to_all(x, "dev", split_axis=0, concat_axis=0, tiled=True)


def exchange_peers(x):
    devices = lax.axis_size("dev")
    groups = [list(range(c, devices, 2)) for c in range(2)]
    return lax.all_to_all(
        x, "dev", split_axis=0, concat_axis=0, axis_index_groups=groups, tiled=True
    )


def swap(x):
    devices = lax.axis_size("dev")
    return lax.ppermute(x, "dev", [(d, d ^ 1) for d in range(devices)])


def local(
    features, w_hidden, w_out, items, routes, cluster_slot, sample_ids, sample_counts, positives
):
    devices = lax.axis_size("dev")
    features_t = features.T
    features_other_t = swap(features_t)
    send, named = route(routes, positives, cluster_slot, features, w_hidden, w_out, devices)
    mass, tabs = tables(sample_ids, sample_counts)
    got = exchange(send)
    got, mass, tabs, features_other_t = lax.optimization_barrier(
        (got, *in_hbm((mass, tabs)), features_other_t)
    )
    dq_slots, weight, queries, losses = owner(got, items, mass, tabs)
    back = exchange(dq_slots)
    prepared = ready(features_t, features_other_t, w_hidden)
    item_grad = item_grads(weight, queries)
    back, prepared, item_grad = lax.optimization_barrier((back, prepared, item_grad))
    dq = collect(back, named, features.shape[0])
    dq_other = swap(dq)
    big, small = tower_own(dq, *prepared[0:2], features_t, w_out)
    partial = tower_other(
        dq_other, big, small, *prepared[2:4], features_other_t, w_out, devices // 2
    )
    summed = exchange_peers(sum_parts(exchange_peers(partial)))
    begun = spread(summed, lambda core: core, w_hidden.shape, w_out.shape)
    grad_hidden, grad_out = spread(
        swap(summed), lambda core: 1 - core, w_hidden.shape, w_out.shape, begun
    )
    slot_loss = losses[:, 0]
    return (slot_loss, grad_hidden, grad_out, item_grad)


def solution(mesh):
    in_specs = (
        P("dev", None),
        P(),
        P(),
        P("dev", None),
        P("dev", None),
        P(),
        P("dev", None),
        P("dev", None),
        P("dev", None),
    )
    out_specs = (P("dev"), P(), P(), P("dev", None))
    return jax.shard_map(local, mesh=mesh, in_specs=in_specs, out_specs=out_specs, check_vma=False)
```

```python
import functools

import jax
import jax.numpy as jnp
from jax import lax
from jax.experimental import pallas as pl
from jax.experimental.pallas import tpu as pltpu
from jax.sharding import PartitionSpec as P

F32 = jnp.float32
BF16 = jnp.bfloat16
NONE = -3.0e38
KEY = 4096
AHEAD = 3
LANES = 128


def vmem(count):
    return [pl.BlockSpec(memory_space=pltpu.VMEM)] * count


def in_hbm(arrays):
    return tuple(pltpu.with_memory_space_constraint(a, pltpu.HBM) for a in arrays)


def outs_hbm(arrays):
    return tuple(pltpu.HBM(a.shape, a.dtype) for a in arrays)


def outs_vmem(arrays):
    return tuple(pltpu.VMEM(a.shape, a.dtype) for a in arrays)


def hbm(count):
    return [pl.BlockSpec(memory_space=pltpu.HBM)] * count


def params(megabytes):
    return pltpu.CompilerParams(vmem_limit_bytes=megabytes << 20)


def iota(shape, axis):
    return lax.broadcasted_iota(jnp.int32, shape, axis)


def one_hot(mask):
    return jnp.where(mask, 1.0, 0.0).astype(BF16)


def mm(a, b, dims=((1,), (0,))):
    return lax.dot_general(a, b, (dims, ((), ())), preferred_element_type=F32)


def route_body(
    routes_hbm,
    pos_hbm,
    cslot_hbm,
    feat_hbm,
    wh_hbm,
    wo_hbm,
    send_hbm,
    named_hbm,
    routes_ref,
    pos_ref,
    cslot_ref,
    feat_ref,
    wh_ref,
    wo_ref,
    send_ref,
    named_ref,
    place_ref,
    in_sem,
    out_sem,
    send_sem,
):
    loads = [
        pltpu.make_async_copy(src, dst, in_sem.at[i])
        for i, (src, dst) in enumerate(
            [
                (routes_hbm, routes_ref),
                (pos_hbm, pos_ref),
                (cslot_hbm, cslot_ref),
                (feat_hbm, feat_ref),
                (wh_hbm, wh_ref),
                (wo_hbm, wo_ref),
            ]
        )
    ]
    for load in loads:
        load.start()
    visits, users = routes_ref.shape
    clusters = cslot_ref.shape[0] * LANES
    devices, rows, width = send_ref.shape
    local = clusters // devices
    for load in loads[:3]:
        load.wait()
    cslot = cslot_ref[...]
    row_at = iota((cslot.shape[0], LANES), 0)
    user_at = iota((1, users), 1)
    slots = []
    keys = []
    for r in range(visits):
        found = []
        for part in range(users // LANES):
            cluster = routes_ref[r : r + 1, part * LANES : (part + 1) * LANES]
            lane = jnp.broadcast_to(cluster & (LANES - 1), cslot.shape)
            row = jnp.take_along_axis(cslot, lane, axis=1)
            found.append(
                jnp.sum(jnp.where(row_at == (cluster >> 7), row, 0), axis=0, keepdims=True)
            )
        slots.append(jnp.concatenate(found, axis=1).astype(F32))
        keys.append((user_at * KEY + pos_ref[r : r + 1, :] + 1).astype(F32))
    block = LANES
    groups = block // local
    sub = iota((block, users), 0).astype(F32)
    stores = []
    named_lane = iota((block, LANES), 1)
    named = [jnp.zeros((block, LANES), F32)]

    def assign(b):
        slot_at = sub + float(b * block)
        key = jnp.zeros((block, users), F32)
        for r in range(visits):
            key = jnp.where(slot_at == slots[r], keys[r], key)
        most = jnp.max(key, axis=1, keepdims=True)
        rest = jnp.sum(key, axis=1, keepdims=True) - most
        parts = []
        for c, chosen in enumerate((most, rest)):
            named[0] = jnp.where(named_lane == 2 * b + c, chosen, named[0])
            chosen = jnp.where(chosen > 0.0, chosen, -1.0)
            parts.append(jnp.where(key == chosen, 1.0, 0.0).reshape(block // 8, 8, users))
        place = jnp.concatenate(parts, axis=1).reshape(2 * block, users).astype(BF16)
        place_ref[b * 2 * block : (b + 1) * 2 * block, :] = place

    def name_users():
        user = jnp.floor((named[0] - 1.0) * (1.0 / KEY))
        named_ref[...] = user
        stores.append(pltpu.make_async_copy(named_ref, named_hbm, out_sem.at[0]))
        stores[-1].start()
        chosen = named[0].T
        user = jnp.floor((chosen - 1.0) * (1.0 / KEY))
        mark = jnp.where(chosen > 0.0, chosen - user * KEY, 0.0)
        top = jnp.floor(mark * (1.0 / 64.0))
        low = mark - top * 64.0
        for b in range(clusters // block):
            tail = jnp.concatenate([top[2 * b : 2 * b + 2], low[2 * b : 2 * b + 2]], axis=0)
            tail = jnp.concatenate([tail, tail], axis=0)
            send_ref[b * groups : (b + 1) * groups, 2 * local : rows, :] = jnp.broadcast_to(
                tail[None], (groups, rows - 2 * local, width)
            ).astype(BF16)
        span = (slice(None), pl.ds(2 * local, rows - 2 * local))
        stores.append(pltpu.make_async_copy(send_ref.at[span], send_hbm.at[span], out_sem.at[1]))
        stores[-1].start()

    early = 4
    for b in range(early):
        assign(b)
    for load in loads[3:]:
        load.wait()
    pre = mm(feat_ref[...], wh_ref[...])
    hidden = (pre * jax.nn.sigmoid(pre)).astype(BF16)
    query = mm(hidden, wo_ref[...]).astype(BF16)
    blocks = clusters // block
    for b in range(blocks):
        if b + early < blocks:
            assign(b + early)
        if b + early == blocks:
            name_users()
        sent = mm(place_ref[b * 2 * block : (b + 1) * 2 * block, :], query).astype(BF16)
        send_ref[b * groups : (b + 1) * groups, 0 : 2 * local, :] = sent.reshape(
            groups, 2 * local, width
        )
        if b % 4 == 3:
            span = (pl.ds((b - 3) * groups, 4 * groups), pl.ds(0, 2 * local))
            stores.append(
                pltpu.make_async_copy(send_ref.at[span], send_hbm.at[span], send_sem.at[b // 4])
            )
            stores[-1].start()
    for store in stores:
        store.wait()


def route(routes, positives, cluster_slot, features, w_hidden, w_out, devices):
    users, visits = routes.shape
    clusters = cluster_slot.shape[0]
    width = w_out.shape[1]
    rows = 2 * clusters // devices + 8
    args = (
        routes.T,
        positives.T,
        cluster_slot.reshape(clusters // LANES, LANES),
        features,
        w_hidden,
        w_out,
    )
    outs = (
        jax.ShapeDtypeStruct((devices, rows, width), BF16),
        jax.ShapeDtypeStruct((LANES, LANES), F32),
    )
    return pl.pallas_call(
        route_body,
        out_shape=outs_hbm(outs),
        in_specs=hbm(6),
        out_specs=hbm(2),
        scratch_shapes=[pltpu.VMEM(a.shape, a.dtype) for a in args + outs]
        + [
            pltpu.VMEM((2 * clusters, users), BF16),
            pltpu.SemaphoreType.DMA((6,)),
            pltpu.SemaphoreType.DMA((2,)),
            pltpu.SemaphoreType.DMA((4,)),
        ],
        compiler_params=params(48),
        name="route",
    )(*in_hbm(args))


def table_body(ids_ref, counts_ref, mass_hbm, tabs_hbm, inv_ref, mass_ref, tabs_ref, sem):
    clusters, chunks, lanes = tabs_ref.shape
    inv_ref[...] = 1.0 / counts_ref[...].astype(F32)
    tabs_ref[...] = ((ids_ref[...] << 12) | counts_ref[...]).reshape(tabs_ref.shape)
    store = pltpu.make_async_copy(tabs_ref, tabs_hbm, sem.at[0])
    store.start()
    item_at = iota((LANES, LANES), 0)

    def cluster(k, carry):
        acc = jnp.zeros((LANES, LANES), F32)
        for h in range(chunks):
            at = k * chunks + h
            hit = item_at == ids_ref[pl.ds(at, 1), :]
            acc = acc + jnp.where(hit, inv_ref[pl.ds(at, 1), :], 0.0)
        mass_ref[k] = jnp.broadcast_to(jnp.sum(acc, axis=1, keepdims=True), acc.shape)
        return carry

    lax.fori_loop(0, clusters, cluster, 0)
    last = pltpu.make_async_copy(mass_ref, mass_hbm, sem.at[1])
    last.start()
    last.wait()
    store.wait()


def tables(sample_ids, sample_counts):
    clusters, samples = sample_ids.shape
    total = sample_ids.size // LANES
    outs = (
        jax.ShapeDtypeStruct((clusters, LANES, LANES), F32),
        jax.ShapeDtypeStruct((clusters, samples // LANES, LANES), jnp.int32),
    )
    return pl.pallas_call(
        table_body,
        out_shape=outs_hbm(outs),
        in_specs=vmem(2),
        out_specs=hbm(2),
        scratch_shapes=[pltpu.VMEM((total, LANES), F32)]
        + [pltpu.VMEM(a.shape, a.dtype) for a in outs]
        + [pltpu.SemaphoreType.DMA((2,))],
        compiler_params=params(16),
        cost_estimate=pl.CostEstimate(flops=30_000_000, bytes_accessed=1 << 20, transcendentals=0),
        name="tables",
    )(sample_ids.reshape(total, LANES), sample_counts.reshape(total, LANES))


def row_of(slot):
    return slot // 8 * 16 + slot % 8


def owner_body(
    got_ref,
    items_hbm,
    mass_hbm,
    tabs_hbm,
    dq_hbm,
    weight_hbm,
    q_hbm,
    loss_ref,
    got32_ref,
    dq32_ref,
    dq_ref,
    weight_ref,
    q_ref,
    items_ref,
    mass_ref,
    tabs_ref,
    losses_ref,
    load_sem,
    dq_sem,
    weight_sem,
    q_sem,
):
    loads = [
        pltpu.make_async_copy(tabs_hbm, tabs_ref, load_sem.at[0]),
        pltpu.make_async_copy(items_hbm, items_ref, load_sem.at[1]),
    ]
    for part in range(mass_ref.shape[0] // 4):
        span = pl.ds(part * 4, 4)
        loads.append(
            pltpu.make_async_copy(mass_hbm.at[span], mass_ref.at[span], load_sem.at[2 + part])
        )
    for load in loads:
        load.start()
    devices, rows, width = got_ref.shape
    local = q_ref.shape[0]
    chunks = tabs_ref.shape[1]
    pairs = 2 * devices
    got32_ref[...] = got_ref[...].astype(F32).reshape(devices * rows, width)
    place_at = lax.axis_index("dev") % (LANES // local) * local
    tail_lane = iota((devices, LANES), 1)
    tail = jnp.zeros((devices, LANES), F32)
    for c in range(2):
        top = got32_ref[pl.ds(2 * local + c, devices, stride=rows), :]
        low = got32_ref[pl.ds(2 * local + 2 + c, devices, stride=rows), :]
        moved = pltpu.roll(top * 64.0 + low, (LANES + c * local - place_at) % LANES, 1)
        tail = jnp.where(tail_lane // local == c, moved, tail)
    tail = tail.T
    marks = [tail[c * local : (c + 1) * local, :] for c in range(2)]
    targets = [jnp.maximum(mark - 1.0, 0.0).astype(jnp.int32) for mark in marks]
    item_at = iota((LANES, pairs), 0)
    row_at = iota((chunks, devices), 0)
    for load in loads[0:2]:
        load.wait()
    stores = []

    def fetch(k):
        packed = []
        for target in targets:
            at = target[k : k + 1, :]
            lane = jnp.broadcast_to(at & (LANES - 1), (chunks, devices))
            found = jnp.take_along_axis(tabs_ref[k], lane, axis=1)
            packed.append(jnp.sum(jnp.where(row_at == (at >> 7), found, 0), axis=0, keepdims=True))
        packed = jnp.concatenate(packed, axis=1)
        live = jnp.concatenate([mark[k : k + 1, :] for mark in marks], axis=1) > 0.0
        queries = jnp.concatenate(
            [
                got32_ref[pl.ds(row_of(k), devices, stride=rows), :],
                got32_ref[pl.ds(row_of(k) + 8, devices, stride=rows), :],
            ],
            axis=0,
        ).astype(BF16)
        q_ref[k] = queries
        stores.append(pltpu.make_async_copy(q_ref.at[k], q_hbm.at[k], q_sem.at[k]))
        stores[-1].start()
        scores = mm(items_ref[k * LANES : (k + 1) * LANES, :], queries, ((1,), (1,)))
        return live, packed, scores

    def soften(k, live, packed, scores):
        item = jnp.where(live, packed >> 12, -1)
        count = (packed & 4095).astype(F32)
        if k % 4 == 0:
            loads[2 + k // 4].wait()
        column = jnp.concatenate([mass_ref[k]] * (pairs // LANES), axis=1)
        masked = jnp.where(column > 0.0, scores, NONE)
        top = jnp.max(masked, axis=0, keepdims=True)
        expo = jnp.exp(masked - top) * column
        total = jnp.sum(expo, axis=0, keepdims=True)
        hit = item_at == item
        picked = jnp.sum(jnp.where(hit, scores, 0.0), axis=0, keepdims=True)
        losses_ref[k : k + 1, :] = jnp.log(total) + top - (picked - jnp.log(count))
        weight = (expo * (1.0 / total) - jnp.where(hit, 1.0, 0.0)).astype(BF16)
        weight_ref[k] = weight
        stores.append(pltpu.make_async_copy(weight_ref.at[k], weight_hbm.at[k], weight_sem.at[k]))
        stores[-1].start()
        return weight

    def give(k, weight):
        dq = mm(weight, items_ref[k * LANES : (k + 1) * LANES, :], ((0,), (0,)))
        dq32_ref[pl.ds(row_of(k), devices, stride=rows), :] = dq[0:devices, :]
        dq32_ref[pl.ds(row_of(k) + 8, devices, stride=rows), :] = dq[devices:pairs, :]
        if k % 8 == 7:
            at = row_of(k) - 7
            dq_ref[:, at : at + 16, :] = (
                dq32_ref[...].reshape(devices, rows, width)[:, at : at + 16, :].astype(BF16)
            )
            span = (slice(None), pl.ds(at, 16))
            stores.append(
                pltpu.make_async_copy(dq_ref.at[span], dq_hbm.at[span], dq_sem.at[k // 8])
            )
            stores[-1].start()

    fetched = [fetch(k) for k in range(AHEAD)]
    for k in range(local):
        if k + AHEAD < local:
            fetched.append(fetch(k + AHEAD))
        give(k, soften(k, *fetched[k]))
    live = jnp.concatenate(marks, axis=1) > 0.0
    total = jnp.sum(jnp.where(live, losses_ref[...], 0.0), axis=1, keepdims=True)
    loss_ref[...] = total / jnp.sum(jnp.where(live, 1.0, 0.0), axis=1, keepdims=True)
    for store in stores:
        store.wait()


def owner(got, items, mass, tabs):
    devices, rows, width = got.shape
    local = items.shape[0] // LANES
    outs = (
        jax.ShapeDtypeStruct((devices, 2 * local, width), BF16),
        jax.ShapeDtypeStruct((local, LANES, 2 * devices), BF16),
        jax.ShapeDtypeStruct((local, 2 * devices, width), BF16),
    )
    return pl.pallas_call(
        owner_body,
        out_shape=outs_hbm(outs) + (jax.ShapeDtypeStruct((local, 1), F32),),
        in_specs=vmem(1) + hbm(3),
        out_specs=hbm(3) + vmem(1),
        scratch_shapes=[
            pltpu.VMEM((devices * rows, width), F32),
            pltpu.VMEM((devices * rows, width), F32),
        ]
        + [pltpu.VMEM(a.shape, a.dtype) for a in outs + (items, mass, tabs)]
        + [
            pltpu.VMEM((local, 2 * devices), F32),
            pltpu.SemaphoreType.DMA((2 + local // 4,)),
            pltpu.SemaphoreType.DMA((local // 8,)),
            pltpu.SemaphoreType.DMA((local,)),
            pltpu.SemaphoreType.DMA((local,)),
        ],
        compiler_params=params(40),
        name="owner",
    )(got, *in_hbm((items, mass, tabs)))


def item_body(weight_ref, q_ref, grad_ref):
    for k in range(weight_ref.shape[0]):
        grad_ref[k * LANES : (k + 1) * LANES, :] = mm(weight_ref[k], q_ref[k])


def item_grads(weight, queries):
    local, pairs, width = queries.shape
    step = 4
    return pl.pallas_call(
        item_body,
        grid=(local // step,),
        out_shape=jax.ShapeDtypeStruct((local * LANES, width), F32),
        in_specs=[
            pl.BlockSpec((step, LANES, pairs), lambda k: (k, 0, 0)),
            pl.BlockSpec((step, pairs, width), lambda k: (k, 0, 0)),
        ],
        out_specs=pl.BlockSpec((step * LANES, width), lambda k: (k, 0)),
        compiler_params=params(8),
        cost_estimate=pl.CostEstimate(
            flops=135_000_000, bytes_accessed=3 << 20, transcendentals=0
        ),
        name="item_grads",
    )(*in_hbm((weight, queries)))


def ready_body(feat_ref, feat_other_ref, wh_ref, *outs):
    half = outs[0].shape[0]
    core = lax.axis_index("dev") % 2
    weight = wh_ref[:, pl.ds(pl.multiple_of(core * half, half), half)]
    for i, ref in enumerate((feat_ref, feat_other_ref)):
        hidden_ref, slope_ref = outs[2 * i : 2 * i + 2]
        pre = mm(weight, ref[...], ((0,), (0,)))
        sig = jax.nn.sigmoid(pre)
        hidden_ref[...] = (pre * sig).astype(BF16)
        slope_ref[...] = (sig * (1.0 + pre * (1.0 - sig))).T


def ready(features_t, features_other_t, w_hidden):
    feats, users = features_t.shape
    hid = w_hidden.shape[1]
    half = hid // 2
    step = users // 2
    outs = (
        jax.ShapeDtypeStruct((half, users), BF16),
        jax.ShapeDtypeStruct((users, half), F32),
    ) * 2
    return pl.pallas_call(
        ready_body,
        grid=(users // step,),
        out_shape=outs_hbm(outs),
        in_specs=[pl.BlockSpec((feats, step), lambda i: (0, i))] * 2
        + [pl.BlockSpec((feats, hid), lambda i: (0, 0))],
        out_specs=[
            pl.BlockSpec((half, step), lambda i: (0, i)),
            pl.BlockSpec((step, half), lambda i: (i, 0)),
        ]
        * 2,
        compiler_params=params(24),
        cost_estimate=pl.CostEstimate(
            flops=550_000_000, bytes_accessed=5 << 20, transcendentals=1 << 19
        ),
        name="ready",
    )(*in_hbm((features_t, features_other_t, w_hidden)))


def collect_body(
    back_ref,
    named_ref,
    hidden_hbm,
    slope_hbm,
    feat_hbm,
    wo_hbm,
    dq_ref,
    hidden_ref,
    slope_ref,
    feat_ref,
    wo_ref,
    sem,
):
    half = hidden_ref.shape[0]
    core = lax.axis_index("dev") % 2
    wo_at = wo_hbm.at[pl.ds(pl.multiple_of(core * half, half), half), :]
    loads = [
        pltpu.make_async_copy(src, dst, sem.at[i])
        for i, (src, dst) in enumerate(
            [
                (wo_at, wo_ref),
                (slope_hbm, slope_ref),
                (feat_hbm, feat_ref),
                (hidden_hbm, hidden_ref),
            ]
        )
    ]
    for load in loads:
        load.start()
    devices, rows, width = back_ref.shape
    users = dq_ref.shape[0]
    block = LANES
    named = named_ref[...]
    lane_user = iota((block, users), 1).astype(F32)
    total = jnp.zeros((width, users), F32)
    group = 2 * block // rows
    for b in range(devices // group):
        parts = [
            jnp.where(lane_user == named[:, 2 * b + c : 2 * b + c + 1], 1.0, 0.0).reshape(
                block // 8, 8, users
            )
            for c in range(2)
        ]
        place = jnp.concatenate(parts, axis=1).reshape(2 * block, users).astype(BF16)
        back = back_ref[b * group : (b + 1) * group].reshape(2 * block, width)
        total = total + mm(back, place, ((0,), (0,)))
    dq_ref[...] = total.T.astype(BF16)
    for load in loads:
        load.wait()


def collect(back, named, hidden, slope, features_t, w_out):
    half, users = hidden.shape
    width = back.shape[2]
    return pl.pallas_call(
        collect_body,
        out_shape=outs_vmem(
            (
                jax.ShapeDtypeStruct((users, width), BF16),
                hidden,
                slope,
                features_t,
                jax.ShapeDtypeStruct((half, width), BF16),
            )
        ),
        in_specs=vmem(2) + hbm(4),
        out_specs=vmem(5),
        scratch_shapes=[pltpu.SemaphoreType.DMA((4,))],
        compiler_params=params(24),
        name="collect",
    )(back, named, *in_hbm((hidden, slope, features_t, w_out)))


def own_body(dq_ref, hidden_ref, slope_ref, feat_ref, wo_ref, big_ref, small_ref):
    dq = dq_ref[...]
    dpre = (mm(dq, wo_ref[...], ((1,), (1,))) * slope_ref[...]).astype(BF16)
    big_ref[...] = mm(feat_ref[...], dpre)
    small_ref[...] = mm(hidden_ref[...], dq)


def tower_own(dq, hidden, slope, features_t, w_half):
    half = hidden.shape[0]
    return pl.pallas_call(
        own_body,
        out_shape=(
            jax.ShapeDtypeStruct((features_t.shape[0], half), F32),
            jax.ShapeDtypeStruct((half, dq.shape[1]), F32),
        ),
        in_specs=vmem(5),
        out_specs=vmem(2),
        compiler_params=params(16),
        cost_estimate=pl.CostEstimate(
            flops=340_000_000, bytes_accessed=3 << 20, transcendentals=0
        ),
        name="tower_own",
    )(dq, hidden, slope, features_t, w_half)


def other_body(
    dq_ref, big_ref, small_ref, hidden_ref, slope_ref, feat_ref, wo_ref, grad_ref
):
    half = hidden_ref.shape[0]
    peers = grad_ref.shape[0]
    dq = dq_ref[...]
    dpre = (mm(dq, wo_ref[...], ((1,), (1,))) * slope_ref[...]).astype(BF16)
    big = big_ref[...] + mm(feat_ref[...], dpre)
    small = small_ref[...] + mm(hidden_ref[...], dq)
    tall = big.shape[0] // peers
    blocks = half // LANES
    for c in range(blocks):
        grad_ref[:, c * tall : (c + 1) * tall, :] = (
            big[:, c * LANES : (c + 1) * LANES].reshape(peers, tall, LANES).astype(BF16)
        )
    filled = half // 8
    at = blocks * tall
    grad_ref[0:filled, at : at + 8, :] = small.reshape(filled, 8, LANES).astype(BF16)
    grad_ref[filled:peers, at : at + 8, :] = jnp.zeros((peers - filled, 8, LANES), BF16)


def tower_other(dq, big, small, hidden, slope, features_t, w_half, peers):
    half = hidden.shape[0]
    rows = half * features_t.shape[0] // peers // LANES + 8
    return pl.pallas_call(
        other_body,
        out_shape=jax.ShapeDtypeStruct((peers, rows, LANES), BF16),
        in_specs=vmem(7),
        out_specs=vmem(1)[0],
        compiler_params=params(16),
        name="tower_other",
    )(dq, big, small, hidden, slope, features_t, w_half)


def sum_body(parts_ref, out_ref):
    total = jnp.sum(parts_ref[...].astype(F32), axis=0, keepdims=True)
    out_ref[...] = jnp.broadcast_to(total, out_ref.shape).astype(BF16)


def sum_parts(parts):
    return pl.pallas_call(
        sum_body,
        out_shape=jax.ShapeDtypeStruct(parts.shape, BF16),
        in_specs=vmem(1),
        out_specs=vmem(1)[0],
        compiler_params=params(24),
        name="sum_parts",
    )(parts)


def spread_body(side_of, got_ref, *refs):
    hidden_hbm, out_hbm, hidden_ref, out_ref, sem = refs[-5:]
    peers = got_ref.shape[0]
    side = lax.axis_index("dev") % 2
    side = side_of(side)
    half = out_ref.shape[0]
    tall = hidden_ref.shape[0] // peers
    blocks = half // LANES
    filled = half // 8
    stores = []
    for c in range(blocks):
        hidden_ref[:, c * LANES : (c + 1) * LANES] = (
            got_ref[:, c * tall : (c + 1) * tall, :].astype(F32).reshape(-1, LANES)
        )
        at = pl.multiple_of(side * half + c * LANES, LANES)
        stores.append(
            pltpu.make_async_copy(
                hidden_ref.at[:, pl.ds(c * LANES, LANES)],
                hidden_hbm.at[:, pl.ds(at, LANES)],
                sem.at[c],
            )
        )
        stores[-1].start()
    at = blocks * tall
    out_ref[...] = got_ref[0:filled, at : at + 8, :].astype(F32).reshape(half, LANES)
    stores.append(
        pltpu.make_async_copy(
            out_ref, out_hbm.at[pl.ds(pl.multiple_of(side * half, half), half), :], sem.at[blocks]
        )
    )
    stores[-1].start()
    for store in stores:
        store.wait()


def spread(got, side_of, hidden_shape, out_shape, begun=()):
    half = out_shape[0] // 2
    outs = (
        jax.ShapeDtypeStruct(hidden_shape, F32),
        jax.ShapeDtypeStruct(out_shape, F32),
    )
    return pl.pallas_call(
        functools.partial(spread_body, side_of),
        out_shape=outs_hbm(outs),
        in_specs=vmem(1) + hbm(len(begun)),
        out_specs=hbm(2),
        scratch_shapes=[
            pltpu.VMEM((hidden_shape[0], half), F32),
            pltpu.VMEM((half, LANES), F32),
            pltpu.SemaphoreType.DMA((half // LANES + 1,)),
        ],
        input_output_aliases={1 + i: i for i in range(len(begun))},
        compiler_params=params(16),
        cost_estimate=pl.CostEstimate(flops=300_000, bytes_accessed=2 << 20, transcendentals=0),
        name="spread",
    )(got, *in_hbm(begun))


def exchange(x):
    return lax.all_to_all(x, "dev", split_axis=0, concat_axis=0, tiled=True)


def exchange_peers(x):
    devices = lax.axis_size("dev")
    groups = [list(range(c, devices, 2)) for c in range(2)]
    return lax.all_to_all(
        x, "dev", split_axis=0, concat_axis=0, axis_index_groups=groups, tiled=True
    )


def swap(x):
    devices = lax.axis_size("dev")
    return lax.ppermute(x, "dev", [(d, d ^ 1) for d in range(devices)])


def local(
    features, w_hidden, w_out, items, routes, cluster_slot, sample_ids, sample_counts, positives
):
    devices = lax.axis_size("dev")
    features_t = features.T
    features_other_t = swap(features_t)
    send, named = route(routes, positives, cluster_slot, features, w_hidden, w_out, devices)
    mass, tabs = tables(sample_ids, sample_counts)
    got = exchange(send)
    got, mass, tabs, features_other_t = lax.optimization_barrier(
        (got, *in_hbm((mass, tabs)), features_other_t)
    )
    dq_slots, weight, queries, losses = owner(got, items, mass, tabs)
    back = exchange(dq_slots)
    prepared = ready(features_t, features_other_t, w_hidden)
    item_grad = item_grads(weight, queries)
    back, prepared, item_grad = lax.optimization_barrier((back, prepared, item_grad))
    dq, *held, w_half = collect(back, named, *prepared[0:2], features_t, w_out)
    dq_other = swap(dq)
    big, small = tower_own(dq, *held, w_half)
    partial = tower_other(
        dq_other, big, small, *prepared[2:4], features_other_t, w_half, devices // 2
    )
    summed = exchange_peers(sum_parts(exchange_peers(partial)))
    begun = spread(summed, lambda core: core, w_hidden.shape, w_out.shape)
    grad_hidden, grad_out = spread(
        swap(summed), lambda core: 1 - core, w_hidden.shape, w_out.shape, begun
    )
    slot_loss = losses[:, 0]
    return (slot_loss, grad_hidden, grad_out, item_grad)


def solution(mesh):
    in_specs = (
        P("dev", None),
        P(),
        P(),
        P("dev", None),
        P("dev", None),
        P(),
        P("dev", None),
        P("dev", None),
        P("dev", None),
    )
    out_specs = (P("dev"), P(), P(), P("dev", None))
    return jax.shard_map(local, mesh=mesh, in_specs=in_specs, out_specs=out_specs, check_vma=False)
```

```python
import functools

import jax
import jax.numpy as jnp
from jax import lax
from jax.experimental import pallas as pl
from jax.experimental.pallas import tpu as pltpu
from jax.sharding import PartitionSpec as P

F32 = jnp.float32
BF16 = jnp.bfloat16
NONE = -3.0e38
KEY = 4096
AHEAD = 4
LANES = 128


def vmem(count):
    return [pl.BlockSpec(memory_space=pltpu.VMEM)] * count


def in_hbm(arrays):
    return tuple(pltpu.with_memory_space_constraint(a, pltpu.HBM) for a in arrays)


def outs_hbm(arrays):
    return tuple(pltpu.HBM(a.shape, a.dtype) for a in arrays)


def outs_vmem(arrays):
    return tuple(pltpu.VMEM(a.shape, a.dtype) for a in arrays)


def hbm(count):
    return [pl.BlockSpec(memory_space=pltpu.HBM)] * count


def params(megabytes):
    return pltpu.CompilerParams(vmem_limit_bytes=megabytes << 20)


def iota(shape, axis):
    return lax.broadcasted_iota(jnp.int32, shape, axis)


def one_hot(mask):
    return jnp.where(mask, 1.0, 0.0).astype(BF16)


def mm(a, b, dims=((1,), (0,))):
    return lax.dot_general(a, b, (dims, ((), ())), preferred_element_type=F32)


def route_body(
    routes_hbm,
    pos_hbm,
    cslot_hbm,
    feat_hbm,
    wh_hbm,
    wo_hbm,
    send_hbm,
    named_hbm,
    routes_ref,
    pos_ref,
    cslot_ref,
    feat_ref,
    wh_ref,
    wo_ref,
    send_ref,
    named_ref,
    place_ref,
    in_sem,
    out_sem,
    send_sem,
):
    loads = [
        pltpu.make_async_copy(src, dst, in_sem.at[i])
        for i, (src, dst) in enumerate(
            [
                (routes_hbm, routes_ref),
                (pos_hbm, pos_ref),
                (cslot_hbm, cslot_ref),
                (feat_hbm, feat_ref),
                (wh_hbm, wh_ref),
                (wo_hbm, wo_ref),
            ]
        )
    ]
    for load in loads:
        load.start()
    visits, users = routes_ref.shape
    clusters = cslot_ref.shape[0] * LANES
    devices, rows, width = send_ref.shape
    local = clusters // devices
    for load in loads[:3]:
        load.wait()
    cslot = cslot_ref[...]
    row_at = iota((cslot.shape[0], LANES), 0)
    user_at = iota((1, users), 1)
    slots = []
    keys = []
    for r in range(visits):
        found = []
        for part in range(users // LANES):
            cluster = routes_ref[r : r + 1, part * LANES : (part + 1) * LANES]
            lane = jnp.broadcast_to(cluster & (LANES - 1), cslot.shape)
            row = jnp.take_along_axis(cslot, lane, axis=1)
            found.append(
                jnp.sum(jnp.where(row_at == (cluster >> 7), row, 0), axis=0, keepdims=True)
            )
        slots.append(jnp.concatenate(found, axis=1).astype(F32))
        keys.append((user_at * KEY + pos_ref[r : r + 1, :] + 1).astype(F32))
    block = LANES
    groups = block // local
    sub = iota((block, users), 0).astype(F32)
    stores = []
    named_lane = iota((block, LANES), 1)
    named = [jnp.zeros((block, LANES), F32)]

    def assign(b):
        slot_at = sub + float(b * block)
        key = jnp.zeros((block, users), F32)
        for r in range(visits):
            key = jnp.where(slot_at == slots[r], keys[r], key)
        most = jnp.max(key, axis=1, keepdims=True)
        rest = jnp.sum(key, axis=1, keepdims=True) - most
        parts = []
        for c, chosen in enumerate((most, rest)):
            named[0] = jnp.where(named_lane == 2 * b + c, chosen, named[0])
            chosen = jnp.where(chosen > 0.0, chosen, -1.0)
            parts.append(jnp.where(key == chosen, 1.0, 0.0).reshape(block // 8, 8, users))
        place = jnp.concatenate(parts, axis=1).reshape(2 * block, users).astype(BF16)
        place_ref[b * 2 * block : (b + 1) * 2 * block, :] = place

    def name_users():
        user = jnp.floor((named[0] - 1.0) * (1.0 / KEY))
        named_ref[...] = user
        stores.append(pltpu.make_async_copy(named_ref, named_hbm, out_sem.at[0]))
        stores[-1].start()
        chosen = named[0].T
        user = jnp.floor((chosen - 1.0) * (1.0 / KEY))
        mark = jnp.where(chosen > 0.0, chosen - user * KEY, 0.0)
        top = jnp.floor(mark * (1.0 / 64.0))
        low = mark - top * 64.0
        for b in range(clusters // block):
            tail = jnp.concatenate([top[2 * b : 2 * b + 2], low[2 * b : 2 * b + 2]], axis=0)
            tail = jnp.concatenate([tail, tail], axis=0)
            send_ref[b * groups : (b + 1) * groups, 2 * local : rows, :] = jnp.broadcast_to(
                tail[None], (groups, rows - 2 * local, width)
            ).astype(BF16)
        span = (slice(None), pl.ds(2 * local, rows - 2 * local))
        stores.append(pltpu.make_async_copy(send_ref.at[span], send_hbm.at[span], out_sem.at[1]))
        stores[-1].start()

    early = 4
    for b in range(early):
        assign(b)
    for load in loads[3:]:
        load.wait()
    pre = mm(feat_ref[...], wh_ref[...])
    hidden = (pre * jax.nn.sigmoid(pre)).astype(BF16)
    query = mm(hidden, wo_ref[...]).astype(BF16)
    blocks = clusters // block
    for b in range(blocks):
        if b + early < blocks:
            assign(b + early)
        if b + early == blocks:
            name_users()
        sent = mm(place_ref[b * 2 * block : (b + 1) * 2 * block, :], query).astype(BF16)
        send_ref[b * groups : (b + 1) * groups, 0 : 2 * local, :] = sent.reshape(
            groups, 2 * local, width
        )
        if b % 4 == 3:
            span = (pl.ds((b - 3) * groups, 4 * groups), pl.ds(0, 2 * local))
            stores.append(
                pltpu.make_async_copy(send_ref.at[span], send_hbm.at[span], send_sem.at[b // 4])
            )
            stores[-1].start()
    for store in stores:
        store.wait()


def route(routes, positives, cluster_slot, features, w_hidden, w_out, devices):
    users, visits = routes.shape
    clusters = cluster_slot.shape[0]
    width = w_out.shape[1]
    rows = 2 * clusters // devices + 8
    args = (
        routes.T,
        positives.T,
        cluster_slot.reshape(clusters // LANES, LANES),
        features,
        w_hidden,
        w_out,
    )
    outs = (
        jax.ShapeDtypeStruct((devices, rows, width), BF16),
        jax.ShapeDtypeStruct((LANES, LANES), F32),
    )
    return pl.pallas_call(
        route_body,
        out_shape=outs_hbm(outs),
        in_specs=hbm(6),
        out_specs=hbm(2),
        scratch_shapes=[pltpu.VMEM(a.shape, a.dtype) for a in args + outs]
        + [
            pltpu.VMEM((2 * clusters, users), BF16),
            pltpu.SemaphoreType.DMA((6,)),
            pltpu.SemaphoreType.DMA((2,)),
            pltpu.SemaphoreType.DMA((4,)),
        ],
        compiler_params=params(48),
        name="route",
    )(*in_hbm(args))


def table_body(ids_ref, counts_ref, mass_hbm, tabs_hbm, inv_ref, mass_ref, tabs_ref, sem):
    clusters, chunks, lanes = tabs_ref.shape
    inv_ref[...] = 1.0 / counts_ref[...].astype(F32)
    tabs_ref[...] = ((ids_ref[...] << 12) | counts_ref[...]).reshape(tabs_ref.shape)
    store = pltpu.make_async_copy(tabs_ref, tabs_hbm, sem.at[0])
    store.start()
    item_at = iota((LANES, LANES), 0)

    def cluster(k, carry):
        acc = jnp.zeros((LANES, LANES), F32)
        for h in range(chunks):
            at = k * chunks + h
            hit = item_at == ids_ref[pl.ds(at, 1), :]
            acc = acc + jnp.where(hit, inv_ref[pl.ds(at, 1), :], 0.0)
        mass_ref[k] = jnp.broadcast_to(jnp.sum(acc, axis=1, keepdims=True), acc.shape)
        return carry

    lax.fori_loop(0, clusters, cluster, 0)
    last = pltpu.make_async_copy(mass_ref, mass_hbm, sem.at[1])
    last.start()
    last.wait()
    store.wait()


def tables(sample_ids, sample_counts):
    clusters, samples = sample_ids.shape
    total = sample_ids.size // LANES
    outs = (
        jax.ShapeDtypeStruct((clusters, LANES, LANES), F32),
        jax.ShapeDtypeStruct((clusters, samples // LANES, LANES), jnp.int32),
    )
    return pl.pallas_call(
        table_body,
        out_shape=outs_hbm(outs),
        in_specs=vmem(2),
        out_specs=hbm(2),
        scratch_shapes=[pltpu.VMEM((total, LANES), F32)]
        + [pltpu.VMEM(a.shape, a.dtype) for a in outs]
        + [pltpu.SemaphoreType.DMA((2,))],
        compiler_params=params(16),
        cost_estimate=pl.CostEstimate(flops=30_000_000, bytes_accessed=1 << 20, transcendentals=0),
        name="tables",
    )(sample_ids.reshape(total, LANES), sample_counts.reshape(total, LANES))


def row_of(slot):
    return slot // 8 * 16 + slot % 8


def owner_body(
    got_ref,
    items_hbm,
    mass_hbm,
    tabs_hbm,
    dq_hbm,
    weight_hbm,
    q_hbm,
    loss_ref,
    got32_ref,
    dq32_ref,
    dq_ref,
    weight_ref,
    q_ref,
    items_ref,
    mass_ref,
    tabs_ref,
    losses_ref,
    load_sem,
    dq_sem,
    weight_sem,
    q_sem,
):
    loads = [
        pltpu.make_async_copy(tabs_hbm, tabs_ref, load_sem.at[0]),
        pltpu.make_async_copy(items_hbm, items_ref, load_sem.at[1]),
    ]
    for part in range(mass_ref.shape[0] // 4):
        span = pl.ds(part * 4, 4)
        loads.append(
            pltpu.make_async_copy(mass_hbm.at[span], mass_ref.at[span], load_sem.at[2 + part])
        )
    for load in loads:
        load.start()
    devices, rows, width = got_ref.shape
    local = q_ref.shape[0]
    chunks = tabs_ref.shape[1]
    pairs = 2 * devices
    got32_ref[...] = got_ref[...].astype(F32).reshape(devices * rows, width)
    place_at = lax.axis_index("dev") % (LANES // local) * local
    tail_lane = iota((devices, LANES), 1)
    tail = jnp.zeros((devices, LANES), F32)
    for c in range(2):
        top = got32_ref[pl.ds(2 * local + c, devices, stride=rows), :]
        low = got32_ref[pl.ds(2 * local + 2 + c, devices, stride=rows), :]
        moved = pltpu.roll(top * 64.0 + low, (LANES + c * local - place_at) % LANES, 1)
        tail = jnp.where(tail_lane // local == c, moved, tail)
    tail = tail.T
    marks = [tail[c * local : (c + 1) * local, :] for c in range(2)]
    targets = [jnp.maximum(mark - 1.0, 0.0).astype(jnp.int32) for mark in marks]
    item_at = iota((LANES, pairs), 0)
    row_at = iota((chunks, devices), 0)
    for load in loads[0:2]:
        load.wait()
    stores = []

    def fetch(k):
        packed = []
        for target in targets:
            at = target[k : k + 1, :]
            lane = jnp.broadcast_to(at & (LANES - 1), (chunks, devices))
            found = jnp.take_along_axis(tabs_ref[k], lane, axis=1)
            packed.append(jnp.sum(jnp.where(row_at == (at >> 7), found, 0), axis=0, keepdims=True))
        packed = jnp.concatenate(packed, axis=1)
        live = jnp.concatenate([mark[k : k + 1, :] for mark in marks], axis=1) > 0.0
        queries = jnp.concatenate(
            [
                got32_ref[pl.ds(row_of(k), devices, stride=rows), :],
                got32_ref[pl.ds(row_of(k) + 8, devices, stride=rows), :],
            ],
            axis=0,
        ).astype(BF16)
        q_ref[k] = queries
        stores.append(pltpu.make_async_copy(q_ref.at[k], q_hbm.at[k], q_sem.at[k]))
        stores[-1].start()
        scores = mm(items_ref[k * LANES : (k + 1) * LANES, :], queries, ((1,), (1,)))
        return live, packed, scores

    def soften(k, live, packed, scores):
        item = jnp.where(live, packed >> 12, -1)
        count = (packed & 4095).astype(F32)
        if k % 4 == 0:
            loads[2 + k // 4].wait()
        column = jnp.concatenate([mass_ref[k]] * (pairs // LANES), axis=1)
        masked = jnp.where(column > 0.0, scores, NONE)
        top = jnp.max(masked, axis=0, keepdims=True)
        expo = jnp.exp(masked - top) * column
        total = jnp.sum(expo, axis=0, keepdims=True)
        hit = item_at == item
        picked = jnp.sum(jnp.where(hit, scores, 0.0), axis=0, keepdims=True)
        losses_ref[k : k + 1, :] = jnp.log(total) + top - (picked - jnp.log(count))
        weight = (expo * (1.0 / total) - jnp.where(hit, 1.0, 0.0)).astype(BF16)
        weight_ref[k] = weight
        stores.append(pltpu.make_async_copy(weight_ref.at[k], weight_hbm.at[k], weight_sem.at[k]))
        stores[-1].start()
        return weight

    def give(k, weight):
        dq = mm(weight, items_ref[k * LANES : (k + 1) * LANES, :], ((0,), (0,)))
        dq32_ref[pl.ds(row_of(k), devices, stride=rows), :] = dq[0:devices, :]
        dq32_ref[pl.ds(row_of(k) + 8, devices, stride=rows), :] = dq[devices:pairs, :]
        if k % 8 == 7:
            at = row_of(k) - 7
            dq_ref[:, at : at + 16, :] = (
                dq32_ref[...].reshape(devices, rows, width)[:, at : at + 16, :].astype(BF16)
            )
            span = (slice(None), pl.ds(at, 16))
            stores.append(
                pltpu.make_async_copy(dq_ref.at[span], dq_hbm.at[span], dq_sem.at[k // 8])
            )
            stores[-1].start()

    fetched = [fetch(k) for k in range(AHEAD)]
    for k in range(local):
        if k + AHEAD < local:
            fetched.append(fetch(k + AHEAD))
        give(k, soften(k, *fetched[k]))
    live = jnp.concatenate(marks, axis=1) > 0.0
    total = jnp.sum(jnp.where(live, losses_ref[...], 0.0), axis=1, keepdims=True)
    loss_ref[...] = total / jnp.sum(jnp.where(live, 1.0, 0.0), axis=1, keepdims=True)
    for store in stores:
        store.wait()


def owner(got, items, mass, tabs):
    devices, rows, width = got.shape
    local = items.shape[0] // LANES
    outs = (
        jax.ShapeDtypeStruct((devices, 2 * local, width), BF16),
        jax.ShapeDtypeStruct((local, LANES, 2 * devices), BF16),
        jax.ShapeDtypeStruct((local, 2 * devices, width), BF16),
    )
    return pl.pallas_call(
        owner_body,
        out_shape=outs_hbm(outs) + (jax.ShapeDtypeStruct((local, 1), F32),),
        in_specs=vmem(1) + hbm(3),
        out_specs=hbm(3) + vmem(1),
        scratch_shapes=[
            pltpu.VMEM((devices * rows, width), F32),
            pltpu.VMEM((devices * rows, width), F32),
        ]
        + [pltpu.VMEM(a.shape, a.dtype) for a in outs + (items, mass, tabs)]
        + [
            pltpu.VMEM((local, 2 * devices), F32),
            pltpu.SemaphoreType.DMA((2 + local // 4,)),
            pltpu.SemaphoreType.DMA((local // 8,)),
            pltpu.SemaphoreType.DMA((local,)),
            pltpu.SemaphoreType.DMA((local,)),
        ],
        compiler_params=params(40),
        name="owner",
    )(got, *in_hbm((items, mass, tabs)))


def item_body(weight_ref, q_ref, grad_ref):
    for k in range(weight_ref.shape[0]):
        grad_ref[k * LANES : (k + 1) * LANES, :] = mm(weight_ref[k], q_ref[k])


def item_grads(weight, queries):
    local, pairs, width = queries.shape
    step = 4
    return pl.pallas_call(
        item_body,
        grid=(local // step,),
        out_shape=jax.ShapeDtypeStruct((local * LANES, width), F32),
        in_specs=[
            pl.BlockSpec((step, LANES, pairs), lambda k: (k, 0, 0)),
            pl.BlockSpec((step, pairs, width), lambda k: (k, 0, 0)),
        ],
        out_specs=pl.BlockSpec((step * LANES, width), lambda k: (k, 0)),
        compiler_params=params(8),
        cost_estimate=pl.CostEstimate(
            flops=135_000_000, bytes_accessed=3 << 20, transcendentals=0
        ),
        name="item_grads",
    )(*in_hbm((weight, queries)))


def ready_body(feat_ref, feat_other_ref, wh_ref, *outs):
    half = outs[0].shape[0]
    core = lax.axis_index("dev") % 2
    weight = wh_ref[:, pl.ds(pl.multiple_of(core * half, half), half)]
    for i, ref in enumerate((feat_ref, feat_other_ref)):
        hidden_ref, slope_ref = outs[2 * i : 2 * i + 2]
        pre = mm(weight, ref[...], ((0,), (0,)))
        sig = jax.nn.sigmoid(pre)
        hidden_ref[...] = (pre * sig).astype(BF16)
        slope_ref[...] = (sig * (1.0 + pre * (1.0 - sig))).T


def ready(features_t, features_other_t, w_hidden):
    feats, users = features_t.shape
    hid = w_hidden.shape[1]
    half = hid // 2
    step = users // 2
    outs = (
        jax.ShapeDtypeStruct((half, users), BF16),
        jax.ShapeDtypeStruct((users, half), F32),
    ) * 2
    return pl.pallas_call(
        ready_body,
        grid=(users // step,),
        out_shape=outs_hbm(outs),
        in_specs=[pl.BlockSpec((feats, step), lambda i: (0, i))] * 2
        + [pl.BlockSpec((feats, hid), lambda i: (0, 0))],
        out_specs=[
            pl.BlockSpec((half, step), lambda i: (0, i)),
            pl.BlockSpec((step, half), lambda i: (i, 0)),
        ]
        * 2,
        compiler_params=params(24),
        cost_estimate=pl.CostEstimate(
            flops=550_000_000, bytes_accessed=5 << 20, transcendentals=1 << 19
        ),
        name="ready",
    )(*in_hbm((features_t, features_other_t, w_hidden)))


def collect_body(
    back_ref,
    named_ref,
    hidden_hbm,
    slope_hbm,
    feat_hbm,
    wo_hbm,
    dq_ref,
    hidden_ref,
    slope_ref,
    feat_ref,
    wo_ref,
    sem,
):
    half = hidden_ref.shape[0]
    core = lax.axis_index("dev") % 2
    wo_at = wo_hbm.at[pl.ds(pl.multiple_of(core * half, half), half), :]
    loads = [
        pltpu.make_async_copy(src, dst, sem.at[i])
        for i, (src, dst) in enumerate(
            [
                (wo_at, wo_ref),
                (slope_hbm, slope_ref),
                (feat_hbm, feat_ref),
                (hidden_hbm, hidden_ref),
            ]
        )
    ]
    for load in loads:
        load.start()
    devices, rows, width = back_ref.shape
    users = dq_ref.shape[0]
    block = LANES
    named = named_ref[...]
    lane_user = iota((block, users), 1).astype(F32)
    total = jnp.zeros((width, users), F32)
    group = 2 * block // rows
    for b in range(devices // group):
        parts = [
            jnp.where(lane_user == named[:, 2 * b + c : 2 * b + c + 1], 1.0, 0.0).reshape(
                block // 8, 8, users
            )
            for c in range(2)
        ]
        place = jnp.concatenate(parts, axis=1).reshape(2 * block, users).astype(BF16)
        back = back_ref[b * group : (b + 1) * group].reshape(2 * block, width)
        total = total + mm(back, place, ((0,), (0,)))
    dq_ref[...] = total.T.astype(BF16)
    for load in loads:
        load.wait()


def collect(back, named, hidden, slope, features_t, w_out):
    half, users = hidden.shape
    width = back.shape[2]
    return pl.pallas_call(
        collect_body,
        out_shape=outs_vmem(
            (
                jax.ShapeDtypeStruct((users, width), BF16),
                hidden,
                slope,
                features_t,
                jax.ShapeDtypeStruct((half, width), BF16),
            )
        ),
        in_specs=vmem(2) + hbm(4),
        out_specs=vmem(5),
        scratch_shapes=[pltpu.SemaphoreType.DMA((4,))],
        compiler_params=params(24),
        name="collect",
    )(back, named, *in_hbm((hidden, slope, features_t, w_out)))


def own_body(dq_ref, hidden_ref, slope_ref, feat_ref, wo_ref, big_ref, small_ref):
    dq = dq_ref[...]
    dpre = (mm(dq, wo_ref[...], ((1,), (1,))) * slope_ref[...]).astype(BF16)
    big_ref[...] = mm(feat_ref[...], dpre)
    small_ref[...] = mm(hidden_ref[...], dq)


def tower_own(dq, hidden, slope, features_t, w_half):
    half = hidden.shape[0]
    return pl.pallas_call(
        own_body,
        out_shape=(
            jax.ShapeDtypeStruct((features_t.shape[0], half), F32),
            jax.ShapeDtypeStruct((half, dq.shape[1]), F32),
        ),
        in_specs=vmem(5),
        out_specs=vmem(2),
        compiler_params=params(16),
        cost_estimate=pl.CostEstimate(
            flops=340_000_000, bytes_accessed=3 << 20, transcendentals=0
        ),
        name="tower_own",
    )(dq, hidden, slope, features_t, w_half)


def other_body(
    dq_ref, big_ref, small_ref, hidden_ref, slope_ref, feat_ref, wo_ref, grad_ref
):
    half = hidden_ref.shape[0]
    peers = grad_ref.shape[0]
    dq = dq_ref[...]
    dpre = (mm(dq, wo_ref[...], ((1,), (1,))) * slope_ref[...]).astype(BF16)
    big = big_ref[...] + mm(feat_ref[...], dpre)
    small = small_ref[...] + mm(hidden_ref[...], dq)
    tall = big.shape[0] // peers
    blocks = half // LANES
    for c in range(blocks):
        grad_ref[:, c * tall : (c + 1) * tall, :] = (
            big[:, c * LANES : (c + 1) * LANES].reshape(peers, tall, LANES).astype(BF16)
        )
    filled = half // 8
    at = blocks * tall
    grad_ref[0:filled, at : at + 8, :] = small.reshape(filled, 8, LANES).astype(BF16)
    grad_ref[filled:peers, at : at + 8, :] = jnp.zeros((peers - filled, 8, LANES), BF16)


def tower_other(dq, big, small, hidden, slope, features_t, w_half, peers):
    half = hidden.shape[0]
    rows = half * features_t.shape[0] // peers // LANES + 8
    return pl.pallas_call(
        other_body,
        out_shape=jax.ShapeDtypeStruct((peers, rows, LANES), BF16),
        in_specs=vmem(7),
        out_specs=vmem(1)[0],
        compiler_params=params(16),
        name="tower_other",
    )(dq, big, small, hidden, slope, features_t, w_half)


def sum_body(parts_ref, out_ref):
    total = jnp.sum(parts_ref[...].astype(F32), axis=0, keepdims=True)
    out_ref[...] = jnp.broadcast_to(total, out_ref.shape).astype(BF16)


def sum_parts(parts):
    return pl.pallas_call(
        sum_body,
        out_shape=jax.ShapeDtypeStruct(parts.shape, BF16),
        in_specs=vmem(1),
        out_specs=vmem(1)[0],
        compiler_params=params(24),
        name="sum_parts",
    )(parts)


def spread_body(side_of, got_ref, *refs):
    hidden_hbm, out_hbm, hidden_ref, out_ref, sem = refs[-5:]
    peers = got_ref.shape[0]
    side = lax.axis_index("dev") % 2
    side = side_of(side)
    half = out_ref.shape[0]
    tall = hidden_ref.shape[0] // peers
    blocks = half // LANES
    filled = half // 8
    stores = []
    for c in range(blocks):
        hidden_ref[:, c * LANES : (c + 1) * LANES] = (
            got_ref[:, c * tall : (c + 1) * tall, :].astype(F32).reshape(-1, LANES)
        )
        at = pl.multiple_of(side * half + c * LANES, LANES)
        stores.append(
            pltpu.make_async_copy(
                hidden_ref.at[:, pl.ds(c * LANES, LANES)],
                hidden_hbm.at[:, pl.ds(at, LANES)],
                sem.at[c],
            )
        )
        stores[-1].start()
    at = blocks * tall
    out_ref[...] = got_ref[0:filled, at : at + 8, :].astype(F32).reshape(half, LANES)
    stores.append(
        pltpu.make_async_copy(
            out_ref, out_hbm.at[pl.ds(pl.multiple_of(side * half, half), half), :], sem.at[blocks]
        )
    )
    stores[-1].start()
    for store in stores:
        store.wait()


def spread(got, side_of, hidden_shape, out_shape, begun=()):
    half = out_shape[0] // 2
    outs = (
        jax.ShapeDtypeStruct(hidden_shape, F32),
        jax.ShapeDtypeStruct(out_shape, F32),
    )
    return pl.pallas_call(
        functools.partial(spread_body, side_of),
        out_shape=outs_hbm(outs),
        in_specs=vmem(1) + hbm(len(begun)),
        out_specs=hbm(2),
        scratch_shapes=[
            pltpu.VMEM((hidden_shape[0], half), F32),
            pltpu.VMEM((half, LANES), F32),
            pltpu.SemaphoreType.DMA((half // LANES + 1,)),
        ],
        input_output_aliases={1 + i: i for i in range(len(begun))},
        compiler_params=params(16),
        cost_estimate=pl.CostEstimate(flops=300_000, bytes_accessed=2 << 20, transcendentals=0),
        name="spread",
    )(got, *in_hbm(begun))


def exchange(x):
    return lax.all_to_all(x, "dev", split_axis=0, concat_axis=0, tiled=True)


def exchange_peers(x):
    devices = lax.axis_size("dev")
    groups = [list(range(c, devices, 2)) for c in range(2)]
    return lax.all_to_all(
        x, "dev", split_axis=0, concat_axis=0, axis_index_groups=groups, tiled=True
    )


def swap(x):
    devices = lax.axis_size("dev")
    return lax.ppermute(x, "dev", [(d, d ^ 1) for d in range(devices)])


def local(
    features, w_hidden, w_out, items, routes, cluster_slot, sample_ids, sample_counts, positives
):
    devices = lax.axis_size("dev")
    features_t = features.T
    features_other_t = swap(features_t)
    send, named = route(routes, positives, cluster_slot, features, w_hidden, w_out, devices)
    mass, tabs = tables(sample_ids, sample_counts)
    got = exchange(send)
    got, mass, tabs, features_other_t = lax.optimization_barrier(
        (got, *in_hbm((mass, tabs)), features_other_t)
    )
    dq_slots, weight, queries, losses = owner(got, items, mass, tabs)
    back = exchange(dq_slots)
    prepared = ready(features_t, features_other_t, w_hidden)
    item_grad = item_grads(weight, queries)
    back, prepared, item_grad = lax.optimization_barrier((back, prepared, item_grad))
    dq, *held, w_half = collect(back, named, *prepared[0:2], features_t, w_out)
    dq_other = swap(dq)
    big, small = tower_own(dq, *held, w_half)
    partial = tower_other(
        dq_other, big, small, *prepared[2:4], features_other_t, w_half, devices // 2
    )
    summed = exchange_peers(sum_parts(exchange_peers(partial)))
    begun = spread(summed, lambda core: core, w_hidden.shape, w_out.shape)
    grad_hidden, grad_out = spread(
        swap(summed), lambda core: 1 - core, w_hidden.shape, w_out.shape, begun
    )
    slot_loss = losses[:, 0]
    return (slot_loss, grad_hidden, grad_out, item_grad)


def solution(mesh):
    in_specs = (
        P("dev", None),
        P(),
        P(),
        P("dev", None),
        P("dev", None),
        P(),
        P("dev", None),
        P("dev", None),
        P("dev", None),
    )
    out_specs = (P("dev"), P(), P(), P("dev", None))
    return jax.shard_map(local, mesh=mesh, in_specs=in_specs, out_specs=out_specs, check_vma=False)
```

```python
import functools

import jax
import jax.numpy as jnp
from jax import lax
from jax.experimental import pallas as pl
from jax.experimental.pallas import tpu as pltpu
from jax.sharding import PartitionSpec as P

F32 = jnp.float32
BF16 = jnp.bfloat16
NONE = -3.0e38
KEY = 4096
AHEAD = 6
LANES = 128


def vmem(count):
    return [pl.BlockSpec(memory_space=pltpu.VMEM)] * count


def in_hbm(arrays):
    return tuple(pltpu.with_memory_space_constraint(a, pltpu.HBM) for a in arrays)


def outs_hbm(arrays):
    return tuple(pltpu.HBM(a.shape, a.dtype) for a in arrays)


def outs_vmem(arrays):
    return tuple(pltpu.VMEM(a.shape, a.dtype) for a in arrays)


def hbm(count):
    return [pl.BlockSpec(memory_space=pltpu.HBM)] * count


def params(megabytes):
    return pltpu.CompilerParams(vmem_limit_bytes=megabytes << 20)


def iota(shape, axis):
    return lax.broadcasted_iota(jnp.int32, shape, axis)


def one_hot(mask):
    return jnp.where(mask, 1.0, 0.0).astype(BF16)


def mm(a, b, dims=((1,), (0,))):
    return lax.dot_general(a, b, (dims, ((), ())), preferred_element_type=F32)


def route_body(
    routes_hbm,
    pos_hbm,
    cslot_hbm,
    feat_hbm,
    wh_hbm,
    wo_hbm,
    send_hbm,
    named_hbm,
    routes_ref,
    pos_ref,
    cslot_ref,
    feat_ref,
    wh_ref,
    wo_ref,
    send_ref,
    named_ref,
    place_ref,
    in_sem,
    out_sem,
    send_sem,
):
    loads = [
        pltpu.make_async_copy(src, dst, in_sem.at[i])
        for i, (src, dst) in enumerate(
            [
                (routes_hbm, routes_ref),
                (pos_hbm, pos_ref),
                (cslot_hbm, cslot_ref),
                (feat_hbm, feat_ref),
                (wh_hbm, wh_ref),
                (wo_hbm, wo_ref),
            ]
        )
    ]
    for load in loads:
        load.start()
    visits, users = routes_ref.shape
    clusters = cslot_ref.shape[0] * LANES
    devices, rows, width = send_ref.shape
    local = clusters // devices
    for load in loads[:3]:
        load.wait()
    cslot = cslot_ref[...]
    row_at = iota((cslot.shape[0], LANES), 0)
    user_at = iota((1, users), 1)
    slots = []
    keys = []
    for r in range(visits):
        found = []
        for part in range(users // LANES):
            cluster = routes_ref[r : r + 1, part * LANES : (part + 1) * LANES]
            lane = jnp.broadcast_to(cluster & (LANES - 1), cslot.shape)
            row = jnp.take_along_axis(cslot, lane, axis=1)
            found.append(
                jnp.sum(jnp.where(row_at == (cluster >> 7), row, 0), axis=0, keepdims=True)
            )
        slots.append(jnp.concatenate(found, axis=1).astype(F32))
        keys.append((user_at * KEY + pos_ref[r : r + 1, :] + 1).astype(F32))
    block = LANES
    groups = block // local
    sub = iota((block, users), 0).astype(F32)
    stores = []
    named_lane = iota((block, LANES), 1)
    named = [jnp.zeros((block, LANES), F32)]

    def assign(b):
        slot_at = sub + float(b * block)
        key = jnp.zeros((block, users), F32)
        for r in range(visits):
            key = jnp.where(slot_at == slots[r], keys[r], key)
        most = jnp.max(key, axis=1, keepdims=True)
        rest = jnp.sum(key, axis=1, keepdims=True) - most
        parts = []
        for c, chosen in enumerate((most, rest)):
            named[0] = jnp.where(named_lane == 2 * b + c, chosen, named[0])
            chosen = jnp.where(chosen > 0.0, chosen, -1.0)
            parts.append(jnp.where(key == chosen, 1.0, 0.0).reshape(block // 8, 8, users))
        place = jnp.concatenate(parts, axis=1).reshape(2 * block, users).astype(BF16)
        place_ref[b * 2 * block : (b + 1) * 2 * block, :] = place

    def name_users():
        user = jnp.floor((named[0] - 1.0) * (1.0 / KEY))
        named_ref[...] = user
        stores.append(pltpu.make_async_copy(named_ref, named_hbm, out_sem.at[0]))
        stores[-1].start()
        chosen = named[0].T
        user = jnp.floor((chosen - 1.0) * (1.0 / KEY))
        mark = jnp.where(chosen > 0.0, chosen - user * KEY, 0.0)
        top = jnp.floor(mark * (1.0 / 64.0))
        low = mark - top * 64.0
        for b in range(clusters // block):
            tail = jnp.concatenate([top[2 * b : 2 * b + 2], low[2 * b : 2 * b + 2]], axis=0)
            tail = jnp.concatenate([tail, tail], axis=0)
            send_ref[b * groups : (b + 1) * groups, 2 * local : rows, :] = jnp.broadcast_to(
                tail[None], (groups, rows - 2 * local, width)
            ).astype(BF16)
        span = (slice(None), pl.ds(2 * local, rows - 2 * local))
        stores.append(pltpu.make_async_copy(send_ref.at[span], send_hbm.at[span], out_sem.at[1]))
        stores[-1].start()

    early = 4
    for b in range(early):
        assign(b)
    for load in loads[3:]:
        load.wait()
    pre = mm(feat_ref[...], wh_ref[...])
    hidden = (pre * jax.nn.sigmoid(pre)).astype(BF16)
    query = mm(hidden, wo_ref[...]).astype(BF16)
    blocks = clusters // block
    for b in range(blocks):
        if b + early < blocks:
            assign(b + early)
        if b + early == blocks:
            name_users()
        sent = mm(place_ref[b * 2 * block : (b + 1) * 2 * block, :], query).astype(BF16)
        send_ref[b * groups : (b + 1) * groups, 0 : 2 * local, :] = sent.reshape(
            groups, 2 * local, width
        )
        if b % 4 == 3:
            span = (pl.ds((b - 3) * groups, 4 * groups), pl.ds(0, 2 * local))
            stores.append(
                pltpu.make_async_copy(send_ref.at[span], send_hbm.at[span], send_sem.at[b // 4])
            )
            stores[-1].start()
    for store in stores:
        store.wait()


def route(routes, positives, cluster_slot, features, w_hidden, w_out, devices):
    users, visits = routes.shape
    clusters = cluster_slot.shape[0]
    width = w_out.shape[1]
    rows = 2 * clusters // devices + 8
    args = (
        routes.T,
        positives.T,
        cluster_slot.reshape(clusters // LANES, LANES),
        features,
        w_hidden,
        w_out,
    )
    outs = (
        jax.ShapeDtypeStruct((devices, rows, width), BF16),
        jax.ShapeDtypeStruct((LANES, LANES), F32),
    )
    return pl.pallas_call(
        route_body,
        out_shape=outs_hbm(outs),
        in_specs=hbm(6),
        out_specs=hbm(2),
        scratch_shapes=[pltpu.VMEM(a.shape, a.dtype) for a in args + outs]
        + [
            pltpu.VMEM((2 * clusters, users), BF16),
            pltpu.SemaphoreType.DMA((6,)),
            pltpu.SemaphoreType.DMA((2,)),
            pltpu.SemaphoreType.DMA((4,)),
        ],
        compiler_params=params(48),
        name="route",
    )(*in_hbm(args))


def table_body(ids_ref, counts_ref, mass_hbm, tabs_hbm, inv_ref, mass_ref, tabs_ref, sem):
    clusters, chunks, lanes = tabs_ref.shape
    inv_ref[...] = 1.0 / counts_ref[...].astype(F32)
    tabs_ref[...] = ((ids_ref[...] << 12) | counts_ref[...]).reshape(tabs_ref.shape)
    store = pltpu.make_async_copy(tabs_ref, tabs_hbm, sem.at[0])
    store.start()
    item_at = iota((LANES, LANES), 0)

    def cluster(k, carry):
        acc = jnp.zeros((LANES, LANES), F32)
        for h in range(chunks):
            at = k * chunks + h
            hit = item_at == ids_ref[pl.ds(at, 1), :]
            acc = acc + jnp.where(hit, inv_ref[pl.ds(at, 1), :], 0.0)
        mass_ref[k] = jnp.broadcast_to(jnp.sum(acc, axis=1, keepdims=True), acc.shape)
        return carry

    lax.fori_loop(0, clusters, cluster, 0)
    last = pltpu.make_async_copy(mass_ref, mass_hbm, sem.at[1])
    last.start()
    last.wait()
    store.wait()


def tables(sample_ids, sample_counts):
    clusters, samples = sample_ids.shape
    total = sample_ids.size // LANES
    outs = (
        jax.ShapeDtypeStruct((clusters, LANES, LANES), F32),
        jax.ShapeDtypeStruct((clusters, samples // LANES, LANES), jnp.int32),
    )
    return pl.pallas_call(
        table_body,
        out_shape=outs_hbm(outs),
        in_specs=vmem(2),
        out_specs=hbm(2),
        scratch_shapes=[pltpu.VMEM((total, LANES), F32)]
        + [pltpu.VMEM(a.shape, a.dtype) for a in outs]
        + [pltpu.SemaphoreType.DMA((2,))],
        compiler_params=params(16),
        cost_estimate=pl.CostEstimate(flops=30_000_000, bytes_accessed=1 << 20, transcendentals=0),
        name="tables",
    )(sample_ids.reshape(total, LANES), sample_counts.reshape(total, LANES))


def row_of(slot):
    return slot // 8 * 16 + slot % 8


def owner_body(
    got_ref,
    items_hbm,
    mass_hbm,
    tabs_hbm,
    dq_hbm,
    weight_hbm,
    q_hbm,
    loss_ref,
    got32_ref,
    dq32_ref,
    dq_ref,
    weight_ref,
    q_ref,
    items_ref,
    mass_ref,
    tabs_ref,
    losses_ref,
    load_sem,
    dq_sem,
    weight_sem,
    q_sem,
):
    loads = [
        pltpu.make_async_copy(tabs_hbm, tabs_ref, load_sem.at[0]),
        pltpu.make_async_copy(items_hbm, items_ref, load_sem.at[1]),
    ]
    for part in range(mass_ref.shape[0] // 4):
        span = pl.ds(part * 4, 4)
        loads.append(
            pltpu.make_async_copy(mass_hbm.at[span], mass_ref.at[span], load_sem.at[2 + part])
        )
    for load in loads:
        load.start()
    devices, rows, width = got_ref.shape
    local = q_ref.shape[0]
    chunks = tabs_ref.shape[1]
    pairs = 2 * devices
    got32_ref[...] = got_ref[...].astype(F32).reshape(devices * rows, width)
    place_at = lax.axis_index("dev") % (LANES // local) * local
    tail_lane = iota((devices, LANES), 1)
    tail = jnp.zeros((devices, LANES), F32)
    for c in range(2):
        top = got32_ref[pl.ds(2 * local + c, devices, stride=rows), :]
        low = got32_ref[pl.ds(2 * local + 2 + c, devices, stride=rows), :]
        moved = pltpu.roll(top * 64.0 + low, (LANES + c * local - place_at) % LANES, 1)
        tail = jnp.where(tail_lane // local == c, moved, tail)
    tail = tail.T
    marks = [tail[c * local : (c + 1) * local, :] for c in range(2)]
    targets = [jnp.maximum(mark - 1.0, 0.0).astype(jnp.int32) for mark in marks]
    item_at = iota((LANES, pairs), 0)
    row_at = iota((chunks, devices), 0)
    for load in loads[0:2]:
        load.wait()
    stores = []

    def fetch(k):
        packed = []
        for target in targets:
            at = target[k : k + 1, :]
            lane = jnp.broadcast_to(at & (LANES - 1), (chunks, devices))
            found = jnp.take_along_axis(tabs_ref[k], lane, axis=1)
            packed.append(jnp.sum(jnp.where(row_at == (at >> 7), found, 0), axis=0, keepdims=True))
        packed = jnp.concatenate(packed, axis=1)
        live = jnp.concatenate([mark[k : k + 1, :] for mark in marks], axis=1) > 0.0
        queries = jnp.concatenate(
            [
                got32_ref[pl.ds(row_of(k), devices, stride=rows), :],
                got32_ref[pl.ds(row_of(k) + 8, devices, stride=rows), :],
            ],
            axis=0,
        ).astype(BF16)
        q_ref[k] = queries
        stores.append(pltpu.make_async_copy(q_ref.at[k], q_hbm.at[k], q_sem.at[k]))
        stores[-1].start()
        scores = mm(items_ref[k * LANES : (k + 1) * LANES, :], queries, ((1,), (1,)))
        return live, packed, scores

    def soften(k, live, packed, scores):
        item = jnp.where(live, packed >> 12, -1)
        count = (packed & 4095).astype(F32)
        if k % 4 == 0:
            loads[2 + k // 4].wait()
        column = jnp.concatenate([mass_ref[k]] * (pairs // LANES), axis=1)
        masked = jnp.where(column > 0.0, scores, NONE)
        top = jnp.max(masked, axis=0, keepdims=True)
        expo = jnp.exp(masked - top) * column
        total = jnp.sum(expo, axis=0, keepdims=True)
        hit = item_at == item
        picked = jnp.sum(jnp.where(hit, scores, 0.0), axis=0, keepdims=True)
        losses_ref[k : k + 1, :] = jnp.log(total) + top - (picked - jnp.log(count))
        weight = (expo * (1.0 / total) - jnp.where(hit, 1.0, 0.0)).astype(BF16)
        weight_ref[k] = weight
        stores.append(pltpu.make_async_copy(weight_ref.at[k], weight_hbm.at[k], weight_sem.at[k]))
        stores[-1].start()
        return weight

    def give(k, weight):
        dq = mm(weight, items_ref[k * LANES : (k + 1) * LANES, :], ((0,), (0,)))
        dq32_ref[pl.ds(row_of(k), devices, stride=rows), :] = dq[0:devices, :]
        dq32_ref[pl.ds(row_of(k) + 8, devices, stride=rows), :] = dq[devices:pairs, :]
        if k % 8 == 7:
            at = row_of(k) - 7
            dq_ref[:, at : at + 16, :] = (
                dq32_ref[...].reshape(devices, rows, width)[:, at : at + 16, :].astype(BF16)
            )
            span = (slice(None), pl.ds(at, 16))
            stores.append(
                pltpu.make_async_copy(dq_ref.at[span], dq_hbm.at[span], dq_sem.at[k // 8])
            )
            stores[-1].start()

    fetched = [fetch(k) for k in range(AHEAD)]
    for k in range(local):
        if k + AHEAD < local:
            fetched.append(fetch(k + AHEAD))
        give(k, soften(k, *fetched[k]))
    live = jnp.concatenate(marks, axis=1) > 0.0
    total = jnp.sum(jnp.where(live, losses_ref[...], 0.0), axis=1, keepdims=True)
    loss_ref[...] = total / jnp.sum(jnp.where(live, 1.0, 0.0), axis=1, keepdims=True)
    for store in stores:
        store.wait()


def owner(got, items, mass, tabs):
    devices, rows, width = got.shape
    local = items.shape[0] // LANES
    outs = (
        jax.ShapeDtypeStruct((devices, 2 * local, width), BF16),
        jax.ShapeDtypeStruct((local, LANES, 2 * devices), BF16),
        jax.ShapeDtypeStruct((local, 2 * devices, width), BF16),
    )
    return pl.pallas_call(
        owner_body,
        out_shape=outs_hbm(outs) + (jax.ShapeDtypeStruct((local, 1), F32),),
        in_specs=vmem(1) + hbm(3),
        out_specs=hbm(3) + vmem(1),
        scratch_shapes=[
            pltpu.VMEM((devices * rows, width), F32),
            pltpu.VMEM((devices * rows, width), F32),
        ]
        + [pltpu.VMEM(a.shape, a.dtype) for a in outs + (items, mass, tabs)]
        + [
            pltpu.VMEM((local, 2 * devices), F32),
            pltpu.SemaphoreType.DMA((2 + local // 4,)),
            pltpu.SemaphoreType.DMA((local // 8,)),
            pltpu.SemaphoreType.DMA((local,)),
            pltpu.SemaphoreType.DMA((local,)),
        ],
        compiler_params=params(40),
        name="owner",
    )(got, *in_hbm((items, mass, tabs)))


def item_body(weight_ref, q_ref, grad_ref):
    for k in range(weight_ref.shape[0]):
        grad_ref[k * LANES : (k + 1) * LANES, :] = mm(weight_ref[k], q_ref[k])


def item_grads(weight, queries):
    local, pairs, width = queries.shape
    step = 4
    return pl.pallas_call(
        item_body,
        grid=(local // step,),
        out_shape=jax.ShapeDtypeStruct((local * LANES, width), F32),
        in_specs=[
            pl.BlockSpec((step, LANES, pairs), lambda k: (k, 0, 0)),
            pl.BlockSpec((step, pairs, width), lambda k: (k, 0, 0)),
        ],
        out_specs=pl.BlockSpec((step * LANES, width), lambda k: (k, 0)),
        compiler_params=params(8),
        cost_estimate=pl.CostEstimate(
            flops=135_000_000, bytes_accessed=3 << 20, transcendentals=0
        ),
        name="item_grads",
    )(*in_hbm((weight, queries)))


def ready_body(feat_ref, feat_other_ref, wh_ref, *outs):
    half = outs[0].shape[0]
    core = lax.axis_index("dev") % 2
    weight = wh_ref[:, pl.ds(pl.multiple_of(core * half, half), half)]
    for i, ref in enumerate((feat_ref, feat_other_ref)):
        hidden_ref, slope_ref = outs[2 * i : 2 * i + 2]
        pre = mm(weight, ref[...], ((0,), (0,)))
        sig = jax.nn.sigmoid(pre)
        hidden_ref[...] = (pre * sig).astype(BF16)
        slope_ref[...] = (sig * (1.0 + pre * (1.0 - sig))).T


def ready(features_t, features_other_t, w_hidden):
    feats, users = features_t.shape
    hid = w_hidden.shape[1]
    half = hid // 2
    step = users // 2
    outs = (
        jax.ShapeDtypeStruct((half, users), BF16),
        jax.ShapeDtypeStruct((users, half), F32),
    ) * 2
    return pl.pallas_call(
        ready_body,
        grid=(users // step,),
        out_shape=outs_hbm(outs),
        in_specs=[pl.BlockSpec((feats, step), lambda i: (0, i))] * 2
        + [pl.BlockSpec((feats, hid), lambda i: (0, 0))],
        out_specs=[
            pl.BlockSpec((half, step), lambda i: (0, i)),
            pl.BlockSpec((step, half), lambda i: (i, 0)),
        ]
        * 2,
        compiler_params=params(24),
        cost_estimate=pl.CostEstimate(
            flops=550_000_000, bytes_accessed=5 << 20, transcendentals=1 << 19
        ),
        name="ready",
    )(*in_hbm((features_t, features_other_t, w_hidden)))


def collect_body(
    back_ref,
    named_ref,
    hidden_hbm,
    slope_hbm,
    feat_hbm,
    wo_hbm,
    dq_ref,
    hidden_ref,
    slope_ref,
    feat_ref,
    wo_ref,
    sem,
):
    half = hidden_ref.shape[0]
    core = lax.axis_index("dev") % 2
    wo_at = wo_hbm.at[pl.ds(pl.multiple_of(core * half, half), half), :]
    loads = [
        pltpu.make_async_copy(src, dst, sem.at[i])
        for i, (src, dst) in enumerate(
            [
                (wo_at, wo_ref),
                (slope_hbm, slope_ref),
                (feat_hbm, feat_ref),
                (hidden_hbm, hidden_ref),
            ]
        )
    ]
    for load in loads:
        load.start()
    devices, rows, width = back_ref.shape
    users = dq_ref.shape[0]
    block = LANES
    named = named_ref[...]
    lane_user = iota((block, users), 1).astype(F32)
    total = jnp.zeros((width, users), F32)
    group = 2 * block // rows
    for b in range(devices // group):
        parts = [
            jnp.where(lane_user == named[:, 2 * b + c : 2 * b + c + 1], 1.0, 0.0).reshape(
                block // 8, 8, users
            )
            for c in range(2)
        ]
        place = jnp.concatenate(parts, axis=1).reshape(2 * block, users).astype(BF16)
        back = back_ref[b * group : (b + 1) * group].reshape(2 * block, width)
        total = total + mm(back, place, ((0,), (0,)))
    dq_ref[...] = total.T.astype(BF16)
    for load in loads:
        load.wait()


def collect(back, named, hidden, slope, features_t, w_out):
    half, users = hidden.shape
    width = back.shape[2]
    return pl.pallas_call(
        collect_body,
        out_shape=outs_vmem(
            (
                jax.ShapeDtypeStruct((users, width), BF16),
                hidden,
                slope,
                features_t,
                jax.ShapeDtypeStruct((half, width), BF16),
            )
        ),
        in_specs=vmem(2) + hbm(4),
        out_specs=vmem(5),
        scratch_shapes=[pltpu.SemaphoreType.DMA((4,))],
        compiler_params=params(24),
        name="collect",
    )(back, named, *in_hbm((hidden, slope, features_t, w_out)))


def own_body(dq_ref, hidden_ref, slope_ref, feat_ref, wo_ref, big_ref, small_ref):
    dq = dq_ref[...]
    dpre = (mm(dq, wo_ref[...], ((1,), (1,))) * slope_ref[...]).astype(BF16)
    big_ref[...] = mm(feat_ref[...], dpre)
    small_ref[...] = mm(hidden_ref[...], dq)


def tower_own(dq, hidden, slope, features_t, w_half):
    half = hidden.shape[0]
    return pl.pallas_call(
        own_body,
        out_shape=(
            jax.ShapeDtypeStruct((features_t.shape[0], half), F32),
            jax.ShapeDtypeStruct((half, dq.shape[1]), F32),
        ),
        in_specs=vmem(5),
        out_specs=vmem(2),
        compiler_params=params(16),
        cost_estimate=pl.CostEstimate(
            flops=340_000_000, bytes_accessed=3 << 20, transcendentals=0
        ),
        name="tower_own",
    )(dq, hidden, slope, features_t, w_half)


def other_body(
    dq_ref, big_ref, small_ref, hidden_ref, slope_ref, feat_ref, wo_ref, grad_ref
):
    half = hidden_ref.shape[0]
    peers = grad_ref.shape[0]
    dq = dq_ref[...]
    dpre = (mm(dq, wo_ref[...], ((1,), (1,))) * slope_ref[...]).astype(BF16)
    big = big_ref[...] + mm(feat_ref[...], dpre)
    small = small_ref[...] + mm(hidden_ref[...], dq)
    tall = big.shape[0] // peers
    blocks = half // LANES
    for c in range(blocks):
        grad_ref[:, c * tall : (c + 1) * tall, :] = (
            big[:, c * LANES : (c + 1) * LANES].reshape(peers, tall, LANES).astype(BF16)
        )
    filled = half // 8
    at = blocks * tall
    grad_ref[0:filled, at : at + 8, :] = small.reshape(filled, 8, LANES).astype(BF16)
    grad_ref[filled:peers, at : at + 8, :] = jnp.zeros((peers - filled, 8, LANES), BF16)


def tower_other(dq, big, small, hidden, slope, features_t, w_half, peers):
    half = hidden.shape[0]
    rows = half * features_t.shape[0] // peers // LANES + 8
    return pl.pallas_call(
        other_body,
        out_shape=jax.ShapeDtypeStruct((peers, rows, LANES), BF16),
        in_specs=vmem(7),
        out_specs=vmem(1)[0],
        compiler_params=params(16),
        name="tower_other",
    )(dq, big, small, hidden, slope, features_t, w_half)


def sum_body(parts_ref, out_ref):
    total = jnp.sum(parts_ref[...].astype(F32), axis=0, keepdims=True)
    out_ref[...] = jnp.broadcast_to(total, out_ref.shape).astype(BF16)


def sum_parts(parts):
    return pl.pallas_call(
        sum_body,
        out_shape=jax.ShapeDtypeStruct(parts.shape, BF16),
        in_specs=vmem(1),
        out_specs=vmem(1)[0],
        compiler_params=params(24),
        name="sum_parts",
    )(parts)


def spread_body(side_of, got_ref, *refs):
    hidden_hbm, out_hbm, hidden_ref, out_ref, sem = refs[-5:]
    peers = got_ref.shape[0]
    side = lax.axis_index("dev") % 2
    side = side_of(side)
    half = out_ref.shape[0]
    tall = hidden_ref.shape[0] // peers
    blocks = half // LANES
    filled = half // 8
    stores = []
    for c in range(blocks):
        hidden_ref[:, c * LANES : (c + 1) * LANES] = (
            got_ref[:, c * tall : (c + 1) * tall, :].astype(F32).reshape(-1, LANES)
        )
        at = pl.multiple_of(side * half + c * LANES, LANES)
        stores.append(
            pltpu.make_async_copy(
                hidden_ref.at[:, pl.ds(c * LANES, LANES)],
                hidden_hbm.at[:, pl.ds(at, LANES)],
                sem.at[c],
            )
        )
        stores[-1].start()
    at = blocks * tall
    out_ref[...] = got_ref[0:filled, at : at + 8, :].astype(F32).reshape(half, LANES)
    stores.append(
        pltpu.make_async_copy(
            out_ref, out_hbm.at[pl.ds(pl.multiple_of(side * half, half), half), :], sem.at[blocks]
        )
    )
    stores[-1].start()
    for store in stores:
        store.wait()


def spread(got, side_of, hidden_shape, out_shape, begun=()):
    half = out_shape[0] // 2
    outs = (
        jax.ShapeDtypeStruct(hidden_shape, F32),
        jax.ShapeDtypeStruct(out_shape, F32),
    )
    return pl.pallas_call(
        functools.partial(spread_body, side_of),
        out_shape=outs_hbm(outs),
        in_specs=vmem(1) + hbm(len(begun)),
        out_specs=hbm(2),
        scratch_shapes=[
            pltpu.VMEM((hidden_shape[0], half), F32),
            pltpu.VMEM((half, LANES), F32),
            pltpu.SemaphoreType.DMA((half // LANES + 1,)),
        ],
        input_output_aliases={1 + i: i for i in range(len(begun))},
        compiler_params=params(16),
        cost_estimate=pl.CostEstimate(flops=300_000, bytes_accessed=2 << 20, transcendentals=0),
        name="spread",
    )(got, *in_hbm(begun))


def exchange(x):
    return lax.all_to_all(x, "dev", split_axis=0, concat_axis=0, tiled=True)


def exchange_peers(x):
    devices = lax.axis_size("dev")
    groups = [list(range(c, devices, 2)) for c in range(2)]
    return lax.all_to_all(
        x, "dev", split_axis=0, concat_axis=0, axis_index_groups=groups, tiled=True
    )


def swap(x):
    devices = lax.axis_size("dev")
    return lax.ppermute(x, "dev", [(d, d ^ 1) for d in range(devices)])


def local(
    features, w_hidden, w_out, items, routes, cluster_slot, sample_ids, sample_counts, positives
):
    devices = lax.axis_size("dev")
    features_t = features.T
    features_other_t = swap(features_t)
    send, named = route(routes, positives, cluster_slot, features, w_hidden, w_out, devices)
    mass, tabs = tables(sample_ids, sample_counts)
    got = exchange(send)
    got, mass, tabs, features_other_t = lax.optimization_barrier(
        (got, *in_hbm((mass, tabs)), features_other_t)
    )
    dq_slots, weight, queries, losses = owner(got, items, mass, tabs)
    back = exchange(dq_slots)
    prepared = ready(features_t, features_other_t, w_hidden)
    item_grad = item_grads(weight, queries)
    back, prepared, item_grad = lax.optimization_barrier((back, prepared, item_grad))
    dq, *held, w_half = collect(back, named, *prepared[0:2], features_t, w_out)
    dq_other = swap(dq)
    big, small = tower_own(dq, *held, w_half)
    partial = tower_other(
        dq_other, big, small, *prepared[2:4], features_other_t, w_half, devices // 2
    )
    summed = exchange_peers(sum_parts(exchange_peers(partial)))
    begun = spread(summed, lambda core: core, w_hidden.shape, w_out.shape)
    grad_hidden, grad_out = spread(
        swap(summed), lambda core: 1 - core, w_hidden.shape, w_out.shape, begun
    )
    slot_loss = losses[:, 0]
    return (slot_loss, grad_hidden, grad_out, item_grad)


def solution(mesh):
    in_specs = (
        P("dev", None),
        P(),
        P(),
        P("dev", None),
        P("dev", None),
        P(),
        P("dev", None),
        P("dev", None),
        P("dev", None),
    )
    out_specs = (P("dev"), P(), P(), P("dev", None))
    return jax.shard_map(local, mesh=mesh, in_specs=in_specs, out_specs=out_specs, check_vma=False)
```
